32 devices in a mesh: wide: 8 (over z, y), narrow: 4 (over x, core).
Axes of the slice: x: 2, y: 2, z: 4, core: 2. Of those that a mesh axis runs over, the one named last changes fastest.
Arguments:
- images: bfloat16 [1088, 50, 512], P(('wide', 'narrow')), may hold values from -6 to 6
- cotangent: bfloat16 [1088, 50, 512], P(('wide', 'narrow')), may hold values from -24 to 24
- counts: int32 [32], P(('wide', 'narrow')), may hold values from 1 to 34, as said below
- in_mats: float32 [512, 4096], P(('wide', 'narrow')), may hold values from -0.25 to 0.25
- in_mats_m: float32 [512, 4096], P(('wide', 'narrow')), may hold values from -0.00036621094 to 0.00036621094
- in_mats_v: float32 [512, 4096], P(('wide', 'narrow')), may hold values from 3.1789144e-10 to 1.2715657e-09
- out_mat: float32 [2048, 512], P(('wide', 'narrow')), may hold values from -0.125 to 0.125
- out_mat_m: float32 [2048, 512], P(('wide', 'narrow')), may hold values from -0.00036621094 to 0.00036621094
- out_mat_v: float32 [2048, 512], P(('wide', 'narrow')), may hold values from 3.1789144e-10 to 1.2715657e-09
- kernels: float32 [58, 512], P(None, ('wide', 'narrow')), may hold values from -1 to 1
- kernels_m: float32 [58, 512], P(None, ('wide', 'narrow')), may hold values from -0.0009765625 to 0.0009765625
- kernels_v: float32 [58, 512], P(None, ('wide', 'narrow')), may hold values from 2.861023e-09 to 1.1444092e-08
- gains: float32 [2, 512], P(None, ('wide', 'narrow')), may hold values from 0.8 to 5, as said below
- gains_m: float32 [2, 512], P(None, ('wide', 'narrow')), may hold values from -0.0009765625 to 0.0009765625
- gains_v: float32 [2, 512], P(None, ('wide', 'narrow')), may hold values from 2.861023e-09 to 1.1444092e-08
- biases: float32 [12, 512], P(None, ('wide', 'narrow')), may hold values from -1.25 to 1.25
- biases_m: float32 [12, 512], P(None, ('wide', 'narrow')), may hold values from -0.0009765625 to 0.0009765625
- biases_v: float32 [12, 512], P(None, ('wide', 'narrow')), may hold values from 2.861023e-09 to 1.1444092e-08
Outputs:
- block_out: bfloat16 [1088, 50, 512], P(('wide', 'narrow'))
- input_grad: float32 [1088, 50, 512], P(('wide', 'narrow'))
- grad_norm: float32 [], replicated
- in_mats_new: float32 [512, 4096], P(('wide', 'narrow'))
- in_mats_m_new: float32 [512, 4096], P(('wide', 'narrow'))
- in_mats_v_new: float32 [512, 4096], P(('wide', 'narrow'))
- in_mats_low: bfloat16 [512, 4096], P(('wide', 'narrow'))
- out_mat_new: float32 [2048, 512], P(('wide', 'narrow'))
- out_mat_m_new: float32 [2048, 512], P(('wide', 'narrow'))
- out_mat_v_new: float32 [2048, 512], P(('wide', 'narrow'))
- out_mat_low: bfloat16 [2048, 512], P(('wide', 'narrow'))
- kernels_new: float32 [58, 512], P(None, ('wide', 'narrow'))
- kernels_m_new: float32 [58, 512], P(None, ('wide', 'narrow'))
- kernels_v_new: float32 [58, 512], P(None, ('wide', 'narrow'))
- kernels_low: bfloat16 [58, 512], P(None, ('wide', 'narrow'))
- gains_new: float32 [2, 512], P(None, ('wide', 'narrow'))
- gains_m_new: float32 [2, 512], P(None, ('wide', 'narrow'))
- gains_v_new: float32 [2, 512], P(None, ('wide', 'narrow'))
- gains_low: bfloat16 [2, 512], P(None, ('wide', 'narrow'))
- biases_new: float32 [12, 512], P(None, ('wide', 'narrow'))
- biases_m_new: float32 [12, 512], P(None, ('wide', 'narrow'))
- biases_v_new: float32 [12, 512], P(None, ('wide', 'narrow'))
- biases_low: bfloat16 [12, 512], P(None, ('wide', 'narrow'))
The draws below stay inside these ranges and needn't reach their ends.
Inputs may be any that keep to these rules, and one draw needn't show every extreme that they name: Each device holds counts[d] live images in its first slots; some device is full. `gains`: gains are positive.
All inputs are finite; a program needn't handle non-finite values.
Results may differ from the reference program's by a relative error of at most 0.012.
Values may be sent and summed in bfloat16 or wider, within the bound.
A program may use at most 512 MiB of HBM per device.

```python
import math
import jax
import jax.numpy as jnp
from jax import lax

D = 512
HEADS = 8
MLP_WIDTH = 2048
GRID = 7
KROWS = 58
STEP = 10
IMG_CAP = 34
TOK = 50
BROWS = 12
NDEV = 32
IMAGES = 1088


def draw_counts(key, part):
    shift_key = jax.random.fold_in(key, 11)
    peak_key = jax.random.fold_in(key, 23)
    shifts = jax.random.randint(shift_key, (NDEV,), 0, 3)
    halved = jnp.where(shifts == 0, IMG_CAP, jnp.where(shifts == 1, IMG_CAP // 2, IMG_CAP // 4))
    peak_rank = jax.random.randint(peak_key, (), 0, NDEV)
    filled = jnp.where(jnp.arange(NDEV) == peak_rank, IMG_CAP, halved)
    return jnp.maximum(filled, 1).astype(jnp.int32)


def draw_gains(key, part):
    noise_key = jax.random.fold_in(key, 37)
    ramp = jnp.arange(D, dtype=jnp.float32) / (D - 1.0)
    rising = 1.0 + 2.0 * ramp
    factors = jax.random.uniform(noise_key, (2, D), jnp.float32, 0.85, 1.15)
    return (rising[None, :] * factors).astype(jnp.float32)


def steps_of(own_key, dims, cuts, least, largest):
    def one(dim, parts):
        steps = jax.random.uniform(jax.random.fold_in(jax.random.fold_in(own_key, 6), dim), (parts,), jnp.float32, least / len(cuts), largest / len(cuts))
        return jnp.repeat(jnp.exp(steps), dims[dim] // parts).reshape((-1,) + (1,) * (len(dims) - dim - 1))

    loudness = one(*cuts[0])
    for cut in cuts[1:]:
        loudness = loudness * one(*cut)
    return loudness


def normal_values(stream_key, extent, spread, bound, cuts=(), held_as=jnp.bfloat16):
    array = spread * jax.random.normal(stream_key, extent, jnp.float32)
    if cuts:
        array = array * steps_of(stream_key, extent, cuts, -0.22, 0.18)
    return jnp.clip(array, -bound, bound).astype(held_as)


def setup_inputs(seed: int = 0) -> dict:
    arg_keys = jax.random.split(jax.random.key(seed), 19)
    images = normal_values(arg_keys[0], (IMAGES, TOK, D), 1.0, 6.0, ((0, 32),))
    cotangent = normal_values(arg_keys[1], (IMAGES, TOK, D), 4.0, 24.0, ((0, 32),))
    counts = draw_counts(jax.random.fold_in(arg_keys[18], 71), 0)
    in_mats = normal_values(arg_keys[3], (D, 4 * D + MLP_WIDTH), D ** -0.5, 0.25, ((0, 32),), jnp.float32)
    in_mats_m = normal_values(arg_keys[4], (D, 4 * D + MLP_WIDTH), (0.11 / (D * (4 * D + 2 * MLP_WIDTH)) ** 0.5), 0.00036621094, ((0, 32),), jnp.float32)
    in_mats_v = jnp.clip(jnp.exp(math.log(1.2715657415895976e-09) - 1.3862944 * jax.random.uniform(arg_keys[5], (D, 4 * D + MLP_WIDTH), jnp.float32) ** steps_of(arg_keys[5], (D, 4 * D + MLP_WIDTH), ((0, 32),), -0.2, 0.2)), 3.178914353973994e-10, 1.2715657415895976e-09)
    out_mat = normal_values(arg_keys[6], (MLP_WIDTH, D), MLP_WIDTH ** -0.5, 0.125, ((0, 32),), jnp.float32)
    out_mat_m = normal_values(arg_keys[7], (MLP_WIDTH, D), (0.11 / (D * (4 * D + 2 * MLP_WIDTH)) ** 0.5), 0.00036621094, ((0, 32),), jnp.float32)
    out_mat_v = jnp.clip(jnp.exp(math.log(1.2715657415895976e-09) - 1.3862944 * jax.random.uniform(arg_keys[8], (MLP_WIDTH, D), jnp.float32) ** steps_of(arg_keys[8], (MLP_WIDTH, D), ((0, 32),), -0.2, 0.2)), 3.178914353973994e-10, 1.2715657415895976e-09)
    kernels = normal_values(arg_keys[9], (KROWS, D), 0.2, 1.0, ((1, 32),), jnp.float32)
    kernels_m = normal_values(arg_keys[10], (KROWS, D), (0.33 / (D * (4 * D + 2 * MLP_WIDTH)) ** 0.5), 0.0009765625, ((1, 32),), jnp.float32)
    kernels_v = jnp.clip(jnp.exp(math.log(1.1444091896350983e-08) - 1.3862944 * jax.random.uniform(arg_keys[11], (KROWS, D), jnp.float32) ** steps_of(arg_keys[11], (KROWS, D), ((1, 32),), -0.2, 0.2)), 2.8610229740877458e-09, 1.1444091896350983e-08)
    gains = draw_gains(jax.random.fold_in(arg_keys[18], 71), 0)
    gains_m = normal_values(arg_keys[13], (2, D), (0.33 / (D * (4 * D + 2 * MLP_WIDTH)) ** 0.5), 0.0009765625, ((1, 32),), jnp.float32)
    gains_v = jnp.clip(jnp.exp(math.log(1.1444091896350983e-08) - 1.3862944 * jax.random.uniform(arg_keys[14], (2, D), jnp.float32) ** steps_of(arg_keys[14], (2, D), ((1, 32),), -0.2, 0.2)), 2.8610229740877458e-09, 1.1444091896350983e-08)
    biases = normal_values(arg_keys[15], (BROWS, D), 0.2, 1.25, ((1, 32),), jnp.float32)
    biases_m = normal_values(arg_keys[16], (BROWS, D), (0.33 / (D * (4 * D + 2 * MLP_WIDTH)) ** 0.5), 0.0009765625, ((1, 32),), jnp.float32)
    biases_v = jnp.clip(jnp.exp(math.log(1.1444091896350983e-08) - 1.3862944 * jax.random.uniform(arg_keys[17], (BROWS, D), jnp.float32) ** steps_of(arg_keys[17], (BROWS, D), ((1, 32),), -0.2, 0.2)), 2.8610229740877458e-09, 1.1444091896350983e-08)
    return dict(images=images, cotangent=cotangent, counts=counts, in_mats=in_mats, in_mats_m=in_mats_m, in_mats_v=in_mats_v, out_mat=out_mat, out_mat_m=out_mat_m, out_mat_v=out_mat_v, kernels=kernels, kernels_m=kernels_m, kernels_v=kernels_v, gains=gains, gains_m=gains_m, gains_v=gains_v, biases=biases, biases_m=biases_m, biases_v=biases_v)


@jax.custom_vjp
def low(v):
    return lax.optimization_barrier(v.astype(jnp.bfloat16)).astype(jnp.float32)

@jax.custom_vjp
def low_back(v):
    return v

def low_keep(v):
    return (low(v), None)

def low_pass(kept, grad):
    return (grad,)

def back_keep(v):
    return (v, None)

def back_low(kept, grad):
    return (low(grad),)
low.defvjp(low_keep, low_pass)
low_back.defvjp(back_keep, back_low)
NORM_EPS = 1e-06
BETA_ONE = 0.9
BETA_TWO = 0.999
ADAM_EPS = 1e-08
HIGHEST = lax.Precision.HIGHEST
RATES = (0.04, 0.02, 0.1, 0.8, 0.25)
DECAYS = (0.05, 0.05, 0.05, 0.0, 0.0)

def layer_norm(values, gain_row, shift_row):
    centred = values - lax.optimization_barrier(jnp.mean(values, axis=-1, keepdims=True))
    variance = lax.optimization_barrier(jnp.mean(centred * centred, axis=-1, keepdims=True))
    return centred * lax.rsqrt(variance + NORM_EPS) * gain_row + shift_row

def depthwise(patch_grid, taps, kernel_width):
    margin = kernel_width // 2
    padded = jnp.pad(patch_grid, ((0, 0), (margin, margin), (margin, margin), (0, 0)))
    summed_taps = jnp.zeros_like(patch_grid)
    for row_tap in range(kernel_width):
        for col_tap in range(kernel_width):
            window = padded[:, row_tap:row_tap + GRID, col_tap:col_tap + GRID, :]
            summed_taps = summed_taps + window * taps[row_tap * kernel_width + col_tap]
    return summed_taps

def tap_mask(channels):
    head_width = channels // HEADS
    channel_ids = jnp.arange(channels, dtype=jnp.int32)
    reach_cells = jnp.where(channel_ids < 2 * head_width, 1, jnp.where(channel_ids < 5 * head_width, 2, 3))
    tap_ids = jnp.arange(49, dtype=jnp.int32)
    row_offset = jnp.abs(tap_ids // 7 - 3)
    col_offset = jnp.abs(tap_ids % 7 - 3)
    inside = (row_offset[:, None] <= reach_cells[None, :]) & (col_offset[:, None] <= reach_cells[None, :])
    return inside.astype(jnp.float32)

def pre_block(inputs, cpe_taps, cpe_shift, gain_row, shift_row):
    num_images, num_tokens, channels = inputs.shape
    patches = inputs[:, 1:].reshape(num_images, GRID, GRID, channels)
    mixed = patches + depthwise(patches, cpe_taps, 3) + cpe_shift
    after_cpe = jnp.concatenate([inputs[:, :1], mixed.reshape(num_images, GRID * GRID, channels)], axis=1)
    return (after_cpe, layer_norm(after_cpe, gain_row, shift_row))

def attend(qkv_rows, crpe_taps, crpe_shift):
    num_images, num_tokens, triple = qkv_rows.shape
    channels = triple // 3
    head_width = channels // HEADS
    queries = qkv_rows[..., :channels]
    key_rows = qkv_rows[..., channels:2 * channels]
    values = qkv_rows[..., 2 * channels:]
    weights = jax.nn.softmax(key_rows, axis=1)
    shape_heads = (num_images, num_tokens, HEADS, head_width)
    context = jnp.einsum('bnhd,bnhe->bhde', weights.reshape(shape_heads), values.reshape(shape_heads), precision=HIGHEST)
    factor = jnp.einsum('bnhd,bhde->bnhe', queries.reshape(shape_heads), context, precision=HIGHEST)
    factor = factor.reshape(num_images, num_tokens, channels)
    grid_values = values[:, 1:].reshape(num_images, GRID, GRID, channels)
    conv_values = depthwise(grid_values, crpe_taps * tap_mask(channels), 7) + crpe_shift
    relative = queries[:, 1:] * conv_values.reshape(num_images, GRID * GRID, channels)
    relative = jnp.concatenate([jnp.zeros((num_images, 1, channels), qkv_rows.dtype), relative], axis=1)
    return factor * head_width ** (-0.5) + relative

def forward(inputs, in_mats, out_mat, kernels, gains, biases):
    w_in = low(in_mats)
    w_out = low(out_mat)
    kern_all = low(kernels)
    gain_all = low(gains)
    bias_all = low(biases)
    num_images, num_tokens, channels = inputs.shape
    flat_rows = num_images * num_tokens
    hidden_rows = MLP_WIDTH // D
    after_cpe, normed = pre_block(inputs, kern_all[:9], bias_all[BROWS - 2], gain_all[0], bias_all[0])
    normed = low(normed).reshape(flat_rows, channels)
    qkv_bias = jnp.concatenate([bias_all[2], jnp.zeros_like(bias_all[2]), bias_all[3]])
    qkv_rows = low_back(jnp.dot(normed, w_in[:, :3 * channels], precision=HIGHEST) + qkv_bias)
    attended = attend(qkv_rows.reshape(num_images, num_tokens, 3 * channels), kern_all[9:], bias_all[BROWS - 1])
    attended = low(attended).reshape(flat_rows, channels)
    projected = low_back(jnp.dot(attended, w_in[:, 3 * channels:4 * channels], precision=HIGHEST) + bias_all[4])
    second = after_cpe.reshape(flat_rows, channels) + projected
    normed_two = low(layer_norm(second, gain_all[1], bias_all[1]))
    fc_bias = bias_all[5:5 + hidden_rows].reshape(-1)
    hidden_pre = low_back(jnp.dot(normed_two, w_in[:, 4 * channels:], precision=HIGHEST) + fc_bias)
    activated = low(jax.nn.gelu(hidden_pre, approximate=False))
    branch_out = low_back(jnp.dot(activated, w_out, precision=HIGHEST) + bias_all[BROWS - 3])
    return (second + branch_out).reshape(num_images, num_tokens, channels)

def adamw_update(master, first_moment, second_moment, gradient, clip_factor, rate, decay):
    clipped = gradient * clip_factor
    first_new = BETA_ONE * first_moment + (1.0 - BETA_ONE) * clipped
    second_new = BETA_TWO * second_moment + (1.0 - BETA_TWO) * clipped * clipped
    first_hat = first_new / (1.0 - BETA_ONE ** STEP)
    second_hat = second_new / (1.0 - BETA_TWO ** STEP)
    master_new = master - rate * (first_hat / (jnp.sqrt(second_hat) + ADAM_EPS) + decay * master)
    return (master_new, first_new, second_new, master_new.astype(jnp.bfloat16))

def reference(images, cotangent, counts, in_mats, in_mats_m, in_mats_v, out_mat, out_mat_m, out_mat_v, kernels, kernels_m, kernels_v, gains, gains_m, gains_v, biases, biases_m, biases_v):
    group_devices = 2
    per_block = group_devices * IMG_CAP
    num_blocks = IMAGES // per_block
    slot_ids = jnp.arange(IMAGES, dtype=jnp.int32)
    live = (slot_ids % IMG_CAP < counts[slot_ids // IMG_CAP]).astype(jnp.float32)
    inputs = images.astype(jnp.float32).reshape(num_blocks, per_block, TOK, D)
    pulled = (cotangent.astype(jnp.float32) * live[:, None, None]).reshape(num_blocks, per_block, TOK, D)
    masters = (in_mats, out_mat, kernels, gains, biases)

    def step_block(carry, pair):
        block_in, block_cot = pair
        block_out, pull_back = jax.vjp(forward, block_in, in_mats, out_mat, kernels, gains, biases)
        gradients = pull_back(block_cot)
        summed = tuple((total_part + piece for total_part, piece in zip(carry, gradients[1:])))
        return (summed, (block_out.astype(jnp.bfloat16), gradients[0]))
    initial = tuple((jnp.zeros_like(weight) for weight in masters))
    carry, (outputs, input_grads) = lax.scan(step_block, initial, (inputs, pulled))
    block_out = outputs.reshape(IMAGES, TOK, D)
    input_grad = input_grads.reshape(IMAGES, TOK, D)
    live_total = jnp.sum(counts).astype(jnp.float32) * TOK
    gradients = tuple((piece / live_total for piece in carry))
    grad_norm = jnp.sqrt(sum((jnp.sum(piece * piece) for piece in gradients)))
    clip_factor = jnp.minimum(1.0, 1.0 / (grad_norm + 1e-06))
    in_new = adamw_update(in_mats, in_mats_m, in_mats_v, gradients[0], clip_factor, RATES[0], DECAYS[0])
    out_new = adamw_update(out_mat, out_mat_m, out_mat_v, gradients[1], clip_factor, RATES[1], DECAYS[1])
    kern_new = adamw_update(kernels, kernels_m, kernels_v, gradients[2], clip_factor, RATES[2], DECAYS[2])
    gain_new = adamw_update(gains, gains_m, gains_v, gradients[3], clip_factor, RATES[3], DECAYS[3])
    bias_new = adamw_update(biases, biases_m, biases_v, gradients[4], clip_factor, RATES[4], DECAYS[4])
    return (block_out, input_grad, grad_norm, in_new[0], in_new[1], in_new[2], in_new[3], out_new[0], out_new[1], out_new[2], out_new[3], kern_new[0], kern_new[1], kern_new[2], kern_new[3], gain_new[0], gain_new[1], gain_new[2], gain_new[3], bias_new[0], bias_new[1], bias_new[2], bias_new[3])
```

```python
import functools

import jax
import jax.numpy as jnp
from jax import lax
from jax.experimental import pallas as pl
from jax.experimental.pallas import tpu as pltpu
from jax.sharding import PartitionSpec as P

D = 512
HEADS = 8
MLP_WIDTH = 2048
GRID = 7
STEP = 10
BROWS = 12


NORM_EPS = 1e-06
BETA_ONE = 0.9
BETA_TWO = 0.999
ADAM_EPS = 1e-08
HIGHEST = lax.Precision.HIGHEST
RATES = (0.04, 0.02, 0.1, 0.8, 0.25)
DECAYS = (0.05, 0.05, 0.05, 0.0, 0.0)


MESH_ID = pl.DeviceIdType.MESH
SPLIT = 3072
SMALL_ROWS = 16


def place():
    w = lax.axis_index("wide")
    n = lax.axis_index("narrow")
    return w // 2, w % 2, n // 2, n % 2


def device(z, y, x, c):
    return (z * 2 + y, x * 2 + c)


def neighbour(at, axis, step=1):
    z, y, x, c = at
    if axis == 0:
        return (lax.rem(z + step, 4), y, x, c)
    if axis == 1:
        return (z, 1 - y, x, c)
    if axis == 2:
        return (z, y, 1 - x, c)
    return (z, y, x, 1 - c)


def gather_kernel(wi, wo, sm, gi, go, gs, send_sem, recv_sem, own_sem):
    at = place()
    z, y, x, c = at
    partners = [device(*neighbour(at, 0, s)) for s in (1, 2, 3)]
    partners += [device(*neighbour(at, a)) for a in (1, 2, 3)]
    barrier = pltpu.get_barrier_semaphore()
    for partner in partners:
        pl.semaphore_signal(barrier, inc=1, device_id=partner, device_id_type=MESH_ID)
    pl.semaphore_wait(barrier, len(partners))

    width = wi.shape[1]
    pieces = (
        (wi, gi, 0, pl.ds(0, SPLIT)),
        (sm, gs, 0, pl.ds(0, 128)),
        (wi, gi, 1, pl.ds(SPLIT, width - SPLIT)),
        (wo, go, 1, pl.ds(0, wo.shape[1])),
    )
    orders = ((0, 1, 2, 3), (0, 2, 1, 3))

    def slot(r):
        zs = lax.rem(z - r[0] + 4, 4)
        ys = 1 - y if r[1] else y
        xs = 1 - x if r[2] else x
        cs = 1 - c if r[3] else c
        return ((zs * 2 + ys) * 2 + xs) * 2 + cs

    def flat(r):
        return ((r[0] * 2 + r[1]) * 2 + r[2]) * 2 + r[3]

    def moved(r, axis, step):
        r = list(r)
        r[axis] = step
        return tuple(r)

    def transfer(p, r, axis, step):
        own, out, color, cols = pieces[p]
        there = out.at[slot(r), :, cols]
        here = own.at[:, cols] if r == (0, 0, 0, 0) else there
        to = moved(r, axis, step)
        return pltpu.make_async_remote_copy(
            src_ref=here,
            dst_ref=there,
            send_sem=send_sem.at[p, flat(to)],
            recv_sem=recv_sem.at[p, flat(to)],
            device_id=device(*neighbour(at, axis, step)),
            device_id_type=MESH_ID,
        )

    def onward(p, r):
        order = orders[pieces[p][2]]
        last = max([i for i in range(4) if r[order[i]]], default=-1)
        for i in range(last + 1, 4):
            axis = order[i]
            for step in (1, 2, 3) if axis == 0 else (1,):
                yield axis, step

    started = []

    def forward(p, r):
        for axis, step in onward(p, r):
            copy = transfer(p, r, axis, step)
            copy.start()
            started.append(copy)

    zero = (0, 0, 0, 0)
    for p in range(4):
        forward(p, zero)
    own_copies = []
    for p in range(4):
        own, out, color, cols = pieces[p]
        copy = pltpu.make_async_copy(
            own.at[:, cols], out.at[slot(zero), :, cols], own_sem.at[p]
        )
        copy.start()
        own_copies.append(copy)

    def arrival(p, r):
        order = orders[pieces[p][2]]
        axis = [a for a in order if r[a]][-1]
        back = moved(r, axis, 0)
        return transfer(p, back, axis, r[axis])

    offsets = [
        (dz, dy, dx, dc) for dz in range(4) for dy in range(2) for dx in range(2) for dc in range(2)
    ]
    cost = {0: 0, 1: 2, 2: 4, 3: 2}

    def when(r):
        return cost[r[0]] + r[1] * 2 + r[2] * 2 + r[3]

    for r in sorted(offsets[1:], key=when):
        for p in range(4):
            copy = arrival(p, r)
            copy.wait_recv()
            forward(p, r)
    for copy in started:
        copy.wait_send()
    for copy in own_copies:
        copy.wait()


def gather_all(in_copy, out_copy, small):
    hbm = pl.BlockSpec(memory_space=pl.ANY)
    return pl.pallas_call(
        gather_kernel,
        out_shape=(
            jax.ShapeDtypeStruct((32,) + in_copy.shape, in_copy.dtype),
            jax.ShapeDtypeStruct((32,) + out_copy.shape, out_copy.dtype),
            jax.ShapeDtypeStruct((32,) + small.shape, small.dtype),
        ),
        in_specs=[hbm] * 3,
        out_specs=(hbm,) * 3,
        scratch_shapes=[
            pltpu.SemaphoreType.DMA((4, 32)),
            pltpu.SemaphoreType.DMA((4, 32)),
            pltpu.SemaphoreType.DMA((4,)),
        ],
        compiler_params=pltpu.CompilerParams(collective_id=0, has_side_effects=True),
        name="gather_all",
    )(in_copy, out_copy, small)


def add_low(left, right):
    return (left.astype(jnp.float32) + right.astype(jnp.float32)).astype(left.dtype)


def reduce_kernel(
    gi, go, gs, fi, fo, fs, fq,
    ai, ao, a_s, b1, b2i, b2o, b2s, b3,
    ri, ro, rs, r1, r2i, r2o, r2s, r3,
    t1, t2i, t2o, t2s, u1, u2i, u2o, u2s,
    squares_narrow, squares_wide, send_sem, recv_sem, norm_send, norm_recv,
):
    at = place()
    z, y, x, c = at
    w = z * 2 + y
    n = x * 2 + c
    partners = [(w, lax.rem(n + s, 4)) for s in (1, 2, 3)]
    partners += [(lax.rem(w + s, 8), n) for s in range(1, 8)]
    barrier = pltpu.get_barrier_semaphore()
    for partner in partners:
        pl.semaphore_signal(barrier, inc=1, device_id=partner, device_id_type=MESH_ID)
    pl.semaphore_wait(barrier, len(partners))

    count = [0]

    def send(src, dst, axis, step=1):
        index = count[0]
        count[0] += 1
        copy = pltpu.make_async_remote_copy(
            src_ref=src,
            dst_ref=dst,
            send_sem=send_sem.at[index],
            recv_sem=recv_sem.at[index],
            device_id=device(*neighbour(at, axis, step)),
            device_id_type=MESH_ID,
        )
        copy.start()
        return copy

    first = [
        send(gi.at[:, :, :, 1 - c], ri, 3),
        send(go.at[:, :, :, 1 - c], ro, 3),
        send(gs.at[:, :, :, 1 - c], rs, 3),
    ]
    for copy in first:
        copy.wait_recv()

    def add_first(k, carry):
        zi, yi, xi = k // 4, lax.rem(k // 2, 2), lax.rem(k, 2)
        ai[zi, yi, xi] = add_low(gi[zi, yi, xi, c], ri[zi, yi, xi])
        ao[zi, yi, xi] = add_low(go[zi, yi, xi, c], ro[zi, yi, xi])
        a_s[zi, yi, xi] = add_low(gs[zi, yi, xi, c], rs[zi, yi, xi])
        return carry

    lax.fori_loop(0, 16, add_first, 0)
    width = gi.shape[-1]
    left, right = pl.ds(0, SPLIT), pl.ds(SPLIT, width - SPLIT)
    second = [
        send(ai.at[:, :, 1 - x, :, left], r1, 2),
        send(ai.at[:, 1 - y, :, :, right], r2i, 1),
        send(ao.at[:, 1 - y], r2o, 1),
        send(a_s.at[:, 1 - y], r2s, 1),
    ]
    for copy in second:
        copy.wait_recv()

    def add_second(k, carry):
        zi, j = k // 2, lax.rem(k, 2)
        b1[zi, j] = add_low(ai[zi, j, x, :, left], r1[zi, j])
        b2i[zi, j] = add_low(ai[zi, y, j, :, right], r2i[zi, j])
        b2o[zi, j] = add_low(ao[zi, y, j], r2o[zi, j])
        b2s[zi, j] = add_low(a_s[zi, y, j], r2s[zi, j])
        return carry

    lax.fori_loop(0, 8, add_second, 0)
    third = [
        send(b1.at[:, 1 - y], r3, 1),
        send(b2i.at[:, 1 - x], t2i, 2),
        send(b2o.at[:, 1 - x], t2o, 2),
        send(b2s.at[:, 1 - x], t2s, 2),
    ]
    for copy in third:
        copy.wait_recv()

    def add_third(k, carry):
        b3[k] = add_low(b1[k, y], r3[k])
        r2i[k, 0] = add_low(b2i[k, x], t2i[k])
        r2o[k, 0] = add_low(b2o[k, x], t2o[k])
        r2s[k, 0] = add_low(b2s[k, x], t2s[k])
        return carry

    lax.fori_loop(0, 4, add_third, 0)
    fourth = []
    for step in (1, 2, 3):
        to = lax.rem(z + step, 4)
        fourth += [
            send(b3.at[to], u1.at[step - 1], 0, step),
            send(r2i.at[to, 0], u2i.at[step - 1], 0, step),
            send(r2o.at[to, 0], u2o.at[step - 1], 0, step),
            send(r2s.at[to, 0], u2s.at[step - 1], 0, step),
        ]
    for copy in fourth:
        copy.wait_recv()

    def total(own, others):
        value = own.astype(jnp.float32)
        for k in range(3):
            value = value + others[k].astype(jnp.float32)
        return value

    squares = jnp.zeros((8, 128), jnp.float32)

    def tile_squares(value, squares):
        rows, cols = value.shape
        for i in range(rows // 8):
            for j in range(cols // 128):
                part = value[i * 8 : i * 8 + 8, j * 128 : j * 128 + 128]
                squares = squares + part * part
        return squares

    for own, others, out, cols in (
        (b3[z], u1, fi, left),
        (r2i[z, 0], u2i, fi, right),
        (r2o[z, 0], u2o, fo, pl.ds(0, fo.shape[1])),
        (r2s[z, 0], u2s, fs, pl.ds(0, 128)),
    ):
        value = total(own, others)
        out[:, cols] = value
        squares = tile_squares(value, squares)

    def exchange(buffer, mine, size, axis, base):
        copies = []
        for step in range(1, size):
            to = lax.rem(mine + step, size)
            copy = pltpu.make_async_remote_copy(
                src_ref=buffer.at[mine],
                dst_ref=buffer.at[mine],
                send_sem=norm_send.at[base + step],
                recv_sem=norm_recv.at[base + step],
                device_id=(to, n) if axis == 0 else (w, to),
                device_id_type=MESH_ID,
            )
            copy.start()
            copies.append(copy)
        for copy in copies:
            copy.wait()
        value = buffer[0]
        for k in range(1, size):
            value = value + buffer[k]
        return value

    squares_narrow[n] = squares
    squares = exchange(squares_narrow, n, 4, 1, 0)
    squares_wide[w] = squares
    fq[...] = exchange(squares_wide, w, 8, 0, 4)
    for copy in first + second + third + fourth:
        copy.wait_send()


def reduce_all(grad_in, grad_out, small):
    low = jnp.bfloat16
    rows_in, width = grad_in.shape[0] // 32, grad_in.shape[1]
    rows_out, cols_out = grad_out.shape[0] // 32, grad_out.shape[1]
    gi = grad_in.reshape(4, 2, 2, 2, rows_in, width)
    go = grad_out.reshape(4, 2, 2, 2, rows_out, cols_out)
    gs = small.reshape(4, 2, 2, 2, SMALL_ROWS, 128)
    rest = width - SPLIT
    vmem = pl.BlockSpec(memory_space=pltpu.VMEM)

    def trio(lead, cols, own=True):
        kinds = [
            pltpu.VMEM(lead + (rows_in, cols), low),
            pltpu.VMEM(lead + (rows_out, cols_out), low),
            pltpu.VMEM(lead + (SMALL_ROWS, 128), jnp.float32),
        ]
        return kinds

    scratch = trio((4, 2, 2), width)
    scratch += [pltpu.VMEM((4, 2, rows_in, SPLIT), low)] + trio((4, 2), rest)
    scratch += [pltpu.VMEM((4, rows_in, SPLIT), low)]
    scratch += trio((4, 2, 2), width)
    scratch += [pltpu.VMEM((4, 2, rows_in, SPLIT), low)] + trio((4, 2), rest)
    scratch += [pltpu.VMEM((4, rows_in, SPLIT), low)]
    scratch += [pltpu.VMEM((1, 8, 128), low)] + trio((4,), rest)
    scratch += [pltpu.VMEM((3, rows_in, SPLIT), low)] + trio((3,), rest)
    scratch += [
        pltpu.VMEM((4, 8, 128), jnp.float32),
        pltpu.VMEM((8, 8, 128), jnp.float32),
        pltpu.SemaphoreType.DMA((23,)),
        pltpu.SemaphoreType.DMA((23,)),
        pltpu.SemaphoreType.DMA((12,)),
        pltpu.SemaphoreType.DMA((12,)),
    ]
    return pl.pallas_call(
        reduce_kernel,
        out_shape=(
            jax.ShapeDtypeStruct((rows_in, width), jnp.float32),
            jax.ShapeDtypeStruct((rows_out, cols_out), jnp.float32),
            jax.ShapeDtypeStruct((SMALL_ROWS, 128), jnp.float32),
            jax.ShapeDtypeStruct((8, 128), jnp.float32),
        ),
        in_specs=[vmem] * 3,
        out_specs=(vmem,) * 4,
        scratch_shapes=scratch,
        compiler_params=pltpu.CompilerParams(
            collective_id=1, has_side_effects=True, vmem_limit_bytes=48 << 20
        ),
        name="reduce_all",
    )(gi, go, gs)


def layer_norm(values, gain_row, shift_row):
    centred = values - jnp.mean(values, axis=-1, keepdims=True)
    variance = jnp.mean(centred * centred, axis=-1, keepdims=True)
    return centred * lax.rsqrt(variance + NORM_EPS) * gain_row + shift_row


def depthwise(patch_grid, taps, kernel_width):
    margin = kernel_width // 2
    padded = jnp.pad(patch_grid, ((0, 0), (margin, margin), (margin, margin), (0, 0)))
    summed_taps = jnp.zeros_like(patch_grid)
    for row_tap in range(kernel_width):
        for col_tap in range(kernel_width):
            window = padded[:, row_tap : row_tap + GRID, col_tap : col_tap + GRID, :]
            summed_taps = summed_taps + window * taps[row_tap * kernel_width + col_tap]
    return summed_taps


def tap_mask(channels):
    head_width = channels // HEADS
    channel_ids = jnp.arange(channels, dtype=jnp.int32)
    reach_cells = jnp.where(
        channel_ids < 2 * head_width, 1, jnp.where(channel_ids < 5 * head_width, 2, 3)
    )
    tap_ids = jnp.arange(49, dtype=jnp.int32)
    row_offset = jnp.abs(tap_ids // 7 - 3)
    col_offset = jnp.abs(tap_ids % 7 - 3)
    inside = (row_offset[:, None] <= reach_cells[None, :]) & (
        col_offset[:, None] <= reach_cells[None, :]
    )
    return inside.astype(jnp.float32)


def pre_block(inputs, cpe_taps, cpe_shift, gain_row, shift_row):
    num_images, num_tokens, channels = inputs.shape
    patches = inputs[:, 1:].reshape(num_images, GRID, GRID, channels)
    mixed = patches + depthwise(patches, cpe_taps, 3) + cpe_shift
    after_cpe = jnp.concatenate(
        [inputs[:, :1], mixed.reshape(num_images, GRID * GRID, channels)], axis=1
    )
    return (after_cpe, layer_norm(after_cpe, gain_row, shift_row))


def attend(qkv_rows, crpe_taps, crpe_shift):
    num_images, num_tokens, triple = qkv_rows.shape
    channels = triple // 3
    head_width = channels // HEADS
    queries = qkv_rows[..., :channels]
    key_rows = qkv_rows[..., channels : 2 * channels]
    values = qkv_rows[..., 2 * channels :]
    weights = jax.nn.softmax(key_rows, axis=1)
    shape_heads = (num_images, num_tokens, HEADS, head_width)
    context = jnp.einsum(
        "bnhd,bnhe->bhde",
        weights.reshape(shape_heads),
        values.reshape(shape_heads),
        precision=HIGHEST,
    )
    factor = jnp.einsum("bnhd,bhde->bnhe", queries.reshape(shape_heads), context, precision=HIGHEST)
    factor = factor.reshape(num_images, num_tokens, channels)
    grid_values = values[:, 1:].reshape(num_images, GRID, GRID, channels)
    conv_values = depthwise(grid_values, crpe_taps * tap_mask(channels), 7) + crpe_shift
    relative = queries[:, 1:] * conv_values.reshape(num_images, GRID * GRID, channels)
    relative = jnp.concatenate(
        [jnp.zeros((num_images, 1, channels), jnp.float32), relative], axis=1
    )
    return factor * head_width ** (-0.5) + relative


def gelu_exact(values):
    return jax.nn.gelu(values, approximate=False)


def cross_rows(left, right):
    return lax.dot_general(
        left, right, (((0,), (0,)), ((), ())), preferred_element_type=jnp.float32
    )


def transposed(gradient, weight):
    return lax.dot_general(
        gradient, weight, (((1,), (1,)), ((), ())), preferred_element_type=jnp.float32
    )


def column_sums(rounded):
    return jnp.sum(rounded.astype(jnp.float32), axis=0)


def adamw_update(master, first_moment, second_moment, gradient, clip_factor, rate, decay):
    clipped = gradient * clip_factor
    first_new = BETA_ONE * first_moment + (1.0 - BETA_ONE) * clipped
    second_new = BETA_TWO * second_moment + (1.0 - BETA_TWO) * clipped * clipped
    first_hat = first_new / (1.0 - BETA_ONE**STEP)
    second_hat = second_new / (1.0 - BETA_TWO**STEP)
    master_new = master - rate * (first_hat / (jnp.sqrt(second_hat) + ADAM_EPS) + decay * master)
    return (master_new, first_new, second_new, master_new.astype(jnp.bfloat16))


def local(
    images,
    cotangent,
    counts,
    in_mats,
    in_mats_m,
    in_mats_v,
    out_mat,
    out_mat_m,
    out_mat_v,
    kernels,
    kernels_m,
    kernels_v,
    gains,
    gains_m,
    gains_v,
    biases,
    biases_m,
    biases_v,
    special,
):
    in_copy = in_mats.astype(jnp.bfloat16)
    out_copy = out_mat.astype(jnp.bfloat16)
    kern_copy = kernels.astype(jnp.bfloat16)
    gain_copy = gains.astype(jnp.bfloat16)
    bias_copy = biases.astype(jnp.bfloat16)
    shards = (kern_copy, gain_copy, bias_copy)
    sizes = [shard.shape[0] for shard in shards]
    if special:
        per = sum(sizes) * kern_copy.shape[1]
        flat = jnp.concatenate(
            [jnp.concatenate(shards, axis=0).reshape(-1), counts.astype(jnp.bfloat16)]
        )
        flat = jnp.pad(flat, (0, SMALL_ROWS * 128 - per - 1)).reshape(SMALL_ROWS, 128)
        all_in, all_out, all_small = gather_all(in_copy, out_copy, flat)
        all_small = all_small.reshape(32, SMALL_ROWS * 128)
        live_total = jnp.sum(all_small[:, per].astype(jnp.float32)) * images.shape[1]
        rows = all_small[:, :per].reshape(32, sum(sizes), -1).transpose(1, 0, 2)
        rows = rows.reshape(sum(sizes), -1)
        gathered = (
            all_in.reshape(-1, in_copy.shape[1]),
            all_out.reshape(-1, out_copy.shape[1]),
            rows[: sizes[0]],
            rows[sizes[0] : sizes[0] + sizes[1]],
            rows[sizes[0] + sizes[1] :],
        )
    else:
        gathered = (
            lax.all_gather(in_copy, ("wide", "narrow"), axis=0, tiled=True),
            lax.all_gather(out_copy, ("wide", "narrow"), axis=0, tiled=True),
            lax.all_gather(kern_copy, ("wide", "narrow"), axis=1, tiled=True),
            lax.all_gather(gain_copy, ("wide", "narrow"), axis=1, tiled=True),
            lax.all_gather(bias_copy, ("wide", "narrow"), axis=1, tiled=True),
        )
        live_total = lax.psum(
            counts[0].astype(jnp.float32) * images.shape[1], ("wide", "narrow")
        )
    wide_in = gathered[0]
    wide_out = gathered[1]
    kern_all = gathered[2].astype(jnp.float32)
    gain_all = gathered[3].astype(jnp.float32)
    bias_all = gathered[4].astype(jnp.float32)
    inputs = images.astype(jnp.float32)
    num_images, num_tokens, channels = inputs.shape
    flat_rows = num_images * num_tokens
    hidden_rows = MLP_WIDTH // D
    live = (jnp.arange(num_images, dtype=jnp.int32) < counts[0]).astype(jnp.float32)
    scale_factor = 1.0 / live_total
    (after_cpe, normed), pre_back = jax.vjp(
        pre_block, inputs, kern_all[:9], bias_all[BROWS - 2], gain_all[0], bias_all[0]
    )
    normed_low = normed.astype(jnp.bfloat16).reshape(flat_rows, channels)
    qkv_bias = jnp.concatenate([bias_all[2], jnp.zeros_like(bias_all[2]), bias_all[3]])
    qkv_rows = (
        jnp.dot(normed_low, wide_in[:, : 3 * channels], preferred_element_type=jnp.float32)
        + qkv_bias
    )
    qkv_shaped = qkv_rows.reshape(num_images, num_tokens, 3 * channels)
    attended, attend_back = jax.vjp(attend, qkv_shaped, kern_all[9:], bias_all[BROWS - 1])
    attended_low = attended.astype(jnp.bfloat16).reshape(flat_rows, channels)
    projected = (
        jnp.dot(
            attended_low,
            wide_in[:, 3 * channels : 4 * channels],
            preferred_element_type=jnp.float32,
        )
        + bias_all[4]
    )
    second = after_cpe.reshape(flat_rows, channels) + projected
    normed_two, norm_back = jax.vjp(layer_norm, second, gain_all[1], bias_all[1])
    normed_two_low = normed_two.astype(jnp.bfloat16)
    fc_bias = bias_all[5 : 5 + hidden_rows].reshape(-1)
    hidden_pre = (
        jnp.dot(normed_two_low, wide_in[:, 4 * channels :], preferred_element_type=jnp.float32)
        + fc_bias
    )
    activated, gelu_back = jax.vjp(gelu_exact, hidden_pre)
    activated_low = activated.astype(jnp.bfloat16)
    branch_out = (
        jnp.dot(activated_low, wide_out, preferred_element_type=jnp.float32) + bias_all[BROWS - 3]
    )
    block_out = (second + branch_out).reshape(num_images, num_tokens, channels).astype(jnp.bfloat16)
    back_in = wide_in
    back_out = wide_out
    out_grad = (cotangent.astype(jnp.float32) * live[:, None, None]).reshape(flat_rows, channels)
    out_grad_low = out_grad.astype(jnp.bfloat16)
    grad_fc2 = cross_rows(activated_low, out_grad_low)
    grad_fc2_bias = column_sums(out_grad_low)
    grad_act = transposed(out_grad_low, back_out)
    grad_hidden = gelu_back(grad_act)[0].astype(jnp.bfloat16)
    grad_fc1 = cross_rows(normed_two_low, grad_hidden)
    grad_fc1_bias = column_sums(grad_hidden).reshape(hidden_rows, channels)
    grad_normed_two = transposed(grad_hidden, back_in[:, 4 * channels :])
    grad_second_norm, grad_gain_two, grad_shift_two = norm_back(grad_normed_two)
    grad_second = out_grad + grad_second_norm
    grad_second_low = grad_second.astype(jnp.bfloat16)
    grad_proj = cross_rows(attended_low, grad_second_low)
    grad_proj_bias = column_sums(grad_second_low)
    grad_attended = transposed(grad_second_low, back_in[:, 3 * channels : 4 * channels])
    grad_qkv, grad_crpe_taps, grad_crpe_shift = attend_back(
        grad_attended.reshape(num_images, num_tokens, channels)
    )
    grad_qkv_low = grad_qkv.reshape(flat_rows, 3 * channels).astype(jnp.bfloat16)
    grad_qkv_mat = cross_rows(normed_low, grad_qkv_low)
    qkv_sums = column_sums(grad_qkv_low)
    grad_normed = transposed(grad_qkv_low, back_in[:, : 3 * channels])
    input_grad, grad_cpe_taps, grad_cpe_shift, grad_gain_one, grad_shift_one = pre_back(
        (
            grad_second.reshape(num_images, num_tokens, channels),
            grad_normed.reshape(num_images, num_tokens, channels),
        )
    )
    grad_kern = jnp.concatenate([grad_cpe_taps, grad_crpe_taps], axis=0)
    grad_gain = jnp.stack([grad_gain_one, grad_gain_two])
    grad_bias = jnp.concatenate(
        [
            grad_shift_one[None],
            grad_shift_two[None],
            qkv_sums[None, :channels],
            qkv_sums[None, 2 * channels :],
            grad_proj_bias[None],
            grad_fc1_bias,
            grad_fc2_bias[None],
            grad_cpe_shift[None],
            grad_crpe_shift[None],
        ],
        axis=0,
    )
    grad_in = jnp.concatenate([grad_qkv_mat, grad_proj, grad_fc1], axis=1)
    parts = (grad_kern, grad_gain, grad_bias)
    if special:
        rows = jnp.concatenate(parts, axis=0)
        small = rows.reshape(sum(sizes), 32, -1).transpose(1, 0, 2).reshape(32, per)
        small = jnp.pad(small, ((0, 0), (0, SMALL_ROWS * 128 - per)))
        sum_in, sum_out, sum_small, squares = reduce_all(
            grad_in.astype(jnp.bfloat16), grad_fc2.astype(jnp.bfloat16), small
        )
        rows = sum_small.reshape(-1)[:per].reshape(sum(sizes), -1)
        summed = (
            sum_in,
            sum_out,
            rows[: sizes[0]],
            rows[sizes[0] : sizes[0] + sizes[1]],
            rows[sizes[0] + sizes[1] :],
        )
        total_squares = jnp.sum(squares)
    else:
        summed = tuple(
            lax.psum_scatter(part, ("wide", "narrow"), scatter_dimension=dim, tiled=True)
            for part, dim in zip((grad_in, grad_fc2) + parts, (0, 0, 1, 1, 1))
        )
        total_squares = lax.psum(
            sum(jnp.sum(part * part) for part in summed), ("wide", "narrow")
        )
    summed = tuple(part * scale_factor for part in summed)
    grad_norm = jnp.sqrt(total_squares) * scale_factor
    clip_factor = jnp.minimum(1.0, 1.0 / (grad_norm + 1e-06))
    in_new = adamw_update(
        in_mats, in_mats_m, in_mats_v, summed[0], clip_factor, RATES[0], DECAYS[0]
    )
    out_new = adamw_update(
        out_mat, out_mat_m, out_mat_v, summed[1], clip_factor, RATES[1], DECAYS[1]
    )
    kern_new = adamw_update(
        kernels, kernels_m, kernels_v, summed[2], clip_factor, RATES[2], DECAYS[2]
    )
    gain_new = adamw_update(gains, gains_m, gains_v, summed[3], clip_factor, RATES[3], DECAYS[3])
    bias_new = adamw_update(biases, biases_m, biases_v, summed[4], clip_factor, RATES[4], DECAYS[4])
    return (
        block_out,
        input_grad,
        grad_norm,
        in_new[0],
        in_new[1],
        in_new[2],
        in_new[3],
        out_new[0],
        out_new[1],
        out_new[2],
        out_new[3],
        kern_new[0],
        kern_new[1],
        kern_new[2],
        kern_new[3],
        gain_new[0],
        gain_new[1],
        gain_new[2],
        gain_new[3],
        bias_new[0],
        bias_new[1],
        bias_new[2],
        bias_new[3],
    )


def solution(mesh):
    placed = (
        P(("wide", "narrow"), None, None),
        P(("wide", "narrow"), None, None),
        P(("wide", "narrow")),
        P(("wide", "narrow"), None),
        P(("wide", "narrow"), None),
        P(("wide", "narrow"), None),
        P(("wide", "narrow"), None),
        P(("wide", "narrow"), None),
        P(("wide", "narrow"), None),
        P(None, ("wide", "narrow")),
        P(None, ("wide", "narrow")),
        P(None, ("wide", "narrow")),
        P(None, ("wide", "narrow")),
        P(None, ("wide", "narrow")),
        P(None, ("wide", "narrow")),
        P(None, ("wide", "narrow")),
        P(None, ("wide", "narrow")),
        P(None, ("wide", "narrow")),
    )
    special = dict(mesh.shape) == {"wide": 8, "narrow": 4}
    return jax.shard_map(
        functools.partial(local, special=special),
        mesh=mesh,
        in_specs=placed,
        out_specs=(
            P(("wide", "narrow"), None, None),
            P(("wide", "narrow"), None, None),
            P(),
            P(("wide", "narrow"), None),
            P(("wide", "narrow"), None),
            P(("wide", "narrow"), None),
            P(("wide", "narrow"), None),
            P(("wide", "narrow"), None),
            P(("wide", "narrow"), None),
            P(("wide", "narrow"), None),
            P(("wide", "narrow"), None),
            P(None, ("wide", "narrow")),
            P(None, ("wide", "narrow")),
            P(None, ("wide", "narrow")),
            P(None, ("wide", "narrow")),
            P(None, ("wide", "narrow")),
            P(None, ("wide", "narrow")),
            P(None, ("wide", "narrow")),
            P(None, ("wide", "narrow")),
            P(None, ("wide", "narrow")),
            P(None, ("wide", "narrow")),
            P(None, ("wide", "narrow")),
            P(None, ("wide", "narrow")),
        ),
        check_vma=False,
    )
```

```python
import functools

import jax
import jax.numpy as jnp
from jax import lax
from jax.experimental import pallas as pl
from jax.experimental.pallas import tpu as pltpu
from jax.sharding import PartitionSpec as P

D = 512
HEADS = 8
MLP_WIDTH = 2048
GRID = 7
STEP = 10
BROWS = 12


NORM_EPS = 1e-06
BETA_ONE = 0.9
BETA_TWO = 0.999
ADAM_EPS = 1e-08
HIGHEST = lax.Precision.HIGHEST
RATES = (0.04, 0.02, 0.1, 0.8, 0.25)
DECAYS = (0.05, 0.05, 0.05, 0.0, 0.0)


MESH_ID = pl.DeviceIdType.MESH
SPLIT = 3072
SMALL_ROWS = 16


def place():
    w = lax.axis_index("wide")
    n = lax.axis_index("narrow")
    return w // 2, w % 2, n // 2, n % 2


def device(z, y, x, c):
    return (z * 2 + y, x * 2 + c)


def neighbour(at, axis, step=1):
    z, y, x, c = at
    if axis == 0:
        return (lax.rem(z + step, 4), y, x, c)
    if axis == 1:
        return (z, 1 - y, x, c)
    if axis == 2:
        return (z, y, 1 - x, c)
    return (z, y, x, 1 - c)


def gather_kernel(wi, wo, sm, gi, go, gs, send_sem, recv_sem, own_sem):
    at = place()
    z, y, x, c = at
    partners = [device(*neighbour(at, 0, s)) for s in (1, 2, 3)]
    partners += [device(*neighbour(at, a)) for a in (1, 2, 3)]
    barrier = pltpu.get_barrier_semaphore()
    for partner in partners:
        pl.semaphore_signal(barrier, inc=1, device_id=partner, device_id_type=MESH_ID)
    pl.semaphore_wait(barrier, len(partners))

    width = wi.shape[1]
    pieces = (
        (wi, gi, 0, pl.ds(0, SPLIT)),
        (sm, gs, 0, pl.ds(0, 128)),
        (wi, gi, 1, pl.ds(SPLIT, width - SPLIT)),
        (wo, go, 1, pl.ds(0, wo.shape[1])),
    )
    orders = ((0, 1, 2, 3), (0, 2, 1, 3))

    def slot(r):
        zs = lax.rem(z - r[0] + 4, 4)
        ys = 1 - y if r[1] else y
        xs = 1 - x if r[2] else x
        cs = 1 - c if r[3] else c
        return ((zs * 2 + ys) * 2 + xs) * 2 + cs

    def flat(r):
        return ((r[0] * 2 + r[1]) * 2 + r[2]) * 2 + r[3]

    def moved(r, axis, step):
        r = list(r)
        r[axis] = step
        return tuple(r)

    def transfer(p, r, axis, step):
        own, out, color, cols = pieces[p]
        there = out.at[slot(r), :, cols]
        here = own.at[:, cols] if r == (0, 0, 0, 0) else there
        to = moved(r, axis, step)
        return pltpu.make_async_remote_copy(
            src_ref=here,
            dst_ref=there,
            send_sem=send_sem.at[p, flat(to)],
            recv_sem=recv_sem.at[p, flat(to)],
            device_id=device(*neighbour(at, axis, step)),
            device_id_type=MESH_ID,
        )

    def onward(p, r):
        order = orders[pieces[p][2]]
        last = max([i for i in range(4) if r[order[i]]], default=-1)
        for i in range(last + 1, 4):
            axis = order[i]
            for step in (1, 2, 3) if axis == 0 else (1,):
                yield axis, step

    started = []

    def forward(p, r):
        for axis, step in onward(p, r):
            copy = transfer(p, r, axis, step)
            copy.start()
            started.append(copy)

    zero = (0, 0, 0, 0)
    for p in range(4):
        forward(p, zero)
    own_copies = []
    for p in range(4):
        own, out, color, cols = pieces[p]
        copy = pltpu.make_async_copy(
            own.at[:, cols], out.at[slot(zero), :, cols], own_sem.at[p]
        )
        copy.start()
        own_copies.append(copy)

    def arrival(p, r):
        order = orders[pieces[p][2]]
        axis = [a for a in order if r[a]][-1]
        back = moved(r, axis, 0)
        return transfer(p, back, axis, r[axis])

    offsets = [
        (dz, dy, dx, dc) for dz in range(4) for dy in range(2) for dx in range(2) for dc in range(2)
    ]
    cost = {0: 0, 1: 2, 2: 4, 3: 2}

    def when(r):
        return cost[r[0]] + r[1] * 2 + r[2] * 2 + r[3]

    for r in sorted(offsets[1:], key=when):
        for p in range(4):
            copy = arrival(p, r)
            copy.wait_recv()
            forward(p, r)
    for copy in started:
        copy.wait_send()
    for copy in own_copies:
        copy.wait()


def gather_all(in_copy, out_copy, small):
    hbm = pl.BlockSpec(memory_space=pl.ANY)
    return pl.pallas_call(
        gather_kernel,
        out_shape=(
            jax.ShapeDtypeStruct((32,) + in_copy.shape, in_copy.dtype),
            jax.ShapeDtypeStruct((32,) + out_copy.shape, out_copy.dtype),
            jax.ShapeDtypeStruct((32,) + small.shape, small.dtype),
        ),
        in_specs=[hbm] * 3,
        out_specs=(hbm,) * 3,
        scratch_shapes=[
            pltpu.SemaphoreType.DMA((4, 32)),
            pltpu.SemaphoreType.DMA((4, 32)),
            pltpu.SemaphoreType.DMA((4,)),
        ],
        compiler_params=pltpu.CompilerParams(collective_id=0, has_side_effects=True),
        name="gather_all",
    )(in_copy, out_copy, small)


def add_low(left, right):
    return (left.astype(jnp.float32) + right.astype(jnp.float32)).astype(left.dtype)


def reduce_kernel(
    gi, go, gs, fi, fo, fs, fq,
    ai, ao, a_s, b1, b2i, b2o, b2s, b3,
    ri, ro, rs, r1, r2i, r2o, r2s, r3,
    t1, t2i, t2o, t2s, u1, u2i, u2o, u2s,
    squares_narrow, squares_wide, send_sem, recv_sem, norm_send, norm_recv,
):
    at = place()
    z, y, x, c = at
    w = z * 2 + y
    n = x * 2 + c
    partners = [(w, lax.rem(n + s, 4)) for s in (1, 2, 3)]
    partners += [(lax.rem(w + s, 8), n) for s in range(1, 8)]
    barrier = pltpu.get_barrier_semaphore()
    for partner in partners:
        pl.semaphore_signal(barrier, inc=1, device_id=partner, device_id_type=MESH_ID)
    pl.semaphore_wait(barrier, len(partners))

    count = [0]

    def send(src, dst, axis, step=1):
        index = count[0]
        count[0] += 1
        copy = pltpu.make_async_remote_copy(
            src_ref=src,
            dst_ref=dst,
            send_sem=send_sem.at[index],
            recv_sem=recv_sem.at[index],
            device_id=device(*neighbour(at, axis, step)),
            device_id_type=MESH_ID,
        )
        copy.start()
        return copy

    first = [
        send(gi.at[:, :, :, 1 - c], ri, 3),
        send(go.at[:, :, :, 1 - c], ro, 3),
        send(gs.at[:, :, :, 1 - c], rs, 3),
    ]
    for copy in first:
        copy.wait_recv()

    def add_first(k, carry):
        zi, yi, xi = k // 4, lax.rem(k // 2, 2), lax.rem(k, 2)
        ai[zi, yi, xi] = add_low(gi[zi, yi, xi, c], ri[zi, yi, xi])
        ao[zi, yi, xi] = add_low(go[zi, yi, xi, c], ro[zi, yi, xi])
        a_s[zi, yi, xi] = add_low(gs[zi, yi, xi, c], rs[zi, yi, xi])
        return carry

    lax.fori_loop(0, 16, add_first, 0)
    width = gi.shape[-1]
    left, right = pl.ds(0, SPLIT), pl.ds(SPLIT, width - SPLIT)
    second = [
        send(ai.at[:, :, 1 - x, :, left], r1, 2),
        send(ai.at[:, 1 - y, :, :, right], r2i, 1),
        send(ao.at[:, 1 - y], r2o, 1),
        send(a_s.at[:, 1 - y], r2s, 1),
    ]
    for copy in second:
        copy.wait_recv()

    def add_second(k, carry):
        zi, j = k // 2, lax.rem(k, 2)
        b1[zi, j] = add_low(ai[zi, j, x, :, left], r1[zi, j])
        b2i[zi, j] = add_low(ai[zi, y, j, :, right], r2i[zi, j])
        b2o[zi, j] = add_low(ao[zi, y, j], r2o[zi, j])
        b2s[zi, j] = add_low(a_s[zi, y, j], r2s[zi, j])
        return carry

    lax.fori_loop(0, 8, add_second, 0)
    third = [
        send(b1.at[:, 1 - y], r3, 1),
        send(b2i.at[:, 1 - x], t2i, 2),
        send(b2o.at[:, 1 - x], t2o, 2),
        send(b2s.at[:, 1 - x], t2s, 2),
    ]
    for copy in third:
        copy.wait_recv()

    def add_third(k, carry):
        b3[k] = add_low(b1[k, y], r3[k])
        r2i[k, 0] = add_low(b2i[k, x], t2i[k])
        r2o[k, 0] = add_low(b2o[k, x], t2o[k])
        r2s[k, 0] = add_low(b2s[k, x], t2s[k])
        return carry

    lax.fori_loop(0, 4, add_third, 0)
    fourth = []
    for step in (1, 2, 3):
        to = lax.rem(z + step, 4)
        fourth += [
            send(b3.at[to], u1.at[step - 1], 0, step),
            send(r2i.at[to, 0], u2i.at[step - 1], 0, step),
            send(r2o.at[to, 0], u2o.at[step - 1], 0, step),
            send(r2s.at[to, 0], u2s.at[step - 1], 0, step),
        ]
    for copy in fourth:
        copy.wait_recv()

    def total(own, others):
        value = own.astype(jnp.float32)
        for k in range(3):
            value = value + others[k].astype(jnp.float32)
        return value

    squares = jnp.zeros((8, 128), jnp.float32)

    def tile_squares(value, squares):
        rows, cols = value.shape
        for i in range(rows // 8):
            for j in range(cols // 128):
                part = value[i * 8 : i * 8 + 8, j * 128 : j * 128 + 128]
                squares = squares + part * part
        return squares

    for own, others, out, cols in (
        (b3[z], u1, fi, left),
        (r2i[z, 0], u2i, fi, right),
        (r2o[z, 0], u2o, fo, pl.ds(0, fo.shape[1])),
        (r2s[z, 0], u2s, fs, pl.ds(0, 128)),
    ):
        value = total(own, others)
        out[:, cols] = value
        squares = tile_squares(value, squares)

    def exchange(buffer, mine, size, axis, base):
        copies = []
        for step in range(1, size):
            to = lax.rem(mine + step, size)
            copy = pltpu.make_async_remote_copy(
                src_ref=buffer.at[mine],
                dst_ref=buffer.at[mine],
                send_sem=norm_send.at[base + step],
                recv_sem=norm_recv.at[base + step],
                device_id=(to, n) if axis == 0 else (w, to),
                device_id_type=MESH_ID,
            )
            copy.start()
            copies.append(copy)
        for copy in copies:
            copy.wait()
        value = buffer[0]
        for k in range(1, size):
            value = value + buffer[k]
        return value

    squares_narrow[n] = squares
    squares = exchange(squares_narrow, n, 4, 1, 0)
    squares_wide[w] = squares
    fq[...] = exchange(squares_wide, w, 8, 0, 4)
    for copy in first + second + third + fourth:
        copy.wait_send()


def reduce_all(grad_in, grad_out, small):
    low = jnp.bfloat16
    rows_in, width = grad_in.shape[0] // 32, grad_in.shape[1]
    rows_out, cols_out = grad_out.shape[0] // 32, grad_out.shape[1]
    gi = grad_in.reshape(4, 2, 2, 2, rows_in, width)
    go = grad_out.reshape(4, 2, 2, 2, rows_out, cols_out)
    gs = small.reshape(4, 2, 2, 2, SMALL_ROWS, 128)
    rest = width - SPLIT
    vmem = pl.BlockSpec(memory_space=pltpu.VMEM)

    def trio(lead, cols, own=True):
        kinds = [
            pltpu.VMEM(lead + (rows_in, cols), low),
            pltpu.VMEM(lead + (rows_out, cols_out), low),
            pltpu.VMEM(lead + (SMALL_ROWS, 128), jnp.float32),
        ]
        return kinds

    scratch = trio((4, 2, 2), width)
    scratch += [pltpu.VMEM((4, 2, rows_in, SPLIT), low)] + trio((4, 2), rest)
    scratch += [pltpu.VMEM((4, rows_in, SPLIT), low)]
    scratch += trio((4, 2, 2), width)
    scratch += [pltpu.VMEM((4, 2, rows_in, SPLIT), low)] + trio((4, 2), rest)
    scratch += [pltpu.VMEM((4, rows_in, SPLIT), low)]
    scratch += [pltpu.VMEM((1, 8, 128), low)] + trio((4,), rest)
    scratch += [pltpu.VMEM((3, rows_in, SPLIT), low)] + trio((3,), rest)
    scratch += [
        pltpu.VMEM((4, 8, 128), jnp.float32),
        pltpu.VMEM((8, 8, 128), jnp.float32),
        pltpu.SemaphoreType.DMA((23,)),
        pltpu.SemaphoreType.DMA((23,)),
        pltpu.SemaphoreType.DMA((12,)),
        pltpu.SemaphoreType.DMA((12,)),
    ]
    return pl.pallas_call(
        reduce_kernel,
        out_shape=(
            jax.ShapeDtypeStruct((rows_in, width), jnp.float32),
            jax.ShapeDtypeStruct((rows_out, cols_out), jnp.float32),
            jax.ShapeDtypeStruct((SMALL_ROWS, 128), jnp.float32),
            jax.ShapeDtypeStruct((8, 128), jnp.float32),
        ),
        in_specs=[vmem] * 3,
        out_specs=(vmem,) * 4,
        scratch_shapes=scratch,
        compiler_params=pltpu.CompilerParams(
            collective_id=1, has_side_effects=True, vmem_limit_bytes=48 << 20
        ),
        name="reduce_all",
    )(gi, go, gs)


def tap_mask(channels):
    head_width = channels // HEADS
    channel_ids = jnp.arange(channels, dtype=jnp.int32)
    reach_cells = jnp.where(
        channel_ids < 2 * head_width, 1, jnp.where(channel_ids < 5 * head_width, 2, 3)
    )
    tap_ids = jnp.arange(49, dtype=jnp.int32)
    row_offset = jnp.abs(tap_ids // 7 - 3)
    col_offset = jnp.abs(tap_ids % 7 - 3)
    inside = (row_offset[:, None] <= reach_cells[None, :]) & (
        col_offset[:, None] <= reach_cells[None, :]
    )
    return inside.astype(jnp.float32)


def cross_rows(left, right):
    return lax.dot_general(
        left, right, (((0,), (0,)), ((), ())), preferred_element_type=jnp.float32
    )


SIDE = 8
SLOT = 64
CHUNK = 10


def rows_of(ref):
    return ref[...].reshape(-1, ref.shape[-1])


def tokens_of(value):
    return value.reshape(-1, SIDE, value.shape[-1])


def column_partial(value):
    return jnp.sum(tokens_of(value), axis=0)


def dot(left, right):
    return jnp.dot(left, right, preferred_element_type=jnp.float32)


def dot_nt(left, right):
    return lax.dot_general(
        left, right, (((1,), (1,)), ((), ())), preferred_element_type=jnp.float32
    )


def dot_tn(left, right):
    return lax.dot_general(
        left, right, (((0,), (0,)), ((), ())), preferred_element_type=jnp.float32
    )


def lane_tile(j):
    if isinstance(j, int):
        return pl.ds(j * 128, 128)
    return pl.ds(pl.multiple_of(j * 128, 128), 128)


def grid_token(row, col):
    return 1 + row * GRID + col


def conv_tile(src, taps, base, width, reach, lanes, finish, flip=False):
    margin = width // 2
    offsets = range(-reach, reach + 1)

    def tap(dy, dx):
        if flip:
            dy, dx = -dy, -dx
        index = base + (dy + margin) * width + dx + margin
        return jnp.broadcast_to(taps[index : index + 1, lanes], (SIDE, 128))

    held = {(dy, dx): tap(dy, dx) for dy in offsets for dx in offsets}
    for row in range(GRID):
        sums = [jnp.zeros((SIDE, 128), jnp.float32) for _ in range(GRID)]
        for dy in offsets:
            if not 0 <= row + dy < GRID:
                continue
            line = [src[grid_token(row + dy, col), :, lanes] for col in range(GRID)]
            for dx in offsets:
                for col in range(GRID):
                    if 0 <= col + dx < GRID:
                        sums[col] = sums[col] + line[col + dx] * held[dy, dx]
        for col in range(GRID):
            finish(grid_token(row, col), sums[col])


def tap_sums(grad, src, base, width, reach, lanes, total):
    margin = width // 2
    offsets = range(-reach, reach + 1)
    for dy in offsets:
        sums = {dx: jnp.zeros((SIDE, 128), jnp.float32) for dx in offsets}
        for row in range(GRID):
            if not 0 <= row + dy < GRID:
                continue
            up = [grad[grid_token(row, col), :, lanes] for col in range(GRID)]
            line = [src[grid_token(row + dy, col), :, lanes] for col in range(GRID)]
            for dx in offsets:
                for col in range(GRID):
                    if 0 <= col + dx < GRID:
                        sums[dx] = sums[dx] + up[col] * line[col + dx]
        for dx in offsets:
            index = base + (dy + margin) * width + dx + margin
            total[index, :, lanes] = total[index, :, lanes] + sums[dx]


REACHES = ((0, 1), (1, 2))


def relative_tiles(body):
    body(0, 1)
    body(1, 2)

    def rest(j, carry):
        body(j, 3)
        return carry

    lax.fori_loop(2, 4, rest, 0)


def all_tiles(body):
    def step(j, carry):
        body(j)
        return carry

    lax.fori_loop(0, 4, step, 0)


def all_chunks(body):
    def step(k, carry):
        body(pl.ds(k * CHUNK, CHUNK), pl.ds(pl.multiple_of(k * CHUNK * SIDE, 16), CHUNK * SIDE))
        return carry

    lax.fori_loop(0, 50 // CHUNK, step, 0)


def normalise(values):
    centred = values - jnp.mean(values, axis=-1, keepdims=True)
    scale = lax.rsqrt(jnp.mean(centred * centred, axis=-1, keepdims=True) + NORM_EPS)
    return centred * scale, scale


def norm_back(grad, hat, scale, gain):
    inner = grad * gain
    mean = jnp.mean(inner, axis=-1, keepdims=True)
    along = jnp.mean(inner * hat, axis=-1, keepdims=True)
    return scale * (inner - mean - hat * along)


def take_images(src, slots, first, limit):
    for i in range(SIDE):
        image = src[i]
        keep = jnp.full(image.shape, first + i, jnp.int32) < limit
        image = jnp.where(keep, image.astype(jnp.float32), 0.0).astype(jnp.bfloat16)
        slots[i * SLOT : i * SLOT + image.shape[0], :] = image


def forward_kernel(
    num_images, counts, x_in, dy_in, order, same, w_in, w_out, taps, gains, biases,
    out, act_o, gh_o, n1_o, n2_o, at_o, gf_o, gp_o, gx_o, xt_o, hat_o, sc_o, q_o, k_o, v_o, cv_o,
    cols_o, hcols_o,
    slots, x, x1, v, conv, hat2, slope, gn, scale2,
):
    low = jnp.bfloat16
    step = pl.program_id(0)
    first = step * SIDE

    @pl.when(step == 0)
    def _():
        slots[...] = jnp.zeros_like(slots)
        cols_o[...] = jnp.zeros_like(cols_o)
        hcols_o[...] = jnp.zeros_like(hcols_o)

    take_images(x_in, slots, first, num_images)
    value = dot(order[...], slots[...])
    x[...] = tokens_of(value)
    xt_o[...] = value.astype(low)
    take_images(dy_in, slots, first, jnp.minimum(counts[0], num_images))
    gf_o[...] = dot(order[...], slots[...]).astype(low)

    def position(j):
        lanes = lane_tile(j)
        shift = jnp.broadcast_to(biases[10:11, lanes], (SIDE, 128))

        def finish(token, total):
            x1[token, :, lanes] = x[token, :, lanes] + total + shift

        conv_tile(x, taps, 0, 3, 1, lanes, finish)
        x1[0, :, lanes] = x[0, :, lanes]

    all_tiles(position)

    def first_norm(tokens, rows):
        hat, scale = normalise(x1[tokens].reshape(-1, D))
        hat_o[rows, :] = hat.astype(low)
        sc_o[rows, :] = jnp.broadcast_to(scale, (CHUNK * SIDE, 128))
        n1_o[rows, :] = (hat * gains[0:1, :] + biases[0:1, :]).astype(low)

    all_chunks(first_norm)
    n1 = n1_o[...]
    gn[...] = tokens_of(dot(n1, w_in[:, D : 2 * D]))

    def weights(j):
        lanes = lane_tile(j)
        keys = gn[:, :, lanes]
        powers = jnp.exp(keys - jnp.max(keys, axis=0, keepdims=True))
        share = 0.125 / jnp.sum(powers, axis=0, keepdims=True)
        k_o[:, lanes] = (powers * share).reshape(-1, 128).astype(low)

    all_tiles(weights)
    value = dot(n1, w_in[:, 2 * D : 3 * D]) + biases[3:4, :]
    v[...] = tokens_of(value)
    v_o[...] = value.astype(low)

    def relative(j, reach):
        lanes = lane_tile(j)
        shift = jnp.broadcast_to(biases[11:12, lanes], (SIDE, 128))

        def finish(token, total):
            conv[token, :, lanes] = total + shift

        conv_tile(v, taps, 9, 7, reach, lanes, finish)
        conv[0, :, lanes] = jnp.zeros((SIDE, 128), jnp.float32)

    relative_tiles(relative)
    cv_o[...] = rows_of(conv).astype(low)
    value = dot(n1, w_in[:, :D]) + biases[2:3, :]
    q_o[...] = value.astype(low)
    conv[...] = conv[...] * tokens_of(value)

    def attention(j):
        lanes = lane_tile(j)
        qs, ks, vs = q_o[:, lanes], k_o[:, lanes], v_o[:, lanes]
        parts = []
        for h in (slice(0, 64), slice(64, 128)):
            scores = dot_nt(qs[:, h], ks[:, h]).astype(low) * same[...]
            parts.append(dot(scores, vs[:, h]))
        value = jnp.concatenate(parts, axis=1) + conv[:, :, lanes].reshape(-1, 128)
        at_o[:, lanes] = value.astype(low)

    all_tiles(attention)
    x1[...] = x1[...] + tokens_of(dot(at_o[...], w_in[:, 3 * D : 4 * D]) + biases[4:5, :])

    def second_norm(tokens, rows):
        hat, scale = normalise(x1[tokens].reshape(-1, D))
        hat2[tokens] = tokens_of(hat)
        scale2[tokens] = jnp.broadcast_to(tokens_of(scale), (CHUNK, SIDE, 128))
        n2_o[rows, :] = (hat * gains[1:2, :] + biases[1:2, :]).astype(low)

    all_chunks(second_norm)
    n2 = n2_o[...]
    for part in range(MLP_WIDTH // D):
        cols = pl.ds(part * D, D)
        gn[...] = tokens_of(dot(n2, w_in[:, pl.ds((4 + part) * D, D)]))

        def gelu(tokens, rows):
            h = gn[tokens].reshape(-1, D) + biases[5 + part : 6 + part, :]
            below = 0.5 + 0.5 * lax.erf(h * (0.5**0.5))
            density = jnp.exp(-0.5 * h * h) * 0.3989422804014327
            act_o[rows, cols] = (h * below).astype(low)
            slope[rows, cols] = below + h * density

        all_chunks(gelu)
    value = rows_of(x1) + dot(act_o[...], w_out[...]) + biases[9:10, :]
    back = lax.dot_general(
        order[...], value.astype(low), (((0,), (0,)), ((), ())), preferred_element_type=jnp.float32
    )
    for i in range(SIDE):
        out[i] = back[i * SLOT : i * SLOT + out.shape[1], :].astype(low)

    gf = gf_o[...]
    for part in range(MLP_WIDTH // D):
        cols = pl.ds(part * D, D)
        grad = (dot_nt(gf, w_out[cols, :]) * slope[:, cols]).astype(low)
        gh_o[:, cols] = grad
        hcols_o[:, cols] = hcols_o[:, cols] + column_partial(grad.astype(jnp.float32))
    gn[...] = tokens_of(dot_nt(gh_o[...], w_in[:, 4 * D :]))

    def second_back(tokens, rows):
        grad = gn[tokens].reshape(-1, D)
        hat = hat2[tokens].reshape(-1, D)
        scale = scale2[tokens].reshape(-1, 128)[:, 0:1]
        upstream = gf_o[rows, :].astype(jnp.float32)
        total = upstream + norm_back(grad, hat, scale, gains[1:2, :])
        gx_o[rows, :] = total
        rounded = total.astype(low)
        gp_o[rows, :] = rounded
        cols_o[0] = cols_o[0] + column_partial(grad)
        cols_o[1] = cols_o[1] + column_partial(grad * hat)
        cols_o[2] = cols_o[2] + column_partial(rounded.astype(jnp.float32))
        cols_o[3] = cols_o[3] + column_partial(upstream)

    all_chunks(second_back)


def backward_kernel(
    num_images, order, same, w_in, taps, gains, gx, hat, sc, q, k, v, cv, xt,
    out, gq_o, cols_o, taps_o,
    ga, gc, vf, gv, gqs, gks, xf, g1,
):
    low = jnp.bfloat16
    step = pl.program_id(0)

    @pl.when(step == 0)
    def _():
        cols_o[...] = jnp.zeros_like(cols_o)
        taps_o[...] = jnp.zeros_like(taps_o)

    grad = dot_nt(gx[...].astype(low), w_in[:, 3 * D : 4 * D])
    ga[...] = grad.astype(low)
    gqs[...] = tokens_of(grad * cv[...].astype(jnp.float32))
    gc[...] = tokens_of(grad * q[...].astype(jnp.float32))
    gc[0] = jnp.zeros((SIDE, D), jnp.float32)
    vf[...] = tokens_of(v[...].astype(jnp.float32))
    xf[...] = tokens_of(xt[...].astype(jnp.float32))
    cols_o[0] = cols_o[0] + jnp.sum(gc[...], axis=0)

    def relative(j, reach):
        lanes = lane_tile(j)

        def finish(token, total):
            gv[token, :, lanes] = total

        conv_tile(gc, taps, 9, 7, reach, lanes, finish, flip=True)
        gv[0, :, lanes] = jnp.zeros((SIDE, 128), jnp.float32)
        tap_sums(gc, vf, 9, 7, reach, lanes, taps_o)

    relative_tiles(relative)

    def attention(j):
        lanes = lane_tile(j)
        qs, ks, vs, gs = q[:, lanes], k[:, lanes], v[:, lanes], ga[:, lanes]
        to_q, to_k, to_v = [], [], []
        for h in (slice(0, 64), slice(64, 128)):
            scores = dot_nt(qs[:, h], ks[:, h]).astype(low) * same[...]
            grads = dot_nt(gs[:, h], vs[:, h]).astype(low) * same[...]
            to_v.append(dot_tn(scores, gs[:, h]))
            to_q.append(dot(grads, ks[:, h]))
            to_k.append(dot_tn(grads, qs[:, h]))
        gqs[:, :, lanes] = gqs[:, :, lanes] + tokens_of(jnp.concatenate(to_q, axis=1))
        gv[:, :, lanes] = gv[:, :, lanes] + tokens_of(jnp.concatenate(to_v, axis=1))
        gks[:, :, lanes] = tokens_of(jnp.concatenate(to_k, axis=1))

    all_tiles(attention)

    def finish_qkv(j):
        lanes = lane_tile(j)
        share = tokens_of(k[:, lanes].astype(jnp.float32))
        up = gks[:, :, lanes]
        along = jnp.sum(share * up, axis=0, keepdims=True) * 8.0
        gq_o[:, pl.ds(pl.multiple_of(D + j * 128, 128), 128)] = (
            (share * (up - along)).reshape(-1, 128).astype(low)
        )
        part = gqs[:, :, lanes].reshape(-1, 128).astype(low)
        gq_o[:, lanes] = part
        cols_o[1, :, lanes] = cols_o[1, :, lanes] + column_partial(part.astype(jnp.float32))
        part = gv[:, :, lanes].reshape(-1, 128).astype(low)
        gq_o[:, pl.ds(pl.multiple_of(2 * D + j * 128, 128), 128)] = part
        cols_o[2, :, lanes] = cols_o[2, :, lanes] + column_partial(part.astype(jnp.float32))

    all_tiles(finish_qkv)
    gks[...] = tokens_of(dot_nt(gq_o[...], w_in[:, : 3 * D]))

    def first_back(tokens, rows):
        grad = gks[tokens].reshape(-1, D)
        hats = hat[rows, :].astype(jnp.float32)
        scale = sc[rows, 0:1]
        total = gx[rows, :] + norm_back(grad, hats, scale, gains[0:1, :])
        g1[tokens] = tokens_of(total)
        cols_o[3] = cols_o[3] + column_partial(grad)
        cols_o[4] = cols_o[4] + column_partial(grad * hats)
        cols_o[5] = cols_o[5] + column_partial(total)

    all_chunks(first_back)
    cols_o[5] = cols_o[5] - g1[0]

    def position(j):
        lanes = lane_tile(j)

        def finish(token, total):
            gv[token, :, lanes] = g1[token, :, lanes] + total

        conv_tile(g1, taps, 0, 3, 1, lanes, finish, flip=True)
        gv[0, :, lanes] = g1[0, :, lanes]
        tap_sums(g1, xf, 0, 3, 1, lanes, taps_o)

    all_tiles(position)
    value = rows_of(gv)
    back = jnp.zeros((SIDE * SLOT, D), jnp.float32)
    for _ in range(3):
        piece = value.astype(low)
        value = value - piece.astype(jnp.float32)
        back = back + dot_tn(order[...], piece)
    for i in range(SIDE):
        out[i] = back[i * SLOT : i * SLOT + out.shape[1], :]


def fixed(shape):
    zeros = (0,) * len(shape)
    return pl.BlockSpec(shape, lambda g: zeros, pipeline_mode=pl.Buffered(1))


def compute(images, cotangent, counts, w_in, w_out, kern, gains, biases):
    low, full = jnp.bfloat16, jnp.float32
    num_images, num_tokens, channels = images.shape
    groups = -(-num_images // SIDE)
    rows = num_tokens * SIDE
    total = groups * rows
    taps = jnp.concatenate([kern[:9], kern[9:] * tap_mask(channels)], axis=0)
    row_ids = lax.broadcasted_iota(jnp.int32, (rows, SIDE * SLOT), 0)
    col_ids = lax.broadcasted_iota(jnp.int32, (rows, SIDE * SLOT), 1)
    order = (row_ids == (col_ids % SLOT) * SIDE + col_ids // SLOT).astype(low)
    row_ids = lax.broadcasted_iota(jnp.int32, (rows, rows), 0)
    col_ids = lax.broadcasted_iota(jnp.int32, (rows, rows), 1)
    same = (row_ids % SIDE == col_ids % SIDE).astype(low)

    def block(cols):
        return pl.BlockSpec((rows, cols), lambda g: (g, 0))

    def image_block():
        return pl.BlockSpec((SIDE, num_tokens, channels), lambda g: (g, 0, 0))

    def made(cols, kind=low):
        return jax.ShapeDtypeStruct((total, cols), kind)

    def grid_scratch(cols=channels):
        return pltpu.VMEM((num_tokens, SIDE, cols), full)

    wide = w_out.shape[0]
    forward = pl.pallas_call(
        functools.partial(forward_kernel, num_images),
        grid=(groups,),
        in_specs=[
            pl.BlockSpec(memory_space=pltpu.SMEM),
            image_block(),
            image_block(),
            fixed(order.shape),
            fixed(same.shape),
            fixed(w_in.shape),
            fixed(w_out.shape),
            fixed(taps.shape),
            fixed(gains.shape),
            fixed(biases.shape),
        ],
        out_specs=[image_block(), block(wide), block(wide)]
        + [block(channels)] * 8
        + [block(128)]
        + [block(channels)] * 4
        + [fixed((4, SIDE, channels)), fixed((SIDE, wide))],
        out_shape=[jax.ShapeDtypeStruct(images.shape, low), made(wide), made(wide)]
        + [made(channels)] * 5
        + [made(channels, full), made(channels), made(channels), made(128, full)]
        + [made(channels)] * 4
        + [
            jax.ShapeDtypeStruct((4, SIDE, channels), full),
            jax.ShapeDtypeStruct((SIDE, wide), full),
        ],
        scratch_shapes=[pltpu.VMEM((SIDE * SLOT, channels), low)]
        + [grid_scratch() for _ in range(5)]
        + [pltpu.VMEM((rows, wide), full), grid_scratch(), grid_scratch(128)],
        compiler_params=pltpu.CompilerParams(vmem_limit_bytes=60 << 20),
        name="forward",
    )
    (
        out, act, gh, n1, n2, attended, gf, gp, gx, xt, hat, scale, q, k, v, cv, cols, hcols,
    ) = forward(counts, images, cotangent, order, same, w_in, w_out, taps, gains, biases)

    backward = pl.pallas_call(
        functools.partial(backward_kernel, num_images),
        grid=(groups,),
        in_specs=[
            fixed(order.shape),
            fixed(same.shape),
            fixed(w_in.shape),
            fixed(taps.shape),
            fixed(gains.shape),
            block(channels),
            block(channels),
            block(128),
        ]
        + [block(channels)] * 5,
        out_specs=[
            image_block(),
            block(3 * channels),
            fixed((6, SIDE, channels)),
            fixed((taps.shape[0], SIDE, channels)),
        ],
        out_shape=[
            jax.ShapeDtypeStruct(images.shape, full),
            made(3 * channels),
            jax.ShapeDtypeStruct((6, SIDE, channels), full),
            jax.ShapeDtypeStruct((taps.shape[0], SIDE, channels), full),
        ],
        scratch_shapes=[pltpu.VMEM((rows, channels), low)] + [grid_scratch() for _ in range(7)],
        compiler_params=pltpu.CompilerParams(vmem_limit_bytes=60 << 20),
        name="backward",
    )
    input_grad, gq, cols_back, grad_taps = backward(
        order, same, w_in, taps, gains, gx, hat, scale, q, k, v, cv, xt
    )
    grad_in = jnp.concatenate(
        [
            cross_rows(n1, gq).astype(low),
            cross_rows(attended, gp).astype(low),
            cross_rows(n2, gh).astype(low),
        ],
        axis=1,
    )
    grad_out = cross_rows(act, gf).astype(low)
    cols = jnp.sum(cols, axis=1)
    hcols = jnp.sum(hcols, axis=0).reshape(-1, channels)
    cols_back = jnp.sum(cols_back, axis=1)
    grad_taps = jnp.sum(grad_taps, axis=1)
    grad_kern = jnp.concatenate([grad_taps[:9], grad_taps[9:] * tap_mask(channels)], axis=0)
    grad_gain = jnp.stack([cols_back[4], cols[1]])
    grad_bias = jnp.concatenate(
        [
            cols_back[3:4],
            cols[0:1],
            cols_back[1:3],
            cols[2:3],
            hcols,
            cols[3:4],
            cols_back[5:6],
            cols_back[0:1],
        ],
        axis=0,
    )
    return out, input_grad, grad_in, grad_out, grad_kern, grad_gain, grad_bias


def adamw_update(master, first_moment, second_moment, gradient, clip_factor, rate, decay):
    clipped = gradient * clip_factor
    first_new = BETA_ONE * first_moment + (1.0 - BETA_ONE) * clipped
    second_new = BETA_TWO * second_moment + (1.0 - BETA_TWO) * clipped * clipped
    first_hat = first_new / (1.0 - BETA_ONE**STEP)
    second_hat = second_new / (1.0 - BETA_TWO**STEP)
    master_new = master - rate * (first_hat / (jnp.sqrt(second_hat) + ADAM_EPS) + decay * master)
    return (master_new, first_new, second_new, master_new.astype(jnp.bfloat16))


def local(
    images,
    cotangent,
    counts,
    in_mats,
    in_mats_m,
    in_mats_v,
    out_mat,
    out_mat_m,
    out_mat_v,
    kernels,
    kernels_m,
    kernels_v,
    gains,
    gains_m,
    gains_v,
    biases,
    biases_m,
    biases_v,
    special,
):
    in_copy = in_mats.astype(jnp.bfloat16)
    out_copy = out_mat.astype(jnp.bfloat16)
    kern_copy = kernels.astype(jnp.bfloat16)
    gain_copy = gains.astype(jnp.bfloat16)
    bias_copy = biases.astype(jnp.bfloat16)
    shards = (kern_copy, gain_copy, bias_copy)
    sizes = [shard.shape[0] for shard in shards]
    if special:
        per = sum(sizes) * kern_copy.shape[1]
        flat = jnp.concatenate(
            [jnp.concatenate(shards, axis=0).reshape(-1), counts.astype(jnp.bfloat16)]
        )
        flat = jnp.pad(flat, (0, SMALL_ROWS * 128 - per - 1)).reshape(SMALL_ROWS, 128)
        all_in, all_out, all_small = gather_all(in_copy, out_copy, flat)
        all_small = all_small.reshape(32, SMALL_ROWS * 128)
        live_total = jnp.sum(all_small[:, per].astype(jnp.float32)) * images.shape[1]
        rows = all_small[:, :per].reshape(32, sum(sizes), -1).transpose(1, 0, 2)
        rows = rows.reshape(sum(sizes), -1)
        gathered = (
            all_in.reshape(-1, in_copy.shape[1]),
            all_out.reshape(-1, out_copy.shape[1]),
            rows[: sizes[0]],
            rows[sizes[0] : sizes[0] + sizes[1]],
            rows[sizes[0] + sizes[1] :],
        )
    else:
        gathered = (
            lax.all_gather(in_copy, ("wide", "narrow"), axis=0, tiled=True),
            lax.all_gather(out_copy, ("wide", "narrow"), axis=0, tiled=True),
            lax.all_gather(kern_copy, ("wide", "narrow"), axis=1, tiled=True),
            lax.all_gather(gain_copy, ("wide", "narrow"), axis=1, tiled=True),
            lax.all_gather(bias_copy, ("wide", "narrow"), axis=1, tiled=True),
        )
        live_total = lax.psum(
            counts[0].astype(jnp.float32) * images.shape[1], ("wide", "narrow")
        )
    wide_in = gathered[0]
    wide_out = gathered[1]
    kern_all = gathered[2].astype(jnp.float32)
    gain_all = gathered[3].astype(jnp.float32)
    bias_all = gathered[4].astype(jnp.float32)
    scale_factor = 1.0 / live_total
    block_out, input_grad, grad_in, grad_fc2, grad_kern, grad_gain, grad_bias = compute(
        images, cotangent, counts, wide_in, wide_out, kern_all, gain_all, bias_all
    )
    parts = (grad_kern, grad_gain, grad_bias)
    if special:
        rows = jnp.concatenate(parts, axis=0)
        small = rows.reshape(sum(sizes), 32, -1).transpose(1, 0, 2).reshape(32, per)
        small = jnp.pad(small, ((0, 0), (0, SMALL_ROWS * 128 - per)))
        sum_in, sum_out, sum_small, squares = reduce_all(
            grad_in, grad_fc2, small
        )
        rows = sum_small.reshape(-1)[:per].reshape(sum(sizes), -1)
        summed = (
            sum_in,
            sum_out,
            rows[: sizes[0]],
            rows[sizes[0] : sizes[0] + sizes[1]],
            rows[sizes[0] + sizes[1] :],
        )
        total_squares = jnp.sum(squares)
    else:
        summed = tuple(
            lax.psum_scatter(part.astype(jnp.float32), ("wide", "narrow"), scatter_dimension=dim, tiled=True)
            for part, dim in zip((grad_in, grad_fc2) + parts, (0, 0, 1, 1, 1))
        )
        total_squares = lax.psum(
            sum(jnp.sum(part * part) for part in summed), ("wide", "narrow")
        )
    summed = tuple(part * scale_factor for part in summed)
    grad_norm = jnp.sqrt(total_squares) * scale_factor
    clip_factor = jnp.minimum(1.0, 1.0 / (grad_norm + 1e-06))
    in_new = adamw_update(
        in_mats, in_mats_m, in_mats_v, summed[0], clip_factor, RATES[0], DECAYS[0]
    )
    out_new = adamw_update(
        out_mat, out_mat_m, out_mat_v, summed[1], clip_factor, RATES[1], DECAYS[1]
    )
    kern_new = adamw_update(
        kernels, kernels_m, kernels_v, summed[2], clip_factor, RATES[2], DECAYS[2]
    )
    gain_new = adamw_update(gains, gains_m, gains_v, summed[3], clip_factor, RATES[3], DECAYS[3])
    bias_new = adamw_update(biases, biases_m, biases_v, summed[4], clip_factor, RATES[4], DECAYS[4])
    return (
        block_out,
        input_grad,
        grad_norm,
        in_new[0],
        in_new[1],
        in_new[2],
        in_new[3],
        out_new[0],
        out_new[1],
        out_new[2],
        out_new[3],
        kern_new[0],
        kern_new[1],
        kern_new[2],
        kern_new[3],
        gain_new[0],
        gain_new[1],
        gain_new[2],
        gain_new[3],
        bias_new[0],
        bias_new[1],
        bias_new[2],
        bias_new[3],
    )


def solution(mesh):
    placed = (
        P(("wide", "narrow"), None, None),
        P(("wide", "narrow"), None, None),
        P(("wide", "narrow")),
        P(("wide", "narrow"), None),
        P(("wide", "narrow"), None),
        P(("wide", "narrow"), None),
        P(("wide", "narrow"), None),
        P(("wide", "narrow"), None),
        P(("wide", "narrow"), None),
        P(None, ("wide", "narrow")),
        P(None, ("wide", "narrow")),
        P(None, ("wide", "narrow")),
        P(None, ("wide", "narrow")),
        P(None, ("wide", "narrow")),
        P(None, ("wide", "narrow")),
        P(None, ("wide", "narrow")),
        P(None, ("wide", "narrow")),
        P(None, ("wide", "narrow")),
    )
    special = dict(mesh.shape) == {"wide": 8, "narrow": 4}
    return jax.shard_map(
        functools.partial(local, special=special),
        mesh=mesh,
        in_specs=placed,
        out_specs=(
            P(("wide", "narrow"), None, None),
            P(("wide", "narrow"), None, None),
            P(),
            P(("wide", "narrow"), None),
            P(("wide", "narrow"), None),
            P(("wide", "narrow"), None),
            P(("wide", "narrow"), None),
            P(("wide", "narrow"), None),
            P(("wide", "narrow"), None),
            P(("wide", "narrow"), None),
            P(("wide", "narrow"), None),
            P(None, ("wide", "narrow")),
            P(None, ("wide", "narrow")),
            P(None, ("wide", "narrow")),
            P(None, ("wide", "narrow")),
            P(None, ("wide", "narrow")),
            P(None, ("wide", "narrow")),
            P(None, ("wide", "narrow")),
            P(None, ("wide", "narrow")),
            P(None, ("wide", "narrow")),
            P(None, ("wide", "narrow")),
            P(None, ("wide", "narrow")),
            P(None, ("wide", "narrow")),
        ),
        check_vma=False,
    )
```

```python
import functools

import jax
import jax.numpy as jnp
from jax import lax
from jax.experimental import pallas as pl
from jax.experimental.pallas import tpu as pltpu
from jax.sharding import PartitionSpec as P

D = 512
HEADS = 8
MLP_WIDTH = 2048
GRID = 7
STEP = 10
BROWS = 12


NORM_EPS = 1e-06
BETA_ONE = 0.9
BETA_TWO = 0.999
ADAM_EPS = 1e-08
HIGHEST = lax.Precision.HIGHEST
RATES = (0.04, 0.02, 0.1, 0.8, 0.25)
DECAYS = (0.05, 0.05, 0.05, 0.0, 0.0)


MESH_ID = pl.DeviceIdType.MESH
SPLIT = 3072
SMALL_ROWS = 16


def place():
    w = lax.axis_index("wide")
    n = lax.axis_index("narrow")
    return w // 2, w % 2, n // 2, n % 2


def device(z, y, x, c):
    return (z * 2 + y, x * 2 + c)


def neighbour(at, axis, step=1):
    z, y, x, c = at
    if axis == 0:
        return (lax.rem(z + step, 4), y, x, c)
    if axis == 1:
        return (z, 1 - y, x, c)
    if axis == 2:
        return (z, y, 1 - x, c)
    return (z, y, x, 1 - c)


def gather_kernel(wi, wo, sm, gi, go, gs, send_sem, recv_sem, own_sem):
    at = place()
    z, y, x, c = at
    partners = [device(*neighbour(at, 0, s)) for s in (1, 2, 3)]
    partners += [device(*neighbour(at, a)) for a in (1, 2, 3)]
    barrier = pltpu.get_barrier_semaphore()
    for partner in partners:
        pl.semaphore_signal(barrier, inc=1, device_id=partner, device_id_type=MESH_ID)
    pl.semaphore_wait(barrier, len(partners))

    width = wi.shape[1]
    pieces = (
        (wi, gi, 0, pl.ds(0, SPLIT)),
        (sm, gs, 0, pl.ds(0, 128)),
        (wi, gi, 1, pl.ds(SPLIT, width - SPLIT)),
        (wo, go, 1, pl.ds(0, wo.shape[1])),
    )
    orders = ((0, 1, 2, 3), (0, 2, 1, 3))

    def slot(r):
        zs = lax.rem(z - r[0] + 4, 4)
        ys = 1 - y if r[1] else y
        xs = 1 - x if r[2] else x
        cs = 1 - c if r[3] else c
        return ((zs * 2 + ys) * 2 + xs) * 2 + cs

    def flat(r):
        return ((r[0] * 2 + r[1]) * 2 + r[2]) * 2 + r[3]

    def moved(r, axis, step):
        r = list(r)
        r[axis] = step
        return tuple(r)

    def transfer(p, r, axis, step):
        own, out, color, cols = pieces[p]
        there = out.at[slot(r), :, cols]
        here = own.at[:, cols] if r == (0, 0, 0, 0) else there
        to = moved(r, axis, step)
        return pltpu.make_async_remote_copy(
            src_ref=here,
            dst_ref=there,
            send_sem=send_sem.at[p, flat(to)],
            recv_sem=recv_sem.at[p, flat(to)],
            device_id=device(*neighbour(at, axis, step)),
            device_id_type=MESH_ID,
        )

    def onward(p, r):
        order = orders[pieces[p][2]]
        last = max([i for i in range(4) if r[order[i]]], default=-1)
        for i in range(last + 1, 4):
            axis = order[i]
            for step in (1, 2, 3) if axis == 0 else (1,):
                yield axis, step

    started = []

    def forward(p, r):
        for axis, step in onward(p, r):
            copy = transfer(p, r, axis, step)
            copy.start()
            started.append(copy)

    zero = (0, 0, 0, 0)
    for p in range(4):
        forward(p, zero)
    own_copies = []
    for p in range(4):
        own, out, color, cols = pieces[p]
        copy = pltpu.make_async_copy(
            own.at[:, cols], out.at[slot(zero), :, cols], own_sem.at[p]
        )
        copy.start()
        own_copies.append(copy)

    def arrival(p, r):
        order = orders[pieces[p][2]]
        axis = [a for a in order if r[a]][-1]
        back = moved(r, axis, 0)
        return transfer(p, back, axis, r[axis])

    offsets = [
        (dz, dy, dx, dc) for dz in range(4) for dy in range(2) for dx in range(2) for dc in range(2)
    ]
    cost = {0: 0, 1: 2, 2: 4, 3: 2}

    def when(r):
        return cost[r[0]] + r[1] * 2 + r[2] * 2 + r[3]

    for r in sorted(offsets[1:], key=when):
        for p in range(4):
            copy = arrival(p, r)
            copy.wait_recv()
            forward(p, r)
    for copy in started:
        copy.wait_send()
    for copy in own_copies:
        copy.wait()


def gather_all(in_copy, out_copy, small):
    hbm = pl.BlockSpec(memory_space=pl.ANY)
    return pl.pallas_call(
        gather_kernel,
        out_shape=(
            jax.ShapeDtypeStruct((32,) + in_copy.shape, in_copy.dtype),
            jax.ShapeDtypeStruct((32,) + out_copy.shape, out_copy.dtype),
            jax.ShapeDtypeStruct((32,) + small.shape, small.dtype),
        ),
        in_specs=[hbm] * 3,
        out_specs=(hbm,) * 3,
        scratch_shapes=[
            pltpu.SemaphoreType.DMA((4, 32)),
            pltpu.SemaphoreType.DMA((4, 32)),
            pltpu.SemaphoreType.DMA((4,)),
        ],
        compiler_params=pltpu.CompilerParams(collective_id=0, has_side_effects=True),
        name="gather_all",
    )(in_copy, out_copy, small)


def add_low(left, right):
    return (left.astype(jnp.float32) + right.astype(jnp.float32)).astype(left.dtype)


def reduce_kernel(
    gi, go, gs, fi, fo, fs, fq,
    ai, ao, a_s, b1, b2i, b2o, b2s, b3,
    ri, ro, rs, r1, r2i, r2o, r2s, r3,
    t1, t2i, t2o, t2s, u1, u2i, u2o, u2s,
    squares_narrow, squares_wide, send_sem, recv_sem, norm_send, norm_recv,
):
    at = place()
    z, y, x, c = at
    w = z * 2 + y
    n = x * 2 + c
    partners = [(w, lax.rem(n + s, 4)) for s in (1, 2, 3)]
    partners += [(lax.rem(w + s, 8), n) for s in range(1, 8)]
    barrier = pltpu.get_barrier_semaphore()
    for partner in partners:
        pl.semaphore_signal(barrier, inc=1, device_id=partner, device_id_type=MESH_ID)
    pl.semaphore_wait(barrier, len(partners))

    count = [0]

    def send(src, dst, axis, step=1):
        index = count[0]
        count[0] += 1
        copy = pltpu.make_async_remote_copy(
            src_ref=src,
            dst_ref=dst,
            send_sem=send_sem.at[index],
            recv_sem=recv_sem.at[index],
            device_id=device(*neighbour(at, axis, step)),
            device_id_type=MESH_ID,
        )
        copy.start()
        return copy

    first = [
        send(gi.at[:, :, :, 1 - c], ri, 3),
        send(go.at[:, :, :, 1 - c], ro, 3),
        send(gs.at[:, :, :, 1 - c], rs, 3),
    ]
    for copy in first:
        copy.wait_recv()

    def add_first(k, carry):
        zi, yi, xi = k // 4, lax.rem(k // 2, 2), lax.rem(k, 2)
        ai[zi, yi, xi] = add_low(gi[zi, yi, xi, c], ri[zi, yi, xi])
        ao[zi, yi, xi] = add_low(go[zi, yi, xi, c], ro[zi, yi, xi])
        a_s[zi, yi, xi] = add_low(gs[zi, yi, xi, c], rs[zi, yi, xi])
        return carry

    lax.fori_loop(0, 16, add_first, 0)
    width = gi.shape[-1]
    left, right = pl.ds(0, SPLIT), pl.ds(SPLIT, width - SPLIT)
    second = [
        send(ai.at[:, :, 1 - x, :, left], r1, 2),
        send(ai.at[:, 1 - y, :, :, right], r2i, 1),
        send(ao.at[:, 1 - y], r2o, 1),
        send(a_s.at[:, 1 - y], r2s, 1),
    ]
    for copy in second:
        copy.wait_recv()

    def add_second(k, carry):
        zi, j = k // 2, lax.rem(k, 2)
        b1[zi, j] = add_low(ai[zi, j, x, :, left], r1[zi, j])
        b2i[zi, j] = add_low(ai[zi, y, j, :, right], r2i[zi, j])
        b2o[zi, j] = add_low(ao[zi, y, j], r2o[zi, j])
        b2s[zi, j] = add_low(a_s[zi, y, j], r2s[zi, j])
        return carry

    lax.fori_loop(0, 8, add_second, 0)
    third = [
        send(b1.at[:, 1 - y], r3, 1),
        send(b2i.at[:, 1 - x], t2i, 2),
        send(b2o.at[:, 1 - x], t2o, 2),
        send(b2s.at[:, 1 - x], t2s, 2),
    ]
    for copy in third:
        copy.wait_recv()

    def add_third(k, carry):
        b3[k] = add_low(b1[k, y], r3[k])
        r2i[k, 0] = add_low(b2i[k, x], t2i[k])
        r2o[k, 0] = add_low(b2o[k, x], t2o[k])
        r2s[k, 0] = add_low(b2s[k, x], t2s[k])
        return carry

    lax.fori_loop(0, 4, add_third, 0)
    fourth = []
    for step in (1, 2, 3):
        to = lax.rem(z + step, 4)
        fourth += [
            send(b3.at[to], u1.at[step - 1], 0, step),
            send(r2i.at[to, 0], u2i.at[step - 1], 0, step),
            send(r2o.at[to, 0], u2o.at[step - 1], 0, step),
            send(r2s.at[to, 0], u2s.at[step - 1], 0, step),
        ]
    for copy in fourth:
        copy.wait_recv()

    def total(own, others):
        value = own.astype(jnp.float32)
        for k in range(3):
            value = value + others[k].astype(jnp.float32)
        return value

    squares = jnp.zeros((8, 128), jnp.float32)

    def tile_squares(value, squares):
        rows, cols = value.shape
        for i in range(rows // 8):
            for j in range(cols // 128):
                part = value[i * 8 : i * 8 + 8, j * 128 : j * 128 + 128]
                squares = squares + part * part
        return squares

    for own, others, out, cols in (
        (b3[z], u1, fi, left),
        (r2i[z, 0], u2i, fi, right),
        (r2o[z, 0], u2o, fo, pl.ds(0, fo.shape[1])),
        (r2s[z, 0], u2s, fs, pl.ds(0, 128)),
    ):
        value = total(own, others)
        out[:, cols] = value
        squares = tile_squares(value, squares)

    def exchange(buffer, mine, size, axis, base):
        copies = []
        for step in range(1, size):
            to = lax.rem(mine + step, size)
            copy = pltpu.make_async_remote_copy(
                src_ref=buffer.at[mine],
                dst_ref=buffer.at[mine],
                send_sem=norm_send.at[base + step],
                recv_sem=norm_recv.at[base + step],
                device_id=(to, n) if axis == 0 else (w, to),
                device_id_type=MESH_ID,
            )
            copy.start()
            copies.append(copy)
        for copy in copies:
            copy.wait()
        value = buffer[0]
        for k in range(1, size):
            value = value + buffer[k]
        return value

    squares_narrow[n] = squares
    squares = exchange(squares_narrow, n, 4, 1, 0)
    squares_wide[w] = squares
    fq[...] = exchange(squares_wide, w, 8, 0, 4)
    for copy in first + second + third + fourth:
        copy.wait_send()


def reduce_all(grad_in, grad_out, small):
    low = jnp.bfloat16
    rows_in, width = grad_in.shape[0] // 32, grad_in.shape[1]
    rows_out, cols_out = grad_out.shape[0] // 32, grad_out.shape[1]
    gi = grad_in.reshape(4, 2, 2, 2, rows_in, width)
    go = grad_out.reshape(4, 2, 2, 2, rows_out, cols_out)
    gs = small.reshape(4, 2, 2, 2, SMALL_ROWS, 128)
    rest = width - SPLIT
    vmem = pl.BlockSpec(memory_space=pltpu.VMEM)

    def trio(lead, cols, own=True):
        kinds = [
            pltpu.VMEM(lead + (rows_in, cols), low),
            pltpu.VMEM(lead + (rows_out, cols_out), low),
            pltpu.VMEM(lead + (SMALL_ROWS, 128), jnp.float32),
        ]
        return kinds

    scratch = trio((4, 2, 2), width)
    scratch += [pltpu.VMEM((4, 2, rows_in, SPLIT), low)] + trio((4, 2), rest)
    scratch += [pltpu.VMEM((4, rows_in, SPLIT), low)]
    scratch += trio((4, 2, 2), width)
    scratch += [pltpu.VMEM((4, 2, rows_in, SPLIT), low)] + trio((4, 2), rest)
    scratch += [pltpu.VMEM((4, rows_in, SPLIT), low)]
    scratch += [pltpu.VMEM((1, 8, 128), low)] + trio((4,), rest)
    scratch += [pltpu.VMEM((3, rows_in, SPLIT), low)] + trio((3,), rest)
    scratch += [
        pltpu.VMEM((4, 8, 128), jnp.float32),
        pltpu.VMEM((8, 8, 128), jnp.float32),
        pltpu.SemaphoreType.DMA((23,)),
        pltpu.SemaphoreType.DMA((23,)),
        pltpu.SemaphoreType.DMA((12,)),
        pltpu.SemaphoreType.DMA((12,)),
    ]
    return pl.pallas_call(
        reduce_kernel,
        out_shape=(
            jax.ShapeDtypeStruct((rows_in, width), jnp.float32),
            jax.ShapeDtypeStruct((rows_out, cols_out), jnp.float32),
            jax.ShapeDtypeStruct((SMALL_ROWS, 128), jnp.float32),
            jax.ShapeDtypeStruct((8, 128), jnp.float32),
        ),
        in_specs=[vmem] * 3,
        out_specs=(vmem,) * 4,
        scratch_shapes=scratch,
        compiler_params=pltpu.CompilerParams(
            collective_id=1, has_side_effects=True, vmem_limit_bytes=48 << 20
        ),
        name="reduce_all",
    )(gi, go, gs)


def cross_rows(left, right):
    return lax.dot_general(
        left, right, (((0,), (0,)), ((), ())), preferred_element_type=jnp.float32
    )


SIDE = 8
TALL = 512
CHUNK = 10
GAIN_ROW = 58
BIAS_ROW = 60


def tokens_of(value):
    return value.reshape(-1, SIDE, value.shape[-1])


def column_partial(value):
    return jnp.sum(tokens_of(value), axis=0)


def dot(left, right):
    return jnp.dot(left, right, preferred_element_type=jnp.float32)


def dot_nt(left, right):
    return lax.dot_general(
        left, right, (((1,), (1,)), ((), ())), preferred_element_type=jnp.float32
    )


def dot_tn(left, right):
    return lax.dot_general(
        left, right, (((0,), (0,)), ((), ())), preferred_element_type=jnp.float32
    )


def lane_tile(j):
    if isinstance(j, int):
        return pl.ds(j * 128, 128)
    return pl.ds(pl.multiple_of(j * 128, 128), 128)


def grid_rows(row, col):
    return pl.ds((1 + row * GRID + col) * SIDE, SIDE)


CLASS_ROWS = pl.ds(0, SIDE)


def put(grid, at, value):
    for j in range(D // 128):
        grid[j, at, :] = value[:, j * 128 : j * 128 + 128]


def get(grid, at, tiles=(0, 1, 2, 3)):
    return jnp.concatenate([grid[j, at, :] for j in tiles], axis=1)


def conv_tile(src, taps, base, width, reach, j, finish, flip=False):
    lanes = lane_tile(j)
    margin = width // 2
    offsets = range(-reach, reach + 1)

    def tap(dy, dx):
        if flip:
            dy, dx = -dy, -dx
        index = base + (dy + margin) * width + dx + margin
        return jnp.broadcast_to(taps[index : index + 1, lanes], (SIDE, 128))

    held = {(dy, dx): tap(dy, dx) for dy in offsets for dx in offsets}
    for row in range(GRID):
        sums = [jnp.zeros((SIDE, 128), jnp.float32) for _ in range(GRID)]
        for dy in offsets:
            if not 0 <= row + dy < GRID:
                continue
            line = [src[j, grid_rows(row + dy, col), :] for col in range(GRID)]
            for dx in offsets:
                for col in range(GRID):
                    if 0 <= col + dx < GRID:
                        sums[col] = sums[col] + line[col + dx] * held[dy, dx]
        for col in range(GRID):
            finish(grid_rows(row, col), sums[col])


def tap_sums(grad, src, base, width, reach, j, total):
    lanes = lane_tile(j)
    margin = width // 2
    offsets = range(-reach, reach + 1)
    for dy in offsets:
        sums = {dx: jnp.zeros((SIDE, 128), jnp.float32) for dx in offsets}
        for row in range(GRID):
            if not 0 <= row + dy < GRID:
                continue
            up = [grad[j, grid_rows(row, col), :] for col in range(GRID)]
            line = [src[j, grid_rows(row + dy, col), :] for col in range(GRID)]
            for dx in offsets:
                for col in range(GRID):
                    if 0 <= col + dx < GRID:
                        sums[dx] = sums[dx] + up[col] * line[col + dx]
        for dx in offsets:
            index = base + (dy + margin) * width + dx + margin
            total[index, :, lanes] = total[index, :, lanes] + sums[dx]


def mask_far_taps(rows):
    lanes = pl.ds(256, 128)
    keep = (lax.broadcasted_iota(jnp.int32, (1, 128), 1) >= 64).astype(jnp.float32)
    for tap in range(49):
        if max(abs(tap // 7 - 3), abs(tap % 7 - 3)) == 3:
            line = pl.ds(9 + tap, 1)
            rows[line, lanes] = rows[line, lanes] * keep


def relative_tiles(body):
    body(0, 1)
    body(1, 2)

    def rest(j, carry):
        body(j, 3)
        return carry

    lax.fori_loop(2, 4, rest, 0)


def all_tiles(body):
    def step(j, carry):
        body(j)
        return carry

    lax.fori_loop(0, 4, step, 0)


def all_chunks(body):
    def step(k, carry):
        body(pl.ds(pl.multiple_of(k * CHUNK * SIDE, 16), CHUNK * SIDE))
        return carry

    lax.fori_loop(0, 50 // CHUNK, step, 0)


def normalise(values):
    centred = values - jnp.mean(values, axis=-1, keepdims=True)
    scale = lax.rsqrt(jnp.mean(centred * centred, axis=-1, keepdims=True) + NORM_EPS)
    return centred * scale, scale


def norm_back(grad, hat, scale, gain):
    inner = grad * gain
    mean = jnp.mean(inner, axis=-1, keepdims=True)
    along = jnp.mean(inner * hat, axis=-1, keepdims=True)
    return scale * (inner - mean - hat * along)


def spread_images(src, grid, first, limit):
    for i in range(SIDE):
        image = src[i]
        keep = jnp.full(image.shape, first + i, jnp.int32) < limit
        at = pl.ds(i, image.shape[0], stride=SIDE)
        put(grid, at, jnp.where(keep, image.astype(jnp.float32), 0.0))


def set_parameters(small, par, heads):
    par[...] = small[...].astype(jnp.float32).T
    mask_far_taps(par)
    row_head = lax.broadcasted_iota(jnp.int32, heads.shape, 0) // 64
    col_head = lax.broadcasted_iota(jnp.int32, heads.shape, 1) // 64
    heads[...] = jnp.where(row_head == col_head, 1.0, 0.0).astype(heads.dtype)


def every_image(body):
    for i in range(SIDE):
        for half in range(2):
            body(pl.ds(i, TALL // SIDE, stride=SIDE), (2 * half, 2 * half + 1))


def forward_kernel(
    num_images, rows, counts, x_in, dy_in, w_in, w_out, small,
    out, act_o, gh_o, n1_o, n2_o, at_o, gf_o, gp_o, gx_o, xt_o, hat_o, sc_o, q_o, k_o, v_o, cv_o,
    cols_o, hcols_o,
    par, heads, x, x1, v, q, k, conv, hat2, slope, gn, scale2,
):
    low = jnp.bfloat16
    step = pl.program_id(0)
    first = step * SIDE
    live = pl.ds(0, rows)

    @pl.when(step == 0)
    def _():
        set_parameters(small, par, heads)
        for grid in (q, k, v):
            grid[...] = jnp.zeros_like(grid)
        cols_o[...] = jnp.zeros_like(cols_o)
        hcols_o[...] = jnp.zeros_like(hcols_o)

    def bias(row):
        return par[BIAS_ROW + row : BIAS_ROW + row + 1, :]

    def gain(row):
        return par[GAIN_ROW + row : GAIN_ROW + row + 1, :]

    spread_images(x_in, x, first, num_images)
    xt_o[...] = get(x, live).astype(low)
    spread_images(dy_in, gn, first, jnp.minimum(counts[0], num_images))
    gf_o[...] = get(gn, live).astype(low)

    def position(j):
        lanes = lane_tile(j)
        shift = jnp.broadcast_to(par[BIAS_ROW + 10 : BIAS_ROW + 11, lanes], (SIDE, 128))

        def finish(at, total):
            x1[j, at, :] = x[j, at, :] + total + shift

        conv_tile(x, par, 0, 3, 1, j, finish)
        x1[j, CLASS_ROWS, :] = x[j, CLASS_ROWS, :]

    all_tiles(position)

    def first_norm(at):
        hat, scale = normalise(get(x1, at))
        hat_o[at, :] = hat.astype(low)
        sc_o[at, :] = jnp.broadcast_to(scale, (CHUNK * SIDE, 128))
        n1_o[at, :] = (hat * gain(0) + bias(0)).astype(low)

    all_chunks(first_norm)
    n1 = n1_o[...]
    put(gn, live, dot(n1, w_in[:, D : 2 * D]))

    def weights(j):
        lanes = lane_tile(j)
        keys = tokens_of(gn[j, live, :])
        powers = jnp.exp(keys - jnp.max(keys, axis=0, keepdims=True))
        share = 0.125 / jnp.sum(powers, axis=0, keepdims=True)
        value = (powers * share).reshape(-1, 128)
        k[j, live, :] = value
        k_o[:, lanes] = value.astype(low)

    all_tiles(weights)
    value = dot(n1, w_in[:, 2 * D : 3 * D]) + bias(3)
    put(v, live, value)
    v_o[...] = value.astype(low)

    def relative(j, reach):
        lanes = lane_tile(j)
        shift = jnp.broadcast_to(par[BIAS_ROW + 11 : BIAS_ROW + 12, lanes], (SIDE, 128))

        def finish(at, total):
            conv[j, at, :] = total + shift

        conv_tile(v, par, 9, 7, reach, j, finish)
        conv[j, CLASS_ROWS, :] = jnp.zeros((SIDE, 128), jnp.float32)

    relative_tiles(relative)
    cv_o[...] = get(conv, live).astype(low)
    value = dot(n1, w_in[:, :D]) + bias(2)
    q_o[...] = value.astype(low)
    put(q, live, value)

    def attention(at, tiles):
        context = dot_tn(get(k, at, tiles).astype(low), get(v, at, tiles).astype(low))
        context = context.astype(low) * heads[...]
        value = dot(get(q, at, tiles).astype(low), context)
        for n, j in enumerate(tiles):
            gn[j, at, :] = value[:, n * 128 : n * 128 + 128]

    every_image(attention)
    for j in range(D // 128):
        at_o[:, lane_tile(j)] = (gn[j, live, :] + conv[j, live, :] * q[j, live, :]).astype(low)
    put(x1, live, get(x1, live) + (dot(at_o[...], w_in[:, 3 * D : 4 * D]) + bias(4)))

    def second_norm(at):
        hat, scale = normalise(get(x1, at))
        hat2[at, :] = hat
        scale2[at, :] = jnp.broadcast_to(scale, (CHUNK * SIDE, 128))
        n2_o[at, :] = (hat * gain(1) + bias(1)).astype(low)

    all_chunks(second_norm)
    n2 = n2_o[...]
    for part in range(MLP_WIDTH // D):
        cols = pl.ds(part * D, D)
        put(gn, live, dot(n2, w_in[:, pl.ds((4 + part) * D, D)]))

        def gelu(at):
            h = get(gn, at) + bias(5 + part)
            below = 0.5 + 0.5 * lax.erf(h * (0.5**0.5))
            density = jnp.exp(-0.5 * h * h) * 0.3989422804014327
            act_o[at, cols] = (h * below).astype(low)
            slope[at, cols] = below + h * density

        all_chunks(gelu)
    put(x1, live, get(x1, live) + dot(act_o[...], w_out[...]) + bias(9))
    for i in range(SIDE):
        out[i] = get(x1, pl.ds(i, out.shape[1], stride=SIDE)).astype(low)

    gf = gf_o[...]
    for part in range(MLP_WIDTH // D):
        cols = pl.ds(part * D, D)
        grad = (dot_nt(gf, w_out[cols, :]) * slope[:, cols]).astype(low)
        gh_o[:, cols] = grad
        hcols_o[:, cols] = hcols_o[:, cols] + column_partial(grad.astype(jnp.float32))
    put(gn, live, dot_nt(gh_o[...], w_in[:, 4 * D :]))

    def second_back(at):
        grad = get(gn, at)
        hat = hat2[at, :]
        scale = scale2[at, 0:1]
        upstream = gf_o[at, :].astype(jnp.float32)
        total = upstream + norm_back(grad, hat, scale, gain(1))
        gx_o[at, :] = total
        rounded = total.astype(low)
        gp_o[at, :] = rounded
        cols_o[0] = cols_o[0] + column_partial(grad)
        cols_o[1] = cols_o[1] + column_partial(grad * hat)
        cols_o[2] = cols_o[2] + column_partial(rounded.astype(jnp.float32))
        cols_o[3] = cols_o[3] + column_partial(upstream)

    all_chunks(second_back)


def backward_kernel(
    rows, w_in, small, cols_in, hcols_in, gx, hat, sc, q_in, k_in, v_in, cv, xt,
    out, gq_o, small_o,
    par, heads, cols, taps, lines, g, gc, q, k, v, gq, gk, gv, x, g1,
):
    low = jnp.bfloat16
    step = pl.program_id(0)
    live = pl.ds(0, rows)

    @pl.when(step == 0)
    def _():
        set_parameters(small, par, heads)
        for grid in (g, q, k, v, gq, gk, gv):
            grid[...] = jnp.zeros_like(grid)
        cols[...] = jnp.zeros_like(cols)
        taps[...] = jnp.zeros_like(taps)

    grad = dot_nt(gx[...].astype(low), w_in[:, 3 * D : 4 * D])
    put(g, live, grad)
    for j in range(D // 128):
        lanes = lane_tile(j)
        part = g[j, live, :]
        queries = q_in[:, lanes].astype(jnp.float32)
        q[j, live, :] = queries
        k[j, live, :] = k_in[:, lanes].astype(jnp.float32)
        v[j, live, :] = v_in[:, lanes].astype(jnp.float32)
        x[j, live, :] = xt[:, lanes].astype(jnp.float32)
        gq[j, live, :] = part * cv[:, lanes].astype(jnp.float32)
        gc[j, live, :] = part * queries
        gc[j, CLASS_ROWS, :] = jnp.zeros((SIDE, 128), jnp.float32)
        cols[0, :, lanes] = cols[0, :, lanes] + column_partial(gc[j, live, :])

    def relative(j, reach):
        def finish(at, total):
            gv[j, at, :] = total

        conv_tile(gc, par, 9, 7, reach, j, finish, flip=True)
        gv[j, CLASS_ROWS, :] = jnp.zeros((SIDE, 128), jnp.float32)
        tap_sums(gc, v, 9, 7, reach, j, taps)

    relative_tiles(relative)

    def attention(at, tiles):
        qs, ks, vs, gs = (get(grid, at, tiles).astype(low) for grid in (q, k, v, g))
        context = dot_tn(ks, vs).astype(low) * heads[...]
        grads = dot_tn(qs, gs).astype(low) * heads[...]
        to_q, to_k, to_v = dot_nt(gs, context), dot_nt(vs, grads), dot(ks, grads)
        for n, j in enumerate(tiles):
            here = slice(n * 128, n * 128 + 128)
            gq[j, at, :] = gq[j, at, :] + to_q[:, here]
            gk[j, at, :] = to_k[:, here]
            gv[j, at, :] = gv[j, at, :] + to_v[:, here]

    every_image(attention)

    def finish_qkv(j):
        lanes = lane_tile(j)
        share = tokens_of(k[j, live, :])
        up = tokens_of(gk[j, live, :])
        along = jnp.sum(share * up, axis=0, keepdims=True) * 8.0
        gq_o[:, pl.ds(pl.multiple_of(D + j * 128, 128), 128)] = (
            (share * (up - along)).reshape(-1, 128).astype(low)
        )
        part = gq[j, live, :].astype(low)
        gq_o[:, lanes] = part
        cols[1, :, lanes] = cols[1, :, lanes] + column_partial(part.astype(jnp.float32))
        part = gv[j, live, :].astype(low)
        gq_o[:, pl.ds(pl.multiple_of(2 * D + j * 128, 128), 128)] = part
        cols[2, :, lanes] = cols[2, :, lanes] + column_partial(part.astype(jnp.float32))

    all_tiles(finish_qkv)
    put(gk, live, dot_nt(gq_o[...], w_in[:, : 3 * D]))

    def first_back(at):
        grad = get(gk, at)
        hats = hat[at, :].astype(jnp.float32)
        total = gx[at, :] + norm_back(grad, hats, sc[at, 0:1], par[GAIN_ROW : GAIN_ROW + 1, :])
        put(g1, at, total)
        cols[3] = cols[3] + column_partial(grad)
        cols[4] = cols[4] + column_partial(grad * hats)
        cols[5] = cols[5] + column_partial(total)

    all_chunks(first_back)
    cols[5] = cols[5] - get(g1, CLASS_ROWS)

    def position(j):
        def finish(at, total):
            gv[j, at, :] = g1[j, at, :] + total

        conv_tile(g1, par, 0, 3, 1, j, finish, flip=True)
        gv[j, CLASS_ROWS, :] = g1[j, CLASS_ROWS, :]
        tap_sums(g1, x, 0, 3, 1, j, taps)

    all_tiles(position)
    for i in range(SIDE):
        out[i] = get(gv, pl.ds(i, out.shape[1], stride=SIDE))

    @pl.when(step == pl.num_programs(0) - 1)
    def _():
        lines[...] = jnp.zeros_like(lines)
        for tap in range(taps.shape[0]):
            lines[tap : tap + 1, :] = jnp.sum(taps[tap], axis=0, keepdims=True)
        mask_far_taps(lines)
        hidden = [hcols_in[:, i * D : i * D + D] for i in range(MLP_WIDTH // D)]
        order = [cols[4], cols_in[1], cols[3], cols_in[0], cols[1], cols[2], cols_in[2]]
        for i, part in enumerate(order + hidden + [cols_in[3], cols[5], cols[0]]):
            row = GAIN_ROW + i
            lines[row : row + 1, :] = jnp.sum(part, axis=0, keepdims=True)
        small_o[...] = lines[...].T


def fixed(shape):
    zeros = (0,) * len(shape)
    return pl.BlockSpec(shape, lambda g: zeros, pipeline_mode=pl.Buffered(1))


def compute(images, cotangent, counts, w_in, w_out, small):
    low, full = jnp.bfloat16, jnp.float32
    num_images, num_tokens, channels = images.shape
    groups = -(-num_images // SIDE)
    rows = num_tokens * SIDE
    total = groups * rows

    def block(cols):
        return pl.BlockSpec((rows, cols), lambda g: (g, 0))

    def image_block():
        return pl.BlockSpec((SIDE, num_tokens, channels), lambda g: (g, 0, 0))

    def made(cols, kind=low):
        return jax.ShapeDtypeStruct((total, cols), kind)

    def grid():
        return pltpu.VMEM((channels // 128, TALL, 128), full)

    shared = [pltpu.VMEM((128, channels), full), pltpu.VMEM((256, 256), low)]
    wide = w_out.shape[0]
    forward = pl.pallas_call(
        functools.partial(forward_kernel, num_images, rows),
        grid=(groups,),
        in_specs=[
            pl.BlockSpec(memory_space=pltpu.SMEM),
            image_block(),
            image_block(),
            fixed(w_in.shape),
            fixed(w_out.shape),
            fixed(small.shape),
        ],
        out_specs=[image_block(), block(wide), block(wide)]
        + [block(channels)] * 8
        + [block(128)]
        + [block(channels)] * 4
        + [fixed((4, SIDE, channels)), fixed((SIDE, wide))],
        out_shape=[jax.ShapeDtypeStruct(images.shape, low), made(wide), made(wide)]
        + [made(channels)] * 5
        + [made(channels, full), made(channels), made(channels), made(128, full)]
        + [made(channels)] * 4
        + [
            jax.ShapeDtypeStruct((4, SIDE, channels), full),
            jax.ShapeDtypeStruct((SIDE, wide), full),
        ],
        scratch_shapes=shared
        + [grid() for _ in range(6)]
        + [pltpu.VMEM((rows, channels), full), pltpu.VMEM((rows, wide), full), grid(), pltpu.VMEM((rows, 128), full)],
        compiler_params=pltpu.CompilerParams(vmem_limit_bytes=60 << 20),
        name="forward",
    )
    (
        out, act, gh, n1, n2, attended, gf, gp, gx, xt, hat, scale, q, k, v, cv, cols, hcols,
    ) = forward(counts, images, cotangent, w_in, w_out, small)

    backward = pl.pallas_call(
        functools.partial(backward_kernel, rows),
        grid=(groups,),
        in_specs=[
            pl.BlockSpec(
                (channels, 4 * channels), lambda g: (0, 0), pipeline_mode=pl.Buffered(1)
            ),
            fixed(small.shape),
            fixed(cols.shape),
            fixed(hcols.shape),
            block(channels),
            block(channels),
            block(128),
        ]
        + [block(channels)] * 5,
        out_specs=[image_block(), block(3 * channels), fixed(small.shape)],
        out_shape=[
            jax.ShapeDtypeStruct(images.shape, full),
            made(3 * channels),
            jax.ShapeDtypeStruct(small.shape, full),
        ],
        scratch_shapes=shared
        + [
            pltpu.VMEM((6, SIDE, channels), full),
            pltpu.VMEM((GAIN_ROW, SIDE, channels), full),
            pltpu.VMEM((128, channels), full),
        ]
        + [grid() for _ in range(10)],
        compiler_params=pltpu.CompilerParams(vmem_limit_bytes=60 << 20),
        name="backward",
    )
    input_grad, gq, grad_small = backward(
        w_in, small, cols, hcols, gx, hat, scale, q, k, v, cv, xt
    )
    grad_in = jnp.concatenate(
        [
            cross_rows(n1, gq).astype(low),
            cross_rows(attended, gp).astype(low),
            cross_rows(n2, gh).astype(low),
        ],
        axis=1,
    )
    grad_out = cross_rows(act, gf).astype(low)
    return out, input_grad, grad_in, grad_out, grad_small


def adamw_update(master, first_moment, second_moment, gradient, clip_factor, rate, decay):
    clipped = gradient * clip_factor
    first_new = BETA_ONE * first_moment + (1.0 - BETA_ONE) * clipped
    second_new = BETA_TWO * second_moment + (1.0 - BETA_TWO) * clipped * clipped
    first_hat = first_new / (1.0 - BETA_ONE**STEP)
    second_hat = second_new / (1.0 - BETA_TWO**STEP)
    master_new = master - rate * (first_hat / (jnp.sqrt(second_hat) + ADAM_EPS) + decay * master)
    return (master_new, first_new, second_new, master_new.astype(jnp.bfloat16))


def local(
    images,
    cotangent,
    counts,
    in_mats,
    in_mats_m,
    in_mats_v,
    out_mat,
    out_mat_m,
    out_mat_v,
    kernels,
    kernels_m,
    kernels_v,
    gains,
    gains_m,
    gains_v,
    biases,
    biases_m,
    biases_v,
    special,
):
    in_copy = in_mats.astype(jnp.bfloat16)
    out_copy = out_mat.astype(jnp.bfloat16)
    shards = (kernels, gains, biases)
    sizes = [shard.shape[0] for shard in shards]
    used = sum(sizes)
    count_row = jnp.broadcast_to(counts.astype(jnp.float32)[:, None], (1, kernels.shape[1]))
    rows = jnp.concatenate(shards + (count_row,), axis=0)
    small = jnp.pad(rows, ((0, 128 - used - 1), (0, 0))).T.astype(jnp.bfloat16)
    if special:
        all_in, all_out, all_small = gather_all(in_copy, out_copy, small)
    else:
        all_in, all_out, all_small = (
            lax.all_gather(part, ("wide", "narrow"), axis=0, tiled=True)
            for part in (in_copy, out_copy, small)
        )
    all_small = all_small.reshape(-1, small.shape[0], 128)
    live_total = jnp.sum(all_small[:, 0, used].astype(jnp.float32)) * images.shape[1]
    scale_factor = 1.0 / live_total
    block_out, input_grad, grad_in, grad_fc2, grad_small = compute(
        images,
        cotangent,
        counts,
        all_in.reshape(-1, in_copy.shape[1]),
        all_out.reshape(-1, out_copy.shape[1]),
        all_small.reshape(-1, 128),
    )
    if special:
        sum_in, sum_out, sum_small, squares = reduce_all(grad_in, grad_fc2, grad_small)
        total_squares = jnp.sum(squares)
    else:
        sum_in, sum_out, sum_small = (
            lax.psum_scatter(
                part.astype(jnp.float32), ("wide", "narrow"), scatter_dimension=0, tiled=True
            )
            for part in (grad_in, grad_fc2, grad_small)
        )
        total_squares = lax.psum(
            sum(jnp.sum(part * part) for part in (sum_in, sum_out, sum_small)),
            ("wide", "narrow"),
        )
    rows = sum_small.T
    summed = (
        sum_in,
        sum_out,
        rows[: sizes[0]],
        rows[sizes[0] : sizes[0] + sizes[1]],
        rows[sizes[0] + sizes[1] : used],
    )
    summed = tuple(part * scale_factor for part in summed)
    grad_norm = jnp.sqrt(total_squares) * scale_factor
    clip_factor = jnp.minimum(1.0, 1.0 / (grad_norm + 1e-06))
    in_new = adamw_update(
        in_mats, in_mats_m, in_mats_v, summed[0], clip_factor, RATES[0], DECAYS[0]
    )
    out_new = adamw_update(
        out_mat, out_mat_m, out_mat_v, summed[1], clip_factor, RATES[1], DECAYS[1]
    )
    kern_new = adamw_update(
        kernels, kernels_m, kernels_v, summed[2], clip_factor, RATES[2], DECAYS[2]
    )
    gain_new = adamw_update(gains, gains_m, gains_v, summed[3], clip_factor, RATES[3], DECAYS[3])
    bias_new = adamw_update(biases, biases_m, biases_v, summed[4], clip_factor, RATES[4], DECAYS[4])
    return (
        block_out,
        input_grad,
        grad_norm,
        in_new[0],
        in_new[1],
        in_new[2],
        in_new[3],
        out_new[0],
        out_new[1],
        out_new[2],
        out_new[3],
        kern_new[0],
        kern_new[1],
        kern_new[2],
        kern_new[3],
        gain_new[0],
        gain_new[1],
        gain_new[2],
        gain_new[3],
        bias_new[0],
        bias_new[1],
        bias_new[2],
        bias_new[3],
    )


def solution(mesh):
    placed = (
        P(("wide", "narrow"), None, None),
        P(("wide", "narrow"), None, None),
        P(("wide", "narrow")),
        P(("wide", "narrow"), None),
        P(("wide", "narrow"), None),
        P(("wide", "narrow"), None),
        P(("wide", "narrow"), None),
        P(("wide", "narrow"), None),
        P(("wide", "narrow"), None),
        P(None, ("wide", "narrow")),
        P(None, ("wide", "narrow")),
        P(None, ("wide", "narrow")),
        P(None, ("wide", "narrow")),
        P(None, ("wide", "narrow")),
        P(None, ("wide", "narrow")),
        P(None, ("wide", "narrow")),
        P(None, ("wide", "narrow")),
        P(None, ("wide", "narrow")),
    )
    special = dict(mesh.shape) == {"wide": 8, "narrow": 4}
    return jax.shard_map(
        functools.partial(local, special=special),
        mesh=mesh,
        in_specs=placed,
        out_specs=(
            P(("wide", "narrow"), None, None),
            P(("wide", "narrow"), None, None),
            P(),
            P(("wide", "narrow"), None),
            P(("wide", "narrow"), None),
            P(("wide", "narrow"), None),
            P(("wide", "narrow"), None),
            P(("wide", "narrow"), None),
            P(("wide", "narrow"), None),
            P(("wide", "narrow"), None),
            P(("wide", "narrow"), None),
            P(None, ("wide", "narrow")),
            P(None, ("wide", "narrow")),
            P(None, ("wide", "narrow")),
            P(None, ("wide", "narrow")),
            P(None, ("wide", "narrow")),
            P(None, ("wide", "narrow")),
            P(None, ("wide", "narrow")),
            P(None, ("wide", "narrow")),
            P(None, ("wide", "narrow")),
            P(None, ("wide", "narrow")),
            P(None, ("wide", "narrow")),
            P(None, ("wide", "narrow")),
        ),
        check_vma=False,
    )
```

```python
import functools

import jax
import jax.numpy as jnp
from jax import lax
from jax.experimental import pallas as pl
from jax.experimental.pallas import tpu as pltpu
from jax.sharding import PartitionSpec as P

D = 512
HEADS = 8
MLP_WIDTH = 2048
GRID = 7
STEP = 10
BROWS = 12


NORM_EPS = 1e-06
BETA_ONE = 0.9
BETA_TWO = 0.999
ADAM_EPS = 1e-08
HIGHEST = lax.Precision.HIGHEST
RATES = (0.04, 0.02, 0.1, 0.8, 0.25)
DECAYS = (0.05, 0.05, 0.05, 0.0, 0.0)


MESH_ID = pl.DeviceIdType.MESH
SPLIT = 3072
SMALL_ROWS = 16


def place():
    w = lax.axis_index("wide")
    n = lax.axis_index("narrow")
    return w // 2, w % 2, n // 2, n % 2


def device(z, y, x, c):
    return (z * 2 + y, x * 2 + c)


def neighbour(at, axis, step=1):
    z, y, x, c = at
    if axis == 0:
        return (lax.rem(z + step, 4), y, x, c)
    if axis == 1:
        return (z, 1 - y, x, c)
    if axis == 2:
        return (z, y, 1 - x, c)
    return (z, y, x, 1 - c)


def gather_kernel(wi, wo, sm, gi, go, gs, send_sem, recv_sem, own_sem):
    at = place()
    z, y, x, c = at
    partners = [device(*neighbour(at, 0, s)) for s in (1, 2, 3)]
    partners += [device(*neighbour(at, a)) for a in (1, 2, 3)]
    barrier = pltpu.get_barrier_semaphore()
    for partner in partners:
        pl.semaphore_signal(barrier, inc=1, device_id=partner, device_id_type=MESH_ID)
    pl.semaphore_wait(barrier, len(partners))

    width = wi.shape[1]
    pieces = (
        (wi, gi, 0, pl.ds(0, SPLIT)),
        (sm, gs, 0, pl.ds(0, 128)),
        (wi, gi, 1, pl.ds(SPLIT, width - SPLIT)),
        (wo, go, 1, pl.ds(0, wo.shape[1])),
    )
    orders = ((0, 1, 2, 3), (0, 2, 1, 3))

    def slot(r):
        zs = lax.rem(z - r[0] + 4, 4)
        ys = 1 - y if r[1] else y
        xs = 1 - x if r[2] else x
        cs = 1 - c if r[3] else c
        return ((zs * 2 + ys) * 2 + xs) * 2 + cs

    def flat(r):
        return ((r[0] * 2 + r[1]) * 2 + r[2]) * 2 + r[3]

    def moved(r, axis, step):
        r = list(r)
        r[axis] = step
        return tuple(r)

    def transfer(p, r, axis, step):
        own, out, color, cols = pieces[p]
        there = out.at[slot(r), :, cols]
        here = own.at[:, cols] if r == (0, 0, 0, 0) else there
        to = moved(r, axis, step)
        return pltpu.make_async_remote_copy(
            src_ref=here,
            dst_ref=there,
            send_sem=send_sem.at[p, flat(to)],
            recv_sem=recv_sem.at[p, flat(to)],
            device_id=device(*neighbour(at, axis, step)),
            device_id_type=MESH_ID,
        )

    def onward(p, r):
        order = orders[pieces[p][2]]
        last = max([i for i in range(4) if r[order[i]]], default=-1)
        for i in range(last + 1, 4):
            axis = order[i]
            for step in (1, 2, 3) if axis == 0 else (1,):
                yield axis, step

    started = []

    def forward(p, r):
        for axis, step in onward(p, r):
            copy = transfer(p, r, axis, step)
            copy.start()
            started.append(copy)

    zero = (0, 0, 0, 0)
    for p in range(4):
        forward(p, zero)
    own_copies = []
    for p in range(4):
        own, out, color, cols = pieces[p]
        copy = pltpu.make_async_copy(
            own.at[:, cols], out.at[slot(zero), :, cols], own_sem.at[p]
        )
        copy.start()
        own_copies.append(copy)

    def arrival(p, r):
        order = orders[pieces[p][2]]
        axis = [a for a in order if r[a]][-1]
        back = moved(r, axis, 0)
        return transfer(p, back, axis, r[axis])

    offsets = [
        (dz, dy, dx, dc) for dz in range(4) for dy in range(2) for dx in range(2) for dc in range(2)
    ]
    cost = {0: 0, 1: 2, 2: 4, 3: 2}

    def when(r):
        return cost[r[0]] + r[1] * 2 + r[2] * 2 + r[3]

    for r in sorted(offsets[1:], key=when):
        for p in range(4):
            copy = arrival(p, r)
            copy.wait_recv()
            forward(p, r)
    for copy in started:
        copy.wait_send()
    for copy in own_copies:
        copy.wait()


def gather_all(in_copy, out_copy, small):
    hbm = pl.BlockSpec(memory_space=pl.ANY)
    return pl.pallas_call(
        gather_kernel,
        out_shape=(
            jax.ShapeDtypeStruct((32,) + in_copy.shape, in_copy.dtype),
            jax.ShapeDtypeStruct((32,) + out_copy.shape, out_copy.dtype),
            jax.ShapeDtypeStruct((32,) + small.shape, small.dtype),
        ),
        in_specs=[hbm] * 3,
        out_specs=(hbm,) * 3,
        scratch_shapes=[
            pltpu.SemaphoreType.DMA((4, 32)),
            pltpu.SemaphoreType.DMA((4, 32)),
            pltpu.SemaphoreType.DMA((4,)),
        ],
        compiler_params=pltpu.CompilerParams(collective_id=0, has_side_effects=True),
        name="gather_all",
    )(in_copy, out_copy, small)


def add_low(left, right):
    return (left.astype(jnp.float32) + right.astype(jnp.float32)).astype(left.dtype)


IN_CHUNKS = 4
OUT_CHUNKS = 2
LAGS = (1, 3, 5, 7)


def reduce_kernel(
    n1_h, gq_h, at_h, gp_h, n2_h, gh_h, act_h, gf_h, gs, fi, fo, fs, fq,
    n1, gq, at_v, gp, n2, gh, act, gf,
    gi, go, r0i, r0o, r0s, r1i, r1o, r1s, r2i, r2o, r2s, r3i, r3o, r3s,
    squares_narrow, squares_wide, load_sem, send_sem, recv_sem, norm_send, norm_recv,
):
    at = place()
    z, y, x, c = at
    w = z * 2 + y
    n = x * 2 + c
    loads = []
    half = gh.shape[1] // 2
    for src, dst, cols in (
        (n2_h, n2, None),
        (gh_h, gh, pl.ds(0, half)),
        (gh_h, gh, pl.ds(half, half)),
        (gf_h, gf, None),
        (act_h, act, None),
        (n1_h, n1, None),
        (gq_h, gq, None),
        (at_h, at_v, None),
        (gp_h, gp, None),
    ):
        real, padded = src.shape[0], dst.shape[0]
        if cols is None:
            cols = pl.ds(0, src.shape[1])
        if padded > real:
            dst[pl.ds(real, padded - real), cols] = jnp.zeros(
                (padded - real, cols.size), dst.dtype
            )
        src, dst = src.at[:, cols], dst.at[pl.ds(0, real), cols]
        copy = pltpu.make_async_copy(src, dst, load_sem.at[len(loads)])
        copy.start()
        loads.append(copy)
    waited = [0]

    def loaded(upto):
        while waited[0] < upto:
            loads[waited[0]].wait()
            waited[0] += 1

    partners = [(w, lax.rem(n + s, 4)) for s in (1, 2, 3)]
    partners += [(lax.rem(w + s, 8), n) for s in range(1, 8)]
    barrier = pltpu.get_barrier_semaphore()
    for partner in partners:
        pl.semaphore_signal(barrier, inc=1, device_id=partner, device_id_type=MESH_ID)

    count = [0]
    sent = []

    def send(src, dst, axis, step=1):
        index = count[0]
        count[0] += 1
        copy = pltpu.make_async_remote_copy(
            src_ref=src,
            dst_ref=dst,
            send_sem=send_sem.at[index],
            recv_sem=recv_sem.at[index],
            device_id=device(*neighbour(at, axis, step)),
            device_id_type=MESH_ID,
        )
        copy.start()
        sent.append(copy)
        return copy

    def product(left, right, cols):
        value = dot_tn(left[...], right[:, cols]).astype(gi.dtype)
        return value.reshape(4, 2, 2, 2, -1, value.shape[1])

    def make_in(chunk):
        width = gi.shape[-1]
        if chunk >= 2:
            loaded(chunk)
            gi[chunk] = product(n2, gh, pl.ds((chunk - 2) * width, width))
        elif chunk == 1:
            loaded(9)
            gi[1, :, :, :, :, :, pl.ds(0, D)] = product(n1, gq, pl.ds(width, D))
            gi[1, :, :, :, :, :, pl.ds(D, D)] = product(at_v, gp, pl.ds(0, D))
        else:
            loaded(7)
            gi[0] = product(n1, gq, pl.ds(0, width))

    def make_out(chunk):
        if chunk:
            return
        loaded(5)
        width = go.shape[-1]

        def block(m, carry):
            left = act[:, pl.ds(pl.multiple_of(m * D, D), D)]
            value = dot_tn(left, gf[...]).astype(go.dtype)
            for k in range(OUT_CHUNKS):
                part = value[:, k * width : k * width + width]
                go[k, m] = part.reshape(2, 2, 2, -1, width)
            return carry

        lax.fori_loop(0, 4, block, 0)

    def entry(make, chunk, color, g, r0, r1, r2, r3, out, cols):
        return dict(
            make=make, chunk=chunk, color=color, g=g, r0=r0, r1=r1, r2=r2, r3=r3, out=out, cols=cols
        )

    entries = [entry(None, 0, 1, gs, r0s, r1s, r2s, r3s, fs, pl.ds(0, 128))]

    def in_entry(chunk, color):
        refs = [ref.at[chunk] for ref in (gi, r0i, r1i, r2i, r3i)]
        width = gi.shape[-1]
        return entry(make_in, chunk, color, *refs, fi, pl.ds(chunk * width, width))

    def out_entry(chunk, color):
        refs = [ref.at[chunk] for ref in (go, r0o, r1o, r2o, r3o)]
        width = go.shape[-1]
        return entry(make_out, chunk, color, *refs, fo, pl.ds(chunk * width, width))

    entries += [in_entry(2, 0), in_entry(3, 1), out_entry(0, 0), out_entry(1, 1)]
    entries += [in_entry(0, 0), in_entry(1, 1)]

    def begin(e):
        e["copy"] = send(e["g"].at[:, :, :, 1 - c], e["r0"], 3)

    def across(e):
        e["copy"].wait_recv()
        g, r0 = e["g"], e["r0"]

        def add(k, carry):
            zi, yi, xi = k // 4, lax.rem(k // 2, 2), lax.rem(k, 2)
            r0[zi, yi, xi] = add_low(g[zi, yi, xi, c], r0[zi, yi, xi])
            return carry

        lax.fori_loop(0, 16, add, 0)
        if e["color"] == 0:
            e["copy"] = send(r0.at[:, :, 1 - x], e["r1"], 2)
        else:
            e["copy"] = send(r0.at[:, 1 - y], e["r1"], 1)

    def onward(e):
        e["copy"].wait_recv()
        r0, r1, color = e["r0"], e["r1"], e["color"]

        def add(k, carry):
            zi, j = k // 2, lax.rem(k, 2)
            own = r0[zi, j, x] if color == 0 else r0[zi, y, j]
            r1[zi, j] = add_low(own, r1[zi, j])
            return carry

        lax.fori_loop(0, 8, add, 0)
        if color == 0:
            e["copy"] = send(r1.at[:, 1 - y], e["r2"], 1)
        else:
            e["copy"] = send(r1.at[:, 1 - x], e["r2"], 2)

    def along(e):
        e["copy"].wait_recv()
        r1, r2, keep = e["r1"], e["r2"], y if e["color"] == 0 else x

        def add(k, carry):
            r2[k] = add_low(r1[k, keep], r2[k])
            return carry

        lax.fori_loop(0, 4, add, 0)
        e["copies"] = [
            send(r2.at[lax.rem(z + step, 4)], e["r3"].at[step - 1], 0, step) for step in (1, 2, 3)
        ]

    squares = [jnp.zeros((8, 128), jnp.float32)]

    def finish(e):
        for copy in e["copies"]:
            copy.wait_recv()
        value = e["r2"][z].astype(jnp.float32)
        for k in range(3):
            value = value + e["r3"][k].astype(jnp.float32)
        e["out"][:, e["cols"]] = value
        rows, cols = value.shape
        total = jnp.sum((value * value).reshape(rows // 8, 8, cols), axis=0)
        for j in range(cols // 128):
            squares[0] = squares[0] + total[:, j * 128 : j * 128 + 128]

    for t in range(len(entries) + LAGS[-1]):
        for action, lag in zip((finish, along, onward, across), LAGS[::-1]):
            if 0 <= t - lag < len(entries):
                action(entries[t - lag])
        if t < len(entries):
            e = entries[t]
            if e["make"] is not None:
                e["make"](e["chunk"])
            if t == 0:
                pl.semaphore_wait(barrier, len(partners))
            begin(e)

    def exchange(buffer, mine, size, axis, base):
        copies = []
        for step in range(1, size):
            to = lax.rem(mine + step, size)
            copy = pltpu.make_async_remote_copy(
                src_ref=buffer.at[mine],
                dst_ref=buffer.at[mine],
                send_sem=norm_send.at[base + step],
                recv_sem=norm_recv.at[base + step],
                device_id=(to, n) if axis == 0 else (w, to),
                device_id_type=MESH_ID,
            )
            copy.start()
            copies.append(copy)
        for copy in copies:
            copy.wait()
        value = buffer[0]
        for k in range(1, size):
            value = value + buffer[k]
        return value

    squares_narrow[n] = squares[0]
    squares_wide[w] = exchange(squares_narrow, n, 4, 1, 0)
    fq[...] = exchange(squares_wide, w, 8, 0, 4)
    for copy in sent:
        copy.wait_send()


def reduce_all(n1, gq, attended, gp, n2, gh, act, gf, small):
    low, full = jnp.bfloat16, jnp.float32
    arrays = (n1, gq, attended, gp, n2, gh, act, gf)
    width = gq.shape[1] + gp.shape[1] + gh.shape[1]
    rows_in, rows_out = n1.shape[1] // 32, act.shape[1] // 32
    cols_out = gf.shape[1]
    vmem = pl.BlockSpec(memory_space=pltpu.VMEM)
    hbm = pl.BlockSpec(memory_space=pl.ANY)

    def trio(lead):
        return [
            pltpu.VMEM((IN_CHUNKS,) + lead + (rows_in, width // IN_CHUNKS), low),
            pltpu.VMEM((OUT_CHUNKS,) + lead + (rows_out, cols_out // OUT_CHUNKS), low),
            pltpu.VMEM(lead + (SMALL_ROWS, 128), full),
        ]

    padded = -(-n1.shape[0] // 256) * 256
    scratch = [pltpu.VMEM((padded, array.shape[1]), array.dtype) for array in arrays]
    scratch += trio((4, 2, 2, 2))[:2] + trio((4, 2, 2)) + trio((4, 2)) + trio((4,)) + trio((3,))
    copies = (IN_CHUNKS + OUT_CHUNKS + 1) * 6
    scratch += [
        pltpu.VMEM((4, 8, 128), full),
        pltpu.VMEM((8, 8, 128), full),
        pltpu.SemaphoreType.DMA((len(arrays) + 1,)),
        pltpu.SemaphoreType.DMA((copies,)),
        pltpu.SemaphoreType.DMA((copies,)),
        pltpu.SemaphoreType.DMA((12,)),
        pltpu.SemaphoreType.DMA((12,)),
    ]
    return pl.pallas_call(
        reduce_kernel,
        out_shape=(
            jax.ShapeDtypeStruct((rows_in, width), full),
            jax.ShapeDtypeStruct((rows_out, cols_out), full),
            jax.ShapeDtypeStruct((SMALL_ROWS, 128), full),
            jax.ShapeDtypeStruct((8, 128), full),
        ),
        in_specs=[hbm] * 8 + [vmem],
        out_specs=(vmem,) * 4,
        scratch_shapes=scratch,
        compiler_params=pltpu.CompilerParams(
            collective_id=1, has_side_effects=True, vmem_limit_bytes=62 << 20
        ),
        name="reduce_all",
    )(*arrays, small.reshape(4, 2, 2, 2, SMALL_ROWS, 128))


def cross_rows(left, right):
    return lax.dot_general(
        left, right, (((0,), (0,)), ((), ())), preferred_element_type=jnp.float32
    )


SIDE = 8
TALL = 512
CHUNK = 10
GAIN_ROW = 58
BIAS_ROW = 60


def tokens_of(value):
    return value.reshape(-1, SIDE, value.shape[-1])


def column_partial(value):
    return jnp.sum(tokens_of(value), axis=0)


def dot(left, right):
    return jnp.dot(left, right, preferred_element_type=jnp.float32)


def dot_nt(left, right):
    return lax.dot_general(
        left, right, (((1,), (1,)), ((), ())), preferred_element_type=jnp.float32
    )


def dot_tn(left, right):
    return lax.dot_general(
        left, right, (((0,), (0,)), ((), ())), preferred_element_type=jnp.float32
    )


def lane_tile(j):
    if isinstance(j, int):
        return pl.ds(j * 128, 128)
    return pl.ds(pl.multiple_of(j * 128, 128), 128)


def grid_rows(row, col):
    return pl.ds((1 + row * GRID + col) * SIDE, SIDE)


CLASS_ROWS = pl.ds(0, SIDE)


def put(grid, at, value):
    for j in range(D // 128):
        grid[j, at, :] = value[:, j * 128 : j * 128 + 128]


def get(grid, at, tiles=(0, 1, 2, 3)):
    return jnp.concatenate([grid[j, at, :] for j in tiles], axis=1)


def conv_tile(src, taps, base, width, reach, j, finish, flip=False):
    lanes = lane_tile(j)
    margin = width // 2
    offsets = range(-reach, reach + 1)

    def tap(dy, dx):
        if flip:
            dy, dx = -dy, -dx
        index = base + (dy + margin) * width + dx + margin
        return jnp.broadcast_to(taps[index : index + 1, lanes], (SIDE, 128))

    held = {(dy, dx): tap(dy, dx) for dy in offsets for dx in offsets}
    for row in range(GRID):
        sums = [jnp.zeros((SIDE, 128), jnp.float32) for _ in range(GRID)]
        for dy in offsets:
            if not 0 <= row + dy < GRID:
                continue
            line = [src[j, grid_rows(row + dy, col), :] for col in range(GRID)]
            for dx in offsets:
                for col in range(GRID):
                    if 0 <= col + dx < GRID:
                        sums[col] = sums[col] + line[col + dx] * held[dy, dx]
        for col in range(GRID):
            finish(grid_rows(row, col), sums[col])


def tap_sums(grad, src, base, width, reach, j, total):
    lanes = lane_tile(j)
    margin = width // 2
    offsets = range(-reach, reach + 1)
    for dy in offsets:
        sums = {dx: jnp.zeros((SIDE, 128), jnp.float32) for dx in offsets}
        for row in range(GRID):
            if not 0 <= row + dy < GRID:
                continue
            up = [grad[j, grid_rows(row, col), :] for col in range(GRID)]
            line = [src[j, grid_rows(row + dy, col), :] for col in range(GRID)]
            for dx in offsets:
                for col in range(GRID):
                    if 0 <= col + dx < GRID:
                        sums[dx] = sums[dx] + up[col] * line[col + dx]
        for dx in offsets:
            index = base + (dy + margin) * width + dx + margin
            total[index, :, lanes] = total[index, :, lanes] + sums[dx]


def mask_far_taps(rows):
    lanes = pl.ds(256, 128)
    keep = (lax.broadcasted_iota(jnp.int32, (1, 128), 1) >= 64).astype(jnp.float32)
    for tap in range(49):
        if max(abs(tap // 7 - 3), abs(tap % 7 - 3)) == 3:
            line = pl.ds(9 + tap, 1)
            rows[line, lanes] = rows[line, lanes] * keep


def relative_tiles(body):
    body(0, 1)
    body(1, 2)

    def rest(j, carry):
        body(j, 3)
        return carry

    lax.fori_loop(2, 4, rest, 0)


def all_tiles(body):
    def step(j, carry):
        body(j)
        return carry

    lax.fori_loop(0, 4, step, 0)


def all_chunks(body):
    def step(k, carry):
        body(pl.ds(pl.multiple_of(k * CHUNK * SIDE, 16), CHUNK * SIDE))
        return carry

    lax.fori_loop(0, 50 // CHUNK, step, 0)


def normalise(values):
    centred = values - jnp.mean(values, axis=-1, keepdims=True)
    scale = lax.rsqrt(jnp.mean(centred * centred, axis=-1, keepdims=True) + NORM_EPS)
    return centred * scale, scale


def norm_back(grad, hat, scale, gain):
    inner = grad * gain
    mean = jnp.mean(inner, axis=-1, keepdims=True)
    along = jnp.mean(inner * hat, axis=-1, keepdims=True)
    return scale * (inner - mean - hat * along)


def spread_images(src, grid, first, limit):
    for i in range(SIDE):
        image = src[i]
        keep = jnp.full(image.shape, first + i, jnp.int32) < limit
        at = pl.ds(i, image.shape[0], stride=SIDE)
        put(grid, at, jnp.where(keep, image.astype(jnp.float32), 0.0))


def set_parameters(small, par, heads):
    par[...] = small[...].astype(jnp.float32).T
    mask_far_taps(par)
    row_head = lax.broadcasted_iota(jnp.int32, heads.shape, 0) // 64
    col_head = lax.broadcasted_iota(jnp.int32, heads.shape, 1) // 64
    heads[...] = jnp.where(row_head == col_head, 1.0, 0.0).astype(heads.dtype)


def every_image(body):
    for i in range(SIDE):
        for half in range(2):
            body(pl.ds(i, TALL // SIDE, stride=SIDE), (2 * half, 2 * half + 1))


def forward_kernel(
    num_images, rows, counts, x_in, dy_in, w_in, w_out, small,
    out, act_o, gh_o, n1_o, n2_o, at_o, gf_o, gp_o, gx_o, xt_o, hat_o, sc_o, q_o, k_o, v_o, cv_o,
    cols_o, hcols_o,
    par, heads, x, x1, v, q, k, conv, hat2, slope, gn, scale2,
):
    low = jnp.bfloat16
    step = pl.program_id(0)
    first = step * SIDE
    live = pl.ds(0, rows)

    @pl.when(step == 0)
    def _():
        set_parameters(small, par, heads)
        for grid in (q, k, v):
            grid[...] = jnp.zeros_like(grid)
        cols_o[...] = jnp.zeros_like(cols_o)
        hcols_o[...] = jnp.zeros_like(hcols_o)

    def bias(row):
        return par[BIAS_ROW + row : BIAS_ROW + row + 1, :]

    def gain(row):
        return par[GAIN_ROW + row : GAIN_ROW + row + 1, :]

    spread_images(x_in, x, first, num_images)
    xt_o[...] = get(x, live).astype(low)
    spread_images(dy_in, gn, first, jnp.minimum(counts[0], num_images))
    gf_o[...] = get(gn, live).astype(low)

    def position(j):
        lanes = lane_tile(j)
        shift = jnp.broadcast_to(par[BIAS_ROW + 10 : BIAS_ROW + 11, lanes], (SIDE, 128))

        def finish(at, total):
            x1[j, at, :] = x[j, at, :] + total + shift

        conv_tile(x, par, 0, 3, 1, j, finish)
        x1[j, CLASS_ROWS, :] = x[j, CLASS_ROWS, :]

    all_tiles(position)

    def first_norm(at):
        hat, scale = normalise(get(x1, at))
        hat_o[at, :] = hat.astype(low)
        sc_o[at, :] = jnp.broadcast_to(scale, (CHUNK * SIDE, 128))
        n1_o[at, :] = (hat * gain(0) + bias(0)).astype(low)

    all_chunks(first_norm)
    n1 = n1_o[...]
    put(gn, live, dot(n1, w_in[:, D : 2 * D]))

    def weights(j):
        lanes = lane_tile(j)
        keys = tokens_of(gn[j, live, :])
        powers = jnp.exp(keys - jnp.max(keys, axis=0, keepdims=True))
        share = 0.125 / jnp.sum(powers, axis=0, keepdims=True)
        value = (powers * share).reshape(-1, 128)
        k[j, live, :] = value
        k_o[:, lanes] = value.astype(low)

    all_tiles(weights)
    value = dot(n1, w_in[:, 2 * D : 3 * D]) + bias(3)
    put(v, live, value)
    v_o[...] = value.astype(low)

    def relative(j, reach):
        lanes = lane_tile(j)
        shift = jnp.broadcast_to(par[BIAS_ROW + 11 : BIAS_ROW + 12, lanes], (SIDE, 128))

        def finish(at, total):
            conv[j, at, :] = total + shift

        conv_tile(v, par, 9, 7, reach, j, finish)
        conv[j, CLASS_ROWS, :] = jnp.zeros((SIDE, 128), jnp.float32)

    relative_tiles(relative)
    cv_o[...] = get(conv, live).astype(low)
    value = dot(n1, w_in[:, :D]) + bias(2)
    q_o[...] = value.astype(low)
    put(q, live, value)

    def attention(at, tiles):
        context = dot_tn(get(k, at, tiles).astype(low), get(v, at, tiles).astype(low))
        context = context.astype(low) * heads[...]
        value = dot(get(q, at, tiles).astype(low), context)
        for n, j in enumerate(tiles):
            gn[j, at, :] = value[:, n * 128 : n * 128 + 128]

    every_image(attention)
    for j in range(D // 128):
        at_o[:, lane_tile(j)] = (gn[j, live, :] + conv[j, live, :] * q[j, live, :]).astype(low)
    put(x1, live, get(x1, live) + (dot(at_o[...], w_in[:, 3 * D : 4 * D]) + bias(4)))

    def second_norm(at):
        hat, scale = normalise(get(x1, at))
        hat2[at, :] = hat
        scale2[at, :] = jnp.broadcast_to(scale, (CHUNK * SIDE, 128))
        n2_o[at, :] = (hat * gain(1) + bias(1)).astype(low)

    all_chunks(second_norm)
    n2 = n2_o[...]
    for part in range(MLP_WIDTH // D):
        cols = pl.ds(part * D, D)
        put(gn, live, dot(n2, w_in[:, pl.ds((4 + part) * D, D)]))

        def gelu(at):
            h = get(gn, at) + bias(5 + part)
            below = 0.5 + 0.5 * lax.erf(h * (0.5**0.5))
            density = jnp.exp(-0.5 * h * h) * 0.3989422804014327
            act_o[at, cols] = (h * below).astype(low)
            slope[at, cols] = below + h * density

        all_chunks(gelu)
    put(x1, live, get(x1, live) + dot(act_o[...], w_out[...]) + bias(9))
    for i in range(SIDE):
        out[i] = get(x1, pl.ds(i, out.shape[1], stride=SIDE)).astype(low)

    gf = gf_o[...]
    for part in range(MLP_WIDTH // D):
        cols = pl.ds(part * D, D)
        grad = (dot_nt(gf, w_out[cols, :]) * slope[:, cols]).astype(low)
        gh_o[:, cols] = grad
        hcols_o[:, cols] = hcols_o[:, cols] + column_partial(grad.astype(jnp.float32))
    put(gn, live, dot_nt(gh_o[...], w_in[:, 4 * D :]))

    def second_back(at):
        grad = get(gn, at)
        hat = hat2[at, :]
        scale = scale2[at, 0:1]
        upstream = gf_o[at, :].astype(jnp.float32)
        total = upstream + norm_back(grad, hat, scale, gain(1))
        gx_o[at, :] = total
        rounded = total.astype(low)
        gp_o[at, :] = rounded
        cols_o[0] = cols_o[0] + column_partial(grad)
        cols_o[1] = cols_o[1] + column_partial(grad * hat)
        cols_o[2] = cols_o[2] + column_partial(rounded.astype(jnp.float32))
        cols_o[3] = cols_o[3] + column_partial(upstream)

    all_chunks(second_back)


def backward_kernel(
    rows, w_in, small, cols_in, hcols_in, gx, hat, sc, q_in, k_in, v_in, cv, xt,
    out, gq_o, small_o,
    par, heads, cols, taps, lines, g, gc, q, k, v, gq, gk, gv, x, g1,
):
    low = jnp.bfloat16
    step = pl.program_id(0)
    live = pl.ds(0, rows)

    @pl.when(step == 0)
    def _():
        set_parameters(small, par, heads)
        for grid in (g, q, k, v, gq, gk, gv):
            grid[...] = jnp.zeros_like(grid)
        cols[...] = jnp.zeros_like(cols)
        taps[...] = jnp.zeros_like(taps)

    grad = dot_nt(gx[...].astype(low), w_in[:, 3 * D : 4 * D])
    put(g, live, grad)
    for j in range(D // 128):
        lanes = lane_tile(j)
        part = g[j, live, :]
        queries = q_in[:, lanes].astype(jnp.float32)
        q[j, live, :] = queries
        k[j, live, :] = k_in[:, lanes].astype(jnp.float32)
        v[j, live, :] = v_in[:, lanes].astype(jnp.float32)
        x[j, live, :] = xt[:, lanes].astype(jnp.float32)
        gq[j, live, :] = part * cv[:, lanes].astype(jnp.float32)
        gc[j, live, :] = part * queries
        gc[j, CLASS_ROWS, :] = jnp.zeros((SIDE, 128), jnp.float32)
        cols[0, :, lanes] = cols[0, :, lanes] + column_partial(gc[j, live, :])

    def relative(j, reach):
        def finish(at, total):
            gv[j, at, :] = total

        conv_tile(gc, par, 9, 7, reach, j, finish, flip=True)
        gv[j, CLASS_ROWS, :] = jnp.zeros((SIDE, 128), jnp.float32)
        tap_sums(gc, v, 9, 7, reach, j, taps)

    relative_tiles(relative)

    def attention(at, tiles):
        qs, ks, vs, gs = (get(grid, at, tiles).astype(low) for grid in (q, k, v, g))
        context = dot_tn(ks, vs).astype(low) * heads[...]
        grads = dot_tn(qs, gs).astype(low) * heads[...]
        to_q, to_k, to_v = dot_nt(gs, context), dot_nt(vs, grads), dot(ks, grads)
        for n, j in enumerate(tiles):
            here = slice(n * 128, n * 128 + 128)
            gq[j, at, :] = gq[j, at, :] + to_q[:, here]
            gk[j, at, :] = to_k[:, here]
            gv[j, at, :] = gv[j, at, :] + to_v[:, here]

    every_image(attention)

    def finish_qkv(j):
        lanes = lane_tile(j)
        share = tokens_of(k[j, live, :])
        up = tokens_of(gk[j, live, :])
        along = jnp.sum(share * up, axis=0, keepdims=True) * 8.0
        gq_o[:, pl.ds(pl.multiple_of(D + j * 128, 128), 128)] = (
            (share * (up - along)).reshape(-1, 128).astype(low)
        )
        part = gq[j, live, :].astype(low)
        gq_o[:, lanes] = part
        cols[1, :, lanes] = cols[1, :, lanes] + column_partial(part.astype(jnp.float32))
        part = gv[j, live, :].astype(low)
        gq_o[:, pl.ds(pl.multiple_of(2 * D + j * 128, 128), 128)] = part
        cols[2, :, lanes] = cols[2, :, lanes] + column_partial(part.astype(jnp.float32))

    all_tiles(finish_qkv)
    put(gk, live, dot_nt(gq_o[...], w_in[:, : 3 * D]))

    def first_back(at):
        grad = get(gk, at)
        hats = hat[at, :].astype(jnp.float32)
        total = gx[at, :] + norm_back(grad, hats, sc[at, 0:1], par[GAIN_ROW : GAIN_ROW + 1, :])
        put(g1, at, total)
        cols[3] = cols[3] + column_partial(grad)
        cols[4] = cols[4] + column_partial(grad * hats)
        cols[5] = cols[5] + column_partial(total)

    all_chunks(first_back)
    cols[5] = cols[5] - get(g1, CLASS_ROWS)

    def position(j):
        def finish(at, total):
            gv[j, at, :] = g1[j, at, :] + total

        conv_tile(g1, par, 0, 3, 1, j, finish, flip=True)
        gv[j, CLASS_ROWS, :] = g1[j, CLASS_ROWS, :]
        tap_sums(g1, x, 0, 3, 1, j, taps)

    all_tiles(position)
    for i in range(SIDE):
        out[i] = get(gv, pl.ds(i, out.shape[1], stride=SIDE))

    @pl.when(step == pl.num_programs(0) - 1)
    def _():
        lines[...] = jnp.zeros_like(lines)
        for tap in range(taps.shape[0]):
            lines[tap : tap + 1, :] = jnp.sum(taps[tap], axis=0, keepdims=True)
        mask_far_taps(lines)
        hidden = [hcols_in[:, i * D : i * D + D] for i in range(MLP_WIDTH // D)]
        order = [cols[4], cols_in[1], cols[3], cols_in[0], cols[1], cols[2], cols_in[2]]
        for i, part in enumerate(order + hidden + [cols_in[3], cols[5], cols[0]]):
            row = GAIN_ROW + i
            lines[row : row + 1, :] = jnp.sum(part, axis=0, keepdims=True)
        small_o[...] = lines[...].T


def fixed(shape):
    zeros = (0,) * len(shape)
    return pl.BlockSpec(shape, lambda g: zeros, pipeline_mode=pl.Buffered(1))


def compute(images, cotangent, counts, w_in, w_out, small):
    low, full = jnp.bfloat16, jnp.float32
    num_images, num_tokens, channels = images.shape
    groups = -(-num_images // SIDE)
    rows = num_tokens * SIDE
    total = groups * rows

    def block(cols):
        return pl.BlockSpec((rows, cols), lambda g: (g, 0))

    def image_block():
        return pl.BlockSpec((SIDE, num_tokens, channels), lambda g: (g, 0, 0))

    def made(cols, kind=low):
        return jax.ShapeDtypeStruct((total, cols), kind)

    def grid():
        return pltpu.VMEM((channels // 128, TALL, 128), full)

    shared = [pltpu.VMEM((128, channels), full), pltpu.VMEM((256, 256), low)]
    wide = w_out.shape[0]
    forward = pl.pallas_call(
        functools.partial(forward_kernel, num_images, rows),
        grid=(groups,),
        in_specs=[
            pl.BlockSpec(memory_space=pltpu.SMEM),
            image_block(),
            image_block(),
            fixed(w_in.shape),
            fixed(w_out.shape),
            fixed(small.shape),
        ],
        out_specs=[image_block(), block(wide), block(wide)]
        + [block(channels)] * 8
        + [block(128)]
        + [block(channels)] * 4
        + [fixed((4, SIDE, channels)), fixed((SIDE, wide))],
        out_shape=[jax.ShapeDtypeStruct(images.shape, low), made(wide), made(wide)]
        + [made(channels)] * 5
        + [made(channels, full), made(channels), made(channels), made(128, full)]
        + [made(channels)] * 4
        + [
            jax.ShapeDtypeStruct((4, SIDE, channels), full),
            jax.ShapeDtypeStruct((SIDE, wide), full),
        ],
        scratch_shapes=shared
        + [grid() for _ in range(6)]
        + [pltpu.VMEM((rows, channels), full), pltpu.VMEM((rows, wide), full), grid(), pltpu.VMEM((rows, 128), full)],
        compiler_params=pltpu.CompilerParams(vmem_limit_bytes=60 << 20),
        name="forward",
    )
    (
        out, act, gh, n1, n2, attended, gf, gp, gx, xt, hat, scale, q, k, v, cv, cols, hcols,
    ) = forward(counts, images, cotangent, w_in, w_out, small)

    backward = pl.pallas_call(
        functools.partial(backward_kernel, rows),
        grid=(groups,),
        in_specs=[
            pl.BlockSpec(
                (channels, 4 * channels), lambda g: (0, 0), pipeline_mode=pl.Buffered(1)
            ),
            fixed(small.shape),
            fixed(cols.shape),
            fixed(hcols.shape),
            block(channels),
            block(channels),
            block(128),
        ]
        + [block(channels)] * 5,
        out_specs=[image_block(), block(3 * channels), fixed(small.shape)],
        out_shape=[
            jax.ShapeDtypeStruct(images.shape, full),
            made(3 * channels),
            jax.ShapeDtypeStruct(small.shape, full),
        ],
        scratch_shapes=shared
        + [
            pltpu.VMEM((6, SIDE, channels), full),
            pltpu.VMEM((GAIN_ROW, SIDE, channels), full),
            pltpu.VMEM((128, channels), full),
        ]
        + [grid() for _ in range(10)],
        compiler_params=pltpu.CompilerParams(vmem_limit_bytes=60 << 20),
        name="backward",
    )
    input_grad, gq, grad_small = backward(
        w_in, small, cols, hcols, gx, hat, scale, q, k, v, cv, xt
    )
    return out, input_grad, (n1, gq, attended, gp, n2, gh, act, gf), grad_small


def adamw_update(master, first_moment, second_moment, gradient, clip_factor, rate, decay):
    clipped = gradient * clip_factor
    first_new = BETA_ONE * first_moment + (1.0 - BETA_ONE) * clipped
    second_new = BETA_TWO * second_moment + (1.0 - BETA_TWO) * clipped * clipped
    first_hat = first_new / (1.0 - BETA_ONE**STEP)
    second_hat = second_new / (1.0 - BETA_TWO**STEP)
    master_new = master - rate * (first_hat / (jnp.sqrt(second_hat) + ADAM_EPS) + decay * master)
    return (master_new, first_new, second_new, master_new.astype(jnp.bfloat16))


def local(
    images,
    cotangent,
    counts,
    in_mats,
    in_mats_m,
    in_mats_v,
    out_mat,
    out_mat_m,
    out_mat_v,
    kernels,
    kernels_m,
    kernels_v,
    gains,
    gains_m,
    gains_v,
    biases,
    biases_m,
    biases_v,
    special,
):
    in_copy = in_mats.astype(jnp.bfloat16)
    out_copy = out_mat.astype(jnp.bfloat16)
    shards = (kernels, gains, biases)
    sizes = [shard.shape[0] for shard in shards]
    used = sum(sizes)
    count_row = jnp.broadcast_to(counts.astype(jnp.float32)[:, None], (1, kernels.shape[1]))
    rows = jnp.concatenate(shards + (count_row,), axis=0)
    small = jnp.pad(rows, ((0, 128 - used - 1), (0, 0))).T.astype(jnp.bfloat16)
    if special:
        all_in, all_out, all_small = gather_all(in_copy, out_copy, small)
    else:
        all_in, all_out, all_small = (
            lax.all_gather(part, ("wide", "narrow"), axis=0, tiled=True)
            for part in (in_copy, out_copy, small)
        )
    all_small = all_small.reshape(-1, small.shape[0], 128)
    live_total = jnp.sum(all_small[:, 0, used].astype(jnp.float32)) * images.shape[1]
    scale_factor = 1.0 / live_total
    block_out, input_grad, factors, grad_small = compute(
        images,
        cotangent,
        counts,
        all_in.reshape(-1, in_copy.shape[1]),
        all_out.reshape(-1, out_copy.shape[1]),
        all_small.reshape(-1, 128),
    )
    if special:
        sum_in, sum_out, sum_small, squares = reduce_all(*factors, grad_small)
        total_squares = jnp.sum(squares)
    else:
        n1, gq, attended, gp, n2, gh, act, gf = factors
        grad_in = jnp.concatenate(
            [cross_rows(n1, gq), cross_rows(attended, gp), cross_rows(n2, gh)], axis=1
        )
        grad_fc2 = cross_rows(act, gf)
        sum_in, sum_out, sum_small = (
            lax.psum_scatter(
                part.astype(jnp.float32), ("wide", "narrow"), scatter_dimension=0, tiled=True
            )
            for part in (grad_in, grad_fc2, grad_small)
        )
        total_squares = lax.psum(
            sum(jnp.sum(part * part) for part in (sum_in, sum_out, sum_small)),
            ("wide", "narrow"),
        )
    rows = sum_small.T
    summed = (
        sum_in,
        sum_out,
        rows[: sizes[0]],
        rows[sizes[0] : sizes[0] + sizes[1]],
        rows[sizes[0] + sizes[1] : used],
    )
    summed = tuple(part * scale_factor for part in summed)
    grad_norm = jnp.sqrt(total_squares) * scale_factor
    clip_factor = jnp.minimum(1.0, 1.0 / (grad_norm + 1e-06))
    in_new = adamw_update(
        in_mats, in_mats_m, in_mats_v, summed[0], clip_factor, RATES[0], DECAYS[0]
    )
    out_new = adamw_update(
        out_mat, out_mat_m, out_mat_v, summed[1], clip_factor, RATES[1], DECAYS[1]
    )
    kern_new = adamw_update(
        kernels, kernels_m, kernels_v, summed[2], clip_factor, RATES[2], DECAYS[2]
    )
    gain_new = adamw_update(gains, gains_m, gains_v, summed[3], clip_factor, RATES[3], DECAYS[3])
    bias_new = adamw_update(biases, biases_m, biases_v, summed[4], clip_factor, RATES[4], DECAYS[4])
    return (
        block_out,
        input_grad,
        grad_norm,
        in_new[0],
        in_new[1],
        in_new[2],
        in_new[3],
        out_new[0],
        out_new[1],
        out_new[2],
        out_new[3],
        kern_new[0],
        kern_new[1],
        kern_new[2],
        kern_new[3],
        gain_new[0],
        gain_new[1],
        gain_new[2],
        gain_new[3],
        bias_new[0],
        bias_new[1],
        bias_new[2],
        bias_new[3],
    )


def solution(mesh):
    placed = (
        P(("wide", "narrow"), None, None),
        P(("wide", "narrow"), None, None),
        P(("wide", "narrow")),
        P(("wide", "narrow"), None),
        P(("wide", "narrow"), None),
        P(("wide", "narrow"), None),
        P(("wide", "narrow"), None),
        P(("wide", "narrow"), None),
        P(("wide", "narrow"), None),
        P(None, ("wide", "narrow")),
        P(None, ("wide", "narrow")),
        P(None, ("wide", "narrow")),
        P(None, ("wide", "narrow")),
        P(None, ("wide", "narrow")),
        P(None, ("wide", "narrow")),
        P(None, ("wide", "narrow")),
        P(None, ("wide", "narrow")),
        P(None, ("wide", "narrow")),
    )
    special = dict(mesh.shape) == {"wide": 8, "narrow": 4}
    return jax.shard_map(
        functools.partial(local, special=special),
        mesh=mesh,
        in_specs=placed,
        out_specs=(
            P(("wide", "narrow"), None, None),
            P(("wide", "narrow"), None, None),
            P(),
            P(("wide", "narrow"), None),
            P(("wide", "narrow"), None),
            P(("wide", "narrow"), None),
            P(("wide", "narrow"), None),
            P(("wide", "narrow"), None),
            P(("wide", "narrow"), None),
            P(("wide", "narrow"), None),
            P(("wide", "narrow"), None),
            P(None, ("wide", "narrow")),
            P(None, ("wide", "narrow")),
            P(None, ("wide", "narrow")),
            P(None, ("wide", "narrow")),
            P(None, ("wide", "narrow")),
            P(None, ("wide", "narrow")),
            P(None, ("wide", "narrow")),
            P(None, ("wide", "narrow")),
            P(None, ("wide", "narrow")),
            P(None, ("wide", "narrow")),
            P(None, ("wide", "narrow")),
            P(None, ("wide", "narrow")),
        ),
        check_vma=False,
    )
```

```python
import functools

import jax
import jax.numpy as jnp
from jax import lax
from jax.experimental import pallas as pl
from jax.experimental.pallas import tpu as pltpu
from jax.sharding import PartitionSpec as P

D = 512
HEADS = 8
MLP_WIDTH = 2048
GRID = 7
STEP = 10
BROWS = 12


NORM_EPS = 1e-06
BETA_ONE = 0.9
BETA_TWO = 0.999
ADAM_EPS = 1e-08
HIGHEST = lax.Precision.HIGHEST
RATES = (0.04, 0.02, 0.1, 0.8, 0.25)
DECAYS = (0.05, 0.05, 0.05, 0.0, 0.0)


MESH_ID = pl.DeviceIdType.MESH
SPLIT = 3072
SMALL_ROWS = 16


def place():
    w = lax.axis_index("wide")
    n = lax.axis_index("narrow")
    return w // 2, w % 2, n // 2, n % 2


def device(z, y, x, c):
    return (z * 2 + y, x * 2 + c)


def neighbour(at, axis, step=1):
    z, y, x, c = at
    if axis == 0:
        return (lax.rem(z + step, 4), y, x, c)
    if axis == 1:
        return (z, 1 - y, x, c)
    if axis == 2:
        return (z, y, 1 - x, c)
    return (z, y, x, 1 - c)


def square_of(lines):
    return jnp.concatenate([lines, jnp.zeros((128 - lines.shape[0], 128), lines.dtype)], axis=0)


def gather_kernel(
    counts, wi_f, wo_f, kern, gain, bias, gi, go, gs, wi, wo, sm, lines, send_sem, recv_sem, own_sem
):
    at = place()
    z, y, x, c = at
    partners = [device(*neighbour(at, 0, s)) for s in (1, 2, 3)]
    partners += [device(*neighbour(at, a)) for a in (1, 2, 3)]
    barrier = pltpu.get_barrier_semaphore()
    for partner in partners:
        pl.semaphore_signal(barrier, inc=1, device_id=partner, device_id_type=MESH_ID)
    low = jnp.bfloat16
    wi[...] = wi_f[...].astype(low)
    wo[...] = wo_f[...].astype(low)
    kept, own = kern.shape[1], kern.shape[0]
    after_gain = kept + gain.shape[0]
    after_bias = after_gain + bias.shape[0]
    lines[...] = jnp.zeros_like(lines)
    lines[kept:after_gain, 0:own] = gain[...]
    lines[after_gain:after_bias, 0:own] = bias[...]
    lines[after_bias : after_bias + 1, :] = jnp.full((1, 128), counts[0], jnp.int32).astype(
        jnp.float32
    )
    turned = lines[...].T[0:own, :]
    lines[0:own, :] = turned
    lines[0:own, 0:kept] = kern[...]
    sm[...] = lines[0:own, :].astype(low)
    pl.semaphore_wait(barrier, len(partners))

    width = wi.shape[1]
    pieces = (
        (wi, gi, 0, pl.ds(0, SPLIT)),
        (sm, gs, 0, pl.ds(0, 128)),
        (wi, gi, 1, pl.ds(SPLIT, width - SPLIT)),
        (wo, go, 1, pl.ds(0, wo.shape[1])),
    )
    orders = ((0, 1, 2, 3), (0, 2, 1, 3))

    def slot(r):
        zs = lax.rem(z - r[0] + 4, 4)
        ys = 1 - y if r[1] else y
        xs = 1 - x if r[2] else x
        cs = 1 - c if r[3] else c
        return ((zs * 2 + ys) * 2 + xs) * 2 + cs

    def flat(r):
        return ((r[0] * 2 + r[1]) * 2 + r[2]) * 2 + r[3]

    def moved(r, axis, step):
        r = list(r)
        r[axis] = step
        return tuple(r)

    def transfer(p, r, axis, step):
        own, out, color, cols = pieces[p]
        there = out.at[slot(r), :, cols]
        here = own.at[:, cols] if r == (0, 0, 0, 0) else there
        to = moved(r, axis, step)
        return pltpu.make_async_remote_copy(
            src_ref=here,
            dst_ref=there,
            send_sem=send_sem.at[p, flat(to)],
            recv_sem=recv_sem.at[p, flat(to)],
            device_id=device(*neighbour(at, axis, step)),
            device_id_type=MESH_ID,
        )

    def onward(p, r):
        order = orders[pieces[p][2]]
        last = max([i for i in range(4) if r[order[i]]], default=-1)
        for i in range(last + 1, 4):
            axis = order[i]
            for step in (1, 2, 3) if axis == 0 else (1,):
                yield axis, step

    started = []

    def forward(p, r):
        for axis, step in onward(p, r):
            copy = transfer(p, r, axis, step)
            copy.start()
            started.append(copy)

    zero = (0, 0, 0, 0)
    for p in range(4):
        forward(p, zero)
    own_copies = []
    for p in range(4):
        own, out, color, cols = pieces[p]
        copy = pltpu.make_async_copy(
            own.at[:, cols], out.at[slot(zero), :, cols], own_sem.at[p]
        )
        copy.start()
        own_copies.append(copy)

    def arrival(p, r):
        order = orders[pieces[p][2]]
        axis = [a for a in order if r[a]][-1]
        back = moved(r, axis, 0)
        return transfer(p, back, axis, r[axis])

    offsets = [
        (dz, dy, dx, dc) for dz in range(4) for dy in range(2) for dx in range(2) for dc in range(2)
    ]
    cost = {0: 0, 1: 2, 2: 4, 3: 2}

    def when(r):
        return cost[r[0]] + r[1] * 2 + r[2] * 2 + r[3]

    for r in sorted(offsets[1:], key=when):
        for p in range(4):
            copy = arrival(p, r)
            copy.wait_recv()
            forward(p, r)
    for copy in started:
        copy.wait_send()
    for copy in own_copies:
        copy.wait()


def gather_all(counts, in_mats, out_mat, kern, gain, bias):
    low = jnp.bfloat16
    hbm = pl.BlockSpec(memory_space=pl.ANY)
    vmem = pl.BlockSpec(memory_space=pltpu.VMEM)
    shapes = (in_mats.shape, out_mat.shape, (SMALL_ROWS, 128))
    return pl.pallas_call(
        gather_kernel,
        out_shape=tuple(jax.ShapeDtypeStruct((32,) + shape, low) for shape in shapes),
        in_specs=[pl.BlockSpec(memory_space=pltpu.SMEM)] + [vmem] * 5,
        out_specs=(hbm,) * 3,
        scratch_shapes=[pltpu.VMEM(shape, low) for shape in shapes]
        + [
            pltpu.VMEM((128, 128), jnp.float32),
            pltpu.SemaphoreType.DMA((4, 32)),
            pltpu.SemaphoreType.DMA((4, 32)),
            pltpu.SemaphoreType.DMA((4,)),
        ],
        compiler_params=pltpu.CompilerParams(collective_id=0, has_side_effects=True),
        name="gather_all",
    )(counts, in_mats, out_mat, kern, gain, bias)


def add_low(left, right):
    return (left.astype(jnp.float32) + right.astype(jnp.float32)).astype(left.dtype)


IN_CHUNKS = 4
OUT_CHUNKS = 2
LAGS = (2, 4, 6, 8)


def reduce_kernel(
    n1_h, gq_h, at_h, gp_h, n2_h, gh_h, act_h, gf_h, gs, fi, fo, fs, fq,
    n1, gq, at_v, gp, n2, gh, act, gf,
    gi, go, r0i, r0o, r0s, r1i, r1o, r1s, r2i, r2o, r2s, r3i, r3o, r3s,
    squares_narrow, squares_wide, load_sem, send_sem, recv_sem, norm_send, norm_recv,
):
    at = place()
    z, y, x, c = at
    w = z * 2 + y
    n = x * 2 + c
    loads = []
    half = gh.shape[1] // 2
    for src, dst, cols in (
        (n2_h, n2, None),
        (gh_h, gh, pl.ds(0, half)),
        (gh_h, gh, pl.ds(half, half)),
        (gf_h, gf, None),
        (act_h, act, None),
        (n1_h, n1, None),
        (gq_h, gq, None),
        (at_h, at_v, None),
        (gp_h, gp, None),
    ):
        real, padded = src.shape[0], dst.shape[0]
        if cols is None:
            cols = pl.ds(0, src.shape[1])
        if padded > real:
            dst[pl.ds(real, padded - real), cols] = jnp.zeros(
                (padded - real, cols.size), dst.dtype
            )
        src, dst = src.at[:, cols], dst.at[pl.ds(0, real), cols]
        copy = pltpu.make_async_copy(src, dst, load_sem.at[len(loads)])
        copy.start()
        loads.append(copy)
    waited = [0]

    def loaded(upto):
        while waited[0] < upto:
            loads[waited[0]].wait()
            waited[0] += 1

    partners = [(w, lax.rem(n + s, 4)) for s in (1, 2, 3)]
    partners += [(lax.rem(w + s, 8), n) for s in range(1, 8)]
    barrier = pltpu.get_barrier_semaphore()
    for partner in partners:
        pl.semaphore_signal(barrier, inc=1, device_id=partner, device_id_type=MESH_ID)

    count = [0]
    sent = []

    def send(src, dst, axis, step=1):
        index = count[0]
        count[0] += 1
        copy = pltpu.make_async_remote_copy(
            src_ref=src,
            dst_ref=dst,
            send_sem=send_sem.at[index],
            recv_sem=recv_sem.at[index],
            device_id=device(*neighbour(at, axis, step)),
            device_id_type=MESH_ID,
        )
        copy.start()
        sent.append(copy)
        return copy

    def product(left, right, cols):
        value = dot_tn(left[...], right[:, cols]).astype(gi.dtype)
        return value.reshape(4, 2, 2, 2, -1, value.shape[1])

    def make_in(chunk):
        width = gi.shape[-1]
        if chunk >= 2:
            loaded(chunk)
            gi[chunk] = product(n2, gh, pl.ds((chunk - 2) * width, width))
        elif chunk == 1:
            loaded(9)
            gi[1, :, :, :, :, :, pl.ds(0, D)] = product(n1, gq, pl.ds(width, D))
            gi[1, :, :, :, :, :, pl.ds(D, D)] = product(at_v, gp, pl.ds(0, D))
        else:
            loaded(7)
            gi[0] = product(n1, gq, pl.ds(0, width))

    def make_out(chunk):
        if chunk:
            return
        loaded(5)
        width = go.shape[-1]

        def block(m, carry):
            left = act[:, pl.ds(pl.multiple_of(m * D, D), D)]
            value = dot_tn(left, gf[...]).astype(go.dtype)
            for k in range(OUT_CHUNKS):
                part = value[:, k * width : k * width + width]
                go[k, m] = part.reshape(2, 2, 2, -1, width)
            return carry

        lax.fori_loop(0, 4, block, 0)

    def entry(make, chunk, color, g, r0, r1, r2, r3, out, cols):
        return dict(
            make=make, chunk=chunk, color=color, g=g, r0=r0, r1=r1, r2=r2, r3=r3, out=out, cols=cols
        )

    entries = [entry(None, 0, 1, gs, r0s, r1s, r2s, r3s, fs, pl.ds(0, 128))]

    def in_entry(chunk, color):
        refs = [ref.at[chunk] for ref in (gi, r0i, r1i, r2i, r3i)]
        width = gi.shape[-1]
        return entry(make_in, chunk, color, *refs, fi, pl.ds(chunk * width, width))

    def out_entry(chunk, color):
        refs = [ref.at[chunk] for ref in (go, r0o, r1o, r2o, r3o)]
        width = go.shape[-1]
        return entry(make_out, chunk, color, *refs, fo, pl.ds(chunk * width, width))

    entries += [in_entry(2, 0), in_entry(3, 1), out_entry(0, 0), out_entry(1, 1)]
    entries += [in_entry(0, 0), in_entry(1, 1)]

    def begin(e):
        e["copy"] = send(e["g"].at[:, :, :, 1 - c], e["r0"], 3)

    def across(e):
        e["copy"].wait_recv()
        g, r0 = e["g"], e["r0"]

        def add(k, carry):
            zi, yi, xi = k // 4, lax.rem(k // 2, 2), lax.rem(k, 2)
            r0[zi, yi, xi] = add_low(g[zi, yi, xi, c], r0[zi, yi, xi])
            return carry

        lax.fori_loop(0, 16, add, 0)
        if e["color"] == 0:
            e["copy"] = send(r0.at[:, :, 1 - x], e["r1"], 2)
        else:
            e["copy"] = send(r0.at[:, 1 - y], e["r1"], 1)

    def onward(e):
        e["copy"].wait_recv()
        r0, r1, color = e["r0"], e["r1"], e["color"]

        def add(k, carry):
            zi, j = k // 2, lax.rem(k, 2)
            own = r0[zi, j, x] if color == 0 else r0[zi, y, j]
            r1[zi, j] = add_low(own, r1[zi, j])
            return carry

        lax.fori_loop(0, 8, add, 0)
        if color == 0:
            e["copy"] = send(r1.at[:, 1 - y], e["r2"], 1)
        else:
            e["copy"] = send(r1.at[:, 1 - x], e["r2"], 2)

    def along(e):
        e["copy"].wait_recv()
        r1, r2, keep = e["r1"], e["r2"], y if e["color"] == 0 else x

        def add(k, carry):
            r2[k] = add_low(r1[k, keep], r2[k])
            return carry

        lax.fori_loop(0, 4, add, 0)
        e["copies"] = [
            send(r2.at[lax.rem(z + step, 4)], e["r3"].at[step - 1], 0, step) for step in (1, 2, 3)
        ]

    squares = [jnp.zeros((8, 128), jnp.float32)]

    def finish(e):
        for copy in e["copies"]:
            copy.wait_recv()
        value = e["r2"][z].astype(jnp.float32)
        for k in range(3):
            value = value + e["r3"][k].astype(jnp.float32)
        e["out"][:, e["cols"]] = value
        rows, cols = value.shape
        total = jnp.sum((value * value).reshape(rows // 8, 8, cols), axis=0)
        for j in range(cols // 128):
            squares[0] = squares[0] + total[:, j * 128 : j * 128 + 128]

    for t in range(len(entries) + LAGS[-1]):
        for action, lag in zip((finish, along, onward, across), LAGS[::-1]):
            if 0 <= t - lag < len(entries):
                action(entries[t - lag])
        if t < len(entries):
            e = entries[t]
            if e["make"] is not None:
                e["make"](e["chunk"])
            if t == 0:
                pl.semaphore_wait(barrier, len(partners))
            begin(e)

    def exchange(buffer, mine, size, axis, base):
        copies = []
        for step in range(1, size):
            to = lax.rem(mine + step, size)
            copy = pltpu.make_async_remote_copy(
                src_ref=buffer.at[mine],
                dst_ref=buffer.at[mine],
                send_sem=norm_send.at[base + step],
                recv_sem=norm_recv.at[base + step],
                device_id=(to, n) if axis == 0 else (w, to),
                device_id_type=MESH_ID,
            )
            copy.start()
            copies.append(copy)
        for copy in copies:
            copy.wait()
        value = buffer[0]
        for k in range(1, size):
            value = value + buffer[k]
        return value

    squares_narrow[n] = squares[0]
    squares_wide[w] = exchange(squares_narrow, n, 4, 1, 0)
    fq[...] = exchange(squares_wide, w, 8, 0, 4)
    for copy in sent:
        copy.wait_send()


def reduce_all(n1, gq, attended, gp, n2, gh, act, gf, small):
    low, full = jnp.bfloat16, jnp.float32
    arrays = (n1, gq, attended, gp, n2, gh, act, gf)
    width = gq.shape[1] + gp.shape[1] + gh.shape[1]
    rows_in, rows_out = n1.shape[1] // 32, act.shape[1] // 32
    cols_out = gf.shape[1]
    vmem = pl.BlockSpec(memory_space=pltpu.VMEM)
    hbm = pl.BlockSpec(memory_space=pl.ANY)

    def trio(lead):
        return [
            pltpu.VMEM((IN_CHUNKS,) + lead + (rows_in, width // IN_CHUNKS), low),
            pltpu.VMEM((OUT_CHUNKS,) + lead + (rows_out, cols_out // OUT_CHUNKS), low),
            pltpu.VMEM(lead + (SMALL_ROWS, 128), full),
        ]

    padded = -(-n1.shape[0] // 256) * 256
    scratch = [pltpu.VMEM((padded, array.shape[1]), array.dtype) for array in arrays]
    scratch += trio((4, 2, 2, 2))[:2] + trio((4, 2, 2)) + trio((4, 2)) + trio((4,)) + trio((3,))
    copies = (IN_CHUNKS + OUT_CHUNKS + 1) * 6
    scratch += [
        pltpu.VMEM((4, 8, 128), full),
        pltpu.VMEM((8, 8, 128), full),
        pltpu.SemaphoreType.DMA((len(arrays) + 1,)),
        pltpu.SemaphoreType.DMA((copies,)),
        pltpu.SemaphoreType.DMA((copies,)),
        pltpu.SemaphoreType.DMA((12,)),
        pltpu.SemaphoreType.DMA((12,)),
    ]
    return pl.pallas_call(
        reduce_kernel,
        out_shape=(
            jax.ShapeDtypeStruct((rows_in, width), full),
            jax.ShapeDtypeStruct((rows_out, cols_out), full),
            jax.ShapeDtypeStruct((SMALL_ROWS, 128), full),
            jax.ShapeDtypeStruct((8, 128), full),
        ),
        in_specs=[hbm] * 8 + [vmem],
        out_specs=(vmem,) * 4,
        scratch_shapes=scratch,
        compiler_params=pltpu.CompilerParams(
            collective_id=1, has_side_effects=True, vmem_limit_bytes=62 << 20
        ),
        name="reduce_all",
    )(*arrays, small.reshape(4, 2, 2, 2, SMALL_ROWS, 128))


def update_kernel(
    num_tokens,
    fi, fo, fs, fq, all_small,
    wi, wi_m, wi_v, wo, wo_m, wo_v, kern, kern_m, kern_v, gain, gain_m, gain_v, bias, bias_m, bias_v,
    norm_o,
    wi_o, wi_m_o, wi_v_o, wi_low, wo_o, wo_m_o, wo_v_o, wo_low,
    kern_o, kern_m_o, kern_v_o, kern_low, gain_o, gain_m_o, gain_v_o, gain_low,
    bias_o, bias_m_o, bias_v_o, bias_low,
):
    total = jnp.sum(fq[...], axis=0, keepdims=True)
    total = jnp.sum(total, axis=1, keepdims=True)
    kept = kern.shape[1]
    after_gain = kept + gain.shape[0]
    after_bias = after_gain + bias.shape[0]
    lives = jnp.sum(all_small[...].astype(jnp.float32), axis=0)[0:1, after_bias : after_bias + 1]
    scale = 1.0 / (lives * num_tokens)
    norm = jnp.sqrt(total) * scale
    norm_o[...] = norm
    clip = jnp.minimum(1.0, 1.0 / (norm + 1e-06))

    def update(group, state, outs, where, gradient):
        news = adamw_update(
            *(ref[where] for ref in state), gradient * scale, clip, RATES[group], DECAYS[group]
        )
        for ref, new in zip(outs, news):
            ref[where] = new

    def update_in(k, carry):
        where = (slice(None), pl.ds(pl.multiple_of(k * D, D), D))
        update(0, (wi, wi_m, wi_v), (wi_o, wi_m_o, wi_v_o, wi_low), where, fi[where])
        return carry

    lax.fori_loop(0, fi.shape[1] // D, update_in, 0)

    def update_out(k, carry):
        where = (pl.ds(pl.multiple_of(k * 16, 16), 16), slice(None))
        update(1, (wo, wo_m, wo_v), (wo_o, wo_m_o, wo_v_o, wo_low), where, fo[where])
        return carry

    lax.fori_loop(0, fo.shape[0] // 16, update_out, 0)
    own = kern.shape[0]
    turned = square_of(fs[...]).T
    update(2, (kern, kern_m, kern_v), (kern_o, kern_m_o, kern_v_o, kern_low), ..., fs[:, 0:kept])
    update(
        3, (gain, gain_m, gain_v), (gain_o, gain_m_o, gain_v_o, gain_low), ...,
        turned[kept:after_gain, 0:own],
    )
    update(
        4, (bias, bias_m, bias_v), (bias_o, bias_m_o, bias_v_o, bias_low), ...,
        turned[after_gain:after_bias, 0:own],
    )


def update_all(sums, all_small, state, num_tokens):
    low, full = jnp.bfloat16, jnp.float32
    vmem = pl.BlockSpec(memory_space=pltpu.VMEM)
    return pl.pallas_call(
        functools.partial(update_kernel, float(num_tokens)),
        out_shape=(jax.ShapeDtypeStruct((1, 1), full),)
        + tuple(
            jax.ShapeDtypeStruct(master.shape, kind)
            for master in state[::3]
            for kind in (full, full, full, low)
        ),
        in_specs=[vmem] * 20,
        out_specs=(vmem,) * 21,
        compiler_params=pltpu.CompilerParams(vmem_limit_bytes=32 << 20),
        name="update_all",
    )(*sums, all_small, *state)


def cross_rows(left, right):
    return lax.dot_general(
        left, right, (((0,), (0,)), ((), ())), preferred_element_type=jnp.float32
    )


SIDE = 8
TALL = 512
CHUNK = 10
GAIN_ROW = 58
BIAS_ROW = 60


def tokens_of(value):
    return value.reshape(-1, SIDE, value.shape[-1])


def column_partial(value):
    return jnp.sum(tokens_of(value), axis=0)


def dot(left, right):
    return jnp.dot(left, right, preferred_element_type=jnp.float32)


def dot_nt(left, right):
    return lax.dot_general(
        left, right, (((1,), (1,)), ((), ())), preferred_element_type=jnp.float32
    )


def dot_tn(left, right):
    return lax.dot_general(
        left, right, (((0,), (0,)), ((), ())), preferred_element_type=jnp.float32
    )


def lane_tile(j):
    if isinstance(j, int):
        return pl.ds(j * 128, 128)
    return pl.ds(pl.multiple_of(j * 128, 128), 128)


def grid_rows(row, col):
    return pl.ds((1 + row * GRID + col) * SIDE, SIDE)


CLASS_ROWS = pl.ds(0, SIDE)


def put(grid, at, value):
    for j in range(D // 128):
        grid[j, at, :] = value[:, j * 128 : j * 128 + 128]


def get(grid, at, tiles=(0, 1, 2, 3)):
    return jnp.concatenate([grid[j, at, :] for j in tiles], axis=1)


def conv_tile(src, taps, base, width, reach, j, finish, flip=False):
    lanes = lane_tile(j)
    margin = width // 2
    offsets = range(-reach, reach + 1)

    def tap(dy, dx):
        if flip:
            dy, dx = -dy, -dx
        index = base + (dy + margin) * width + dx + margin
        return jnp.broadcast_to(taps[index : index + 1, lanes], (SIDE, 128))

    held = {(dy, dx): tap(dy, dx) for dy in offsets for dx in offsets}
    for row in range(GRID):
        sums = [jnp.zeros((SIDE, 128), jnp.float32) for _ in range(GRID)]
        for dy in offsets:
            if not 0 <= row + dy < GRID:
                continue
            line = [src[j, grid_rows(row + dy, col), :] for col in range(GRID)]
            for dx in offsets:
                for col in range(GRID):
                    if 0 <= col + dx < GRID:
                        sums[col] = sums[col] + line[col + dx] * held[dy, dx]
        for col in range(GRID):
            finish(grid_rows(row, col), sums[col])


def tap_sums(grad, src, base, width, reach, j, total):
    lanes = lane_tile(j)
    margin = width // 2
    offsets = range(-reach, reach + 1)
    for dy in offsets:
        sums = {dx: jnp.zeros((SIDE, 128), jnp.float32) for dx in offsets}
        for row in range(GRID):
            if not 0 <= row + dy < GRID:
                continue
            up = [grad[j, grid_rows(row, col), :] for col in range(GRID)]
            line = [src[j, grid_rows(row + dy, col), :] for col in range(GRID)]
            for dx in offsets:
                for col in range(GRID):
                    if 0 <= col + dx < GRID:
                        sums[dx] = sums[dx] + up[col] * line[col + dx]
        for dx in offsets:
            index = base + (dy + margin) * width + dx + margin
            total[index, :, lanes] = total[index, :, lanes] + sums[dx]


def mask_far_taps(rows):
    lanes = pl.ds(256, 128)
    keep = (lax.broadcasted_iota(jnp.int32, (1, 128), 1) >= 64).astype(jnp.float32)
    for tap in range(49):
        if max(abs(tap // 7 - 3), abs(tap % 7 - 3)) == 3:
            line = pl.ds(9 + tap, 1)
            rows[line, lanes] = rows[line, lanes] * keep


def relative_tiles(body):
    body(0, 1)
    body(1, 2)

    def rest(j, carry):
        body(j, 3)
        return carry

    lax.fori_loop(2, 4, rest, 0)


def all_tiles(body):
    def step(j, carry):
        body(j)
        return carry

    lax.fori_loop(0, 4, step, 0)


def all_chunks(body):
    def step(k, carry):
        body(pl.ds(pl.multiple_of(k * CHUNK * SIDE, 16), CHUNK * SIDE))
        return carry

    lax.fori_loop(0, 50 // CHUNK, step, 0)


def normalise(values):
    centred = values - jnp.mean(values, axis=-1, keepdims=True)
    scale = lax.rsqrt(jnp.mean(centred * centred, axis=-1, keepdims=True) + NORM_EPS)
    return centred * scale, scale


def norm_back(grad, hat, scale, gain):
    inner = grad * gain
    mean = jnp.mean(inner, axis=-1, keepdims=True)
    along = jnp.mean(inner * hat, axis=-1, keepdims=True)
    return scale * (inner - mean - hat * along)


def spread_images(src, grid, first, limit):
    for i in range(SIDE):
        image = src[i]
        keep = jnp.full(image.shape, first + i, jnp.int32) < limit
        at = pl.ds(i, image.shape[0], stride=SIDE)
        put(grid, at, jnp.where(keep, image.astype(jnp.float32), 0.0))


def set_parameters(small, par, heads):
    par[...] = small[...].astype(jnp.float32).T
    mask_far_taps(par)
    row_head = lax.broadcasted_iota(jnp.int32, heads.shape, 0) // 64
    col_head = lax.broadcasted_iota(jnp.int32, heads.shape, 1) // 64
    heads[...] = jnp.where(row_head == col_head, 1.0, 0.0).astype(heads.dtype)


def every_image(body):
    for i in range(SIDE):
        for half in range(2):
            body(pl.ds(i, TALL // SIDE, stride=SIDE), (2 * half, 2 * half + 1))


def forward_kernel(
    num_images, rows, counts, x_in, dy_in, w_in, w_out, small,
    out, act_o, gh_o, n1_o, n2_o, at_o, gf_o, gp_o, gx_o, xt_o, hat_o, sc_o, q_o, k_o, v_o, cv_o,
    cols_o, hcols_o,
    par, heads, x, x1, v, q, k, conv, hat2, slope, gn, scale2,
):
    low = jnp.bfloat16
    step = pl.program_id(0)
    first = step * SIDE
    live = pl.ds(0, rows)

    @pl.when(step == 0)
    def _():
        set_parameters(small, par, heads)
        for grid in (q, k, v):
            grid[...] = jnp.zeros_like(grid)
        cols_o[...] = jnp.zeros_like(cols_o)
        hcols_o[...] = jnp.zeros_like(hcols_o)

    def bias(row):
        return par[BIAS_ROW + row : BIAS_ROW + row + 1, :]

    def gain(row):
        return par[GAIN_ROW + row : GAIN_ROW + row + 1, :]

    spread_images(x_in, x, first, num_images)
    xt_o[...] = get(x, live).astype(low)
    spread_images(dy_in, gn, first, jnp.minimum(counts[0], num_images))
    gf_o[...] = get(gn, live).astype(low)

    def position(j):
        lanes = lane_tile(j)
        shift = jnp.broadcast_to(par[BIAS_ROW + 10 : BIAS_ROW + 11, lanes], (SIDE, 128))

        def finish(at, total):
            x1[j, at, :] = x[j, at, :] + total + shift

        conv_tile(x, par, 0, 3, 1, j, finish)
        x1[j, CLASS_ROWS, :] = x[j, CLASS_ROWS, :]

    all_tiles(position)

    def first_norm(at):
        hat, scale = normalise(get(x1, at))
        hat_o[at, :] = hat.astype(low)
        sc_o[at, :] = jnp.broadcast_to(scale, (CHUNK * SIDE, 128))
        n1_o[at, :] = (hat * gain(0) + bias(0)).astype(low)

    all_chunks(first_norm)
    n1 = n1_o[...]
    put(gn, live, dot(n1, w_in[:, D : 2 * D]))

    def weights(j):
        lanes = lane_tile(j)
        keys = tokens_of(gn[j, live, :])
        powers = jnp.exp(keys - jnp.max(keys, axis=0, keepdims=True))
        share = 0.125 / jnp.sum(powers, axis=0, keepdims=True)
        value = (powers * share).reshape(-1, 128)
        k[j, live, :] = value
        k_o[:, lanes] = value.astype(low)

    all_tiles(weights)
    value = dot(n1, w_in[:, 2 * D : 3 * D]) + bias(3)
    put(v, live, value)
    v_o[...] = value.astype(low)

    def relative(j, reach):
        lanes = lane_tile(j)
        shift = jnp.broadcast_to(par[BIAS_ROW + 11 : BIAS_ROW + 12, lanes], (SIDE, 128))

        def finish(at, total):
            conv[j, at, :] = total + shift

        conv_tile(v, par, 9, 7, reach, j, finish)
        conv[j, CLASS_ROWS, :] = jnp.zeros((SIDE, 128), jnp.float32)

    relative_tiles(relative)
    cv_o[...] = get(conv, live).astype(low)
    value = dot(n1, w_in[:, :D]) + bias(2)
    q_o[...] = value.astype(low)
    put(q, live, value)

    def attention(at, tiles):
        context = dot_tn(get(k, at, tiles).astype(low), get(v, at, tiles).astype(low))
        context = context.astype(low) * heads[...]
        value = dot(get(q, at, tiles).astype(low), context)
        for n, j in enumerate(tiles):
            gn[j, at, :] = value[:, n * 128 : n * 128 + 128]

    every_image(attention)
    for j in range(D // 128):
        at_o[:, lane_tile(j)] = (gn[j, live, :] + conv[j, live, :] * q[j, live, :]).astype(low)
    put(x1, live, get(x1, live) + (dot(at_o[...], w_in[:, 3 * D : 4 * D]) + bias(4)))

    def second_norm(at):
        hat, scale = normalise(get(x1, at))
        hat2[at, :] = hat
        scale2[at, :] = jnp.broadcast_to(scale, (CHUNK * SIDE, 128))
        n2_o[at, :] = (hat * gain(1) + bias(1)).astype(low)

    all_chunks(second_norm)
    n2 = n2_o[...]
    for part in range(MLP_WIDTH // D):
        cols = pl.ds(part * D, D)
        put(gn, live, dot(n2, w_in[:, pl.ds((4 + part) * D, D)]))

        def gelu(at):
            h = get(gn, at) + bias(5 + part)
            below = 0.5 + 0.5 * lax.erf(h * (0.5**0.5))
            density = jnp.exp(-0.5 * h * h) * 0.3989422804014327
            act_o[at, cols] = (h * below).astype(low)
            slope[at, cols] = below + h * density

        all_chunks(gelu)
    put(x1, live, get(x1, live) + dot(act_o[...], w_out[...]) + bias(9))
    for i in range(SIDE):
        out[i] = get(x1, pl.ds(i, out.shape[1], stride=SIDE)).astype(low)

    gf = gf_o[...]
    for part in range(MLP_WIDTH // D):
        cols = pl.ds(part * D, D)
        grad = (dot_nt(gf, w_out[cols, :]) * slope[:, cols]).astype(low)
        gh_o[:, cols] = grad
        hcols_o[:, cols] = hcols_o[:, cols] + column_partial(grad.astype(jnp.float32))
    put(gn, live, dot_nt(gh_o[...], w_in[:, 4 * D :]))

    def second_back(at):
        grad = get(gn, at)
        hat = hat2[at, :]
        scale = scale2[at, 0:1]
        upstream = gf_o[at, :].astype(jnp.float32)
        total = upstream + norm_back(grad, hat, scale, gain(1))
        gx_o[at, :] = total
        rounded = total.astype(low)
        gp_o[at, :] = rounded
        cols_o[0] = cols_o[0] + column_partial(grad)
        cols_o[1] = cols_o[1] + column_partial(grad * hat)
        cols_o[2] = cols_o[2] + column_partial(rounded.astype(jnp.float32))
        cols_o[3] = cols_o[3] + column_partial(upstream)

    all_chunks(second_back)


def backward_kernel(
    rows, w_in, small, cols_in, hcols_in, gx, hat, sc, q_in, k_in, v_in, cv, xt,
    out, gq_o, small_o,
    par, heads, cols, taps, lines, g, gc, q, k, v, gq, gk, gv, x, g1,
):
    low = jnp.bfloat16
    step = pl.program_id(0)
    live = pl.ds(0, rows)

    @pl.when(step == 0)
    def _():
        set_parameters(small, par, heads)
        for grid in (g, q, k, v, gq, gk, gv):
            grid[...] = jnp.zeros_like(grid)
        cols[...] = jnp.zeros_like(cols)
        taps[...] = jnp.zeros_like(taps)

    grad = dot_nt(gx[...].astype(low), w_in[:, 3 * D : 4 * D])
    put(g, live, grad)
    for j in range(D // 128):
        lanes = lane_tile(j)
        part = g[j, live, :]
        queries = q_in[:, lanes].astype(jnp.float32)
        q[j, live, :] = queries
        k[j, live, :] = k_in[:, lanes].astype(jnp.float32)
        v[j, live, :] = v_in[:, lanes].astype(jnp.float32)
        x[j, live, :] = xt[:, lanes].astype(jnp.float32)
        gq[j, live, :] = part * cv[:, lanes].astype(jnp.float32)
        gc[j, live, :] = part * queries
        gc[j, CLASS_ROWS, :] = jnp.zeros((SIDE, 128), jnp.float32)
        cols[0, :, lanes] = cols[0, :, lanes] + column_partial(gc[j, live, :])

    def relative(j, reach):
        def finish(at, total):
            gv[j, at, :] = total

        conv_tile(gc, par, 9, 7, reach, j, finish, flip=True)
        gv[j, CLASS_ROWS, :] = jnp.zeros((SIDE, 128), jnp.float32)
        tap_sums(gc, v, 9, 7, reach, j, taps)

    relative_tiles(relative)

    def attention(at, tiles):
        qs, ks, vs, gs = (get(grid, at, tiles).astype(low) for grid in (q, k, v, g))
        context = dot_tn(ks, vs).astype(low) * heads[...]
        grads = dot_tn(qs, gs).astype(low) * heads[...]
        to_q, to_k, to_v = dot_nt(gs, context), dot_nt(vs, grads), dot(ks, grads)
        for n, j in enumerate(tiles):
            here = slice(n * 128, n * 128 + 128)
            gq[j, at, :] = gq[j, at, :] + to_q[:, here]
            gk[j, at, :] = to_k[:, here]
            gv[j, at, :] = gv[j, at, :] + to_v[:, here]

    every_image(attention)

    def finish_qkv(j):
        lanes = lane_tile(j)
        share = tokens_of(k[j, live, :])
        up = tokens_of(gk[j, live, :])
        along = jnp.sum(share * up, axis=0, keepdims=True) * 8.0
        gq_o[:, pl.ds(pl.multiple_of(D + j * 128, 128), 128)] = (
            (share * (up - along)).reshape(-1, 128).astype(low)
        )
        part = gq[j, live, :].astype(low)
        gq_o[:, lanes] = part
        cols[1, :, lanes] = cols[1, :, lanes] + column_partial(part.astype(jnp.float32))
        part = gv[j, live, :].astype(low)
        gq_o[:, pl.ds(pl.multiple_of(2 * D + j * 128, 128), 128)] = part
        cols[2, :, lanes] = cols[2, :, lanes] + column_partial(part.astype(jnp.float32))

    all_tiles(finish_qkv)
    put(gk, live, dot_nt(gq_o[...], w_in[:, : 3 * D]))

    def first_back(at):
        grad = get(gk, at)
        hats = hat[at, :].astype(jnp.float32)
        total = gx[at, :] + norm_back(grad, hats, sc[at, 0:1], par[GAIN_ROW : GAIN_ROW + 1, :])
        put(g1, at, total)
        cols[3] = cols[3] + column_partial(grad)
        cols[4] = cols[4] + column_partial(grad * hats)
        cols[5] = cols[5] + column_partial(total)

    all_chunks(first_back)
    cols[5] = cols[5] - get(g1, CLASS_ROWS)

    def position(j):
        def finish(at, total):
            gv[j, at, :] = g1[j, at, :] + total

        conv_tile(g1, par, 0, 3, 1, j, finish, flip=True)
        gv[j, CLASS_ROWS, :] = g1[j, CLASS_ROWS, :]
        tap_sums(g1, x, 0, 3, 1, j, taps)

    all_tiles(position)
    for i in range(SIDE):
        out[i] = get(gv, pl.ds(i, out.shape[1], stride=SIDE))

    @pl.when(step == pl.num_programs(0) - 1)
    def _():
        lines[...] = jnp.zeros_like(lines)
        for tap in range(taps.shape[0]):
            lines[tap : tap + 1, :] = jnp.sum(taps[tap], axis=0, keepdims=True)
        mask_far_taps(lines)
        hidden = [hcols_in[:, i * D : i * D + D] for i in range(MLP_WIDTH // D)]
        order = [cols[4], cols_in[1], cols[3], cols_in[0], cols[1], cols[2], cols_in[2]]
        for i, part in enumerate(order + hidden + [cols_in[3], cols[5], cols[0]]):
            row = GAIN_ROW + i
            lines[row : row + 1, :] = jnp.sum(part, axis=0, keepdims=True)
        small_o[...] = lines[...].T


def fixed(shape):
    zeros = (0,) * len(shape)
    return pl.BlockSpec(shape, lambda g: zeros, pipeline_mode=pl.Buffered(1))


def compute(images, cotangent, counts, w_in, w_out, small):
    low, full = jnp.bfloat16, jnp.float32
    num_images, num_tokens, channels = images.shape
    groups = -(-num_images // SIDE)
    rows = num_tokens * SIDE
    total = groups * rows

    def block(cols):
        return pl.BlockSpec((rows, cols), lambda g: (g, 0))

    def image_block():
        return pl.BlockSpec((SIDE, num_tokens, channels), lambda g: (g, 0, 0))

    def made(cols, kind=low):
        return jax.ShapeDtypeStruct((total, cols), kind)

    def grid():
        return pltpu.VMEM((channels // 128, TALL, 128), full)

    shared = [pltpu.VMEM((128, channels), full), pltpu.VMEM((256, 256), low)]
    wide = w_out.shape[0]
    forward = pl.pallas_call(
        functools.partial(forward_kernel, num_images, rows),
        grid=(groups,),
        in_specs=[
            pl.BlockSpec(memory_space=pltpu.SMEM),
            image_block(),
            image_block(),
            fixed(w_in.shape),
            fixed(w_out.shape),
            fixed(small.shape),
        ],
        out_specs=[image_block(), block(wide), block(wide)]
        + [block(channels)] * 8
        + [block(128)]
        + [block(channels)] * 4
        + [fixed((4, SIDE, channels)), fixed((SIDE, wide))],
        out_shape=[jax.ShapeDtypeStruct(images.shape, low), made(wide), made(wide)]
        + [made(channels)] * 5
        + [made(channels, full), made(channels), made(channels), made(128, full)]
        + [made(channels)] * 4
        + [
            jax.ShapeDtypeStruct((4, SIDE, channels), full),
            jax.ShapeDtypeStruct((SIDE, wide), full),
        ],
        scratch_shapes=shared
        + [grid() for _ in range(6)]
        + [pltpu.VMEM((rows, channels), full), pltpu.VMEM((rows, wide), full), grid(), pltpu.VMEM((rows, 128), full)],
        compiler_params=pltpu.CompilerParams(vmem_limit_bytes=60 << 20),
        name="forward",
    )
    (
        out, act, gh, n1, n2, attended, gf, gp, gx, xt, hat, scale, q, k, v, cv, cols, hcols,
    ) = forward(counts, images, cotangent, w_in, w_out, small)

    backward = pl.pallas_call(
        functools.partial(backward_kernel, rows),
        grid=(groups,),
        in_specs=[
            pl.BlockSpec(
                (channels, 4 * channels), lambda g: (0, 0), pipeline_mode=pl.Buffered(1)
            ),
            fixed(small.shape),
            fixed(cols.shape),
            fixed(hcols.shape),
            block(channels),
            block(channels),
            block(128),
        ]
        + [block(channels)] * 5,
        out_specs=[image_block(), block(3 * channels), fixed(small.shape)],
        out_shape=[
            jax.ShapeDtypeStruct(images.shape, full),
            made(3 * channels),
            jax.ShapeDtypeStruct(small.shape, full),
        ],
        scratch_shapes=shared
        + [
            pltpu.VMEM((6, SIDE, channels), full),
            pltpu.VMEM((GAIN_ROW, SIDE, channels), full),
            pltpu.VMEM((128, channels), full),
        ]
        + [grid() for _ in range(10)],
        compiler_params=pltpu.CompilerParams(vmem_limit_bytes=60 << 20),
        name="backward",
    )
    input_grad, gq, grad_small = backward(
        w_in, small, cols, hcols, gx, hat, scale, q, k, v, cv, xt
    )
    return out, input_grad, (n1, gq, attended, gp, n2, gh, act, gf), grad_small


def adamw_update(master, first_moment, second_moment, gradient, clip_factor, rate, decay):
    clipped = gradient * clip_factor
    first_new = BETA_ONE * first_moment + (1.0 - BETA_ONE) * clipped
    second_new = BETA_TWO * second_moment + (1.0 - BETA_TWO) * clipped * clipped
    first_hat = first_new / (1.0 - BETA_ONE**STEP)
    second_hat = second_new / (1.0 - BETA_TWO**STEP)
    master_new = master - rate * (first_hat / (jnp.sqrt(second_hat) + ADAM_EPS) + decay * master)
    return (master_new, first_new, second_new, master_new.astype(jnp.bfloat16))


def local(
    images,
    cotangent,
    counts,
    in_mats,
    in_mats_m,
    in_mats_v,
    out_mat,
    out_mat_m,
    out_mat_v,
    kernels,
    kernels_m,
    kernels_v,
    gains,
    gains_m,
    gains_v,
    biases,
    biases_m,
    biases_v,
    special,
):
    if special:
        all_in, all_out, all_small = gather_all(counts, in_mats, out_mat, kernels.T, gains, biases)
        block_out, input_grad, factors, grad_small = compute(
            images,
            cotangent,
            counts,
            all_in.reshape(-1, in_mats.shape[1]),
            all_out.reshape(-1, out_mat.shape[1]),
            all_small.reshape(-1, 128),
        )
        sums = reduce_all(*factors, grad_small)
        state = (
            in_mats, in_mats_m, in_mats_v,
            out_mat, out_mat_m, out_mat_v,
            kernels.T, kernels_m.T, kernels_v.T,
            gains, gains_m, gains_v,
            biases, biases_m, biases_v,
        )
        norm, *news = update_all(sums, all_small, state, images.shape[1])
        news[8:12] = [part.T for part in news[8:12]]
        return (block_out, input_grad, norm.reshape(()), *news)
    in_copy = in_mats.astype(jnp.bfloat16)
    out_copy = out_mat.astype(jnp.bfloat16)
    shards = (kernels, gains, biases)
    sizes = [shard.shape[0] for shard in shards]
    used = sum(sizes)
    count_row = jnp.broadcast_to(counts.astype(jnp.float32)[:, None], (1, kernels.shape[1]))
    rows = jnp.concatenate(shards + (count_row,), axis=0)
    small = jnp.pad(rows, ((0, 128 - used - 1), (0, 0))).T.astype(jnp.bfloat16)
    all_in, all_out, all_small = (
        lax.all_gather(part, ("wide", "narrow"), axis=0, tiled=True)
        for part in (in_copy, out_copy, small)
    )
    all_small = all_small.reshape(-1, small.shape[0], 128)
    live_total = jnp.sum(all_small[:, 0, used].astype(jnp.float32)) * images.shape[1]
    scale_factor = 1.0 / live_total
    block_out, input_grad, factors, grad_small = compute(
        images,
        cotangent,
        counts,
        all_in.reshape(-1, in_copy.shape[1]),
        all_out.reshape(-1, out_copy.shape[1]),
        all_small.reshape(-1, 128),
    )
    n1, gq, attended, gp, n2, gh, act, gf = factors
    grad_in = jnp.concatenate(
        [cross_rows(n1, gq), cross_rows(attended, gp), cross_rows(n2, gh)], axis=1
    )
    grad_fc2 = cross_rows(act, gf)
    sum_in, sum_out, sum_small = (
        lax.psum_scatter(part, ("wide", "narrow"), scatter_dimension=0, tiled=True)
        for part in (grad_in, grad_fc2, grad_small)
    )
    total_squares = lax.psum(
        sum(jnp.sum(part * part) for part in (sum_in, sum_out, sum_small)), ("wide", "narrow")
    )
    rows = sum_small.T
    summed = (
        sum_in,
        sum_out,
        rows[: sizes[0]],
        rows[sizes[0] : sizes[0] + sizes[1]],
        rows[sizes[0] + sizes[1] : used],
    )
    summed = tuple(part * scale_factor for part in summed)
    grad_norm = jnp.sqrt(total_squares) * scale_factor
    clip_factor = jnp.minimum(1.0, 1.0 / (grad_norm + 1e-06))
    in_new = adamw_update(
        in_mats, in_mats_m, in_mats_v, summed[0], clip_factor, RATES[0], DECAYS[0]
    )
    out_new = adamw_update(
        out_mat, out_mat_m, out_mat_v, summed[1], clip_factor, RATES[1], DECAYS[1]
    )
    kern_new = adamw_update(
        kernels, kernels_m, kernels_v, summed[2], clip_factor, RATES[2], DECAYS[2]
    )
    gain_new = adamw_update(gains, gains_m, gains_v, summed[3], clip_factor, RATES[3], DECAYS[3])
    bias_new = adamw_update(biases, biases_m, biases_v, summed[4], clip_factor, RATES[4], DECAYS[4])
    return (
        block_out,
        input_grad,
        grad_norm,
        in_new[0],
        in_new[1],
        in_new[2],
        in_new[3],
        out_new[0],
        out_new[1],
        out_new[2],
        out_new[3],
        kern_new[0],
        kern_new[1],
        kern_new[2],
        kern_new[3],
        gain_new[0],
        gain_new[1],
        gain_new[2],
        gain_new[3],
        bias_new[0],
        bias_new[1],
        bias_new[2],
        bias_new[3],
    )


def solution(mesh):
    placed = (
        P(("wide", "narrow"), None, None),
        P(("wide", "narrow"), None, None),
        P(("wide", "narrow")),
        P(("wide", "narrow"), None),
        P(("wide", "narrow"), None),
        P(("wide", "narrow"), None),
        P(("wide", "narrow"), None),
        P(("wide", "narrow"), None),
        P(("wide", "narrow"), None),
        P(None, ("wide", "narrow")),
        P(None, ("wide", "narrow")),
        P(None, ("wide", "narrow")),
        P(None, ("wide", "narrow")),
        P(None, ("wide", "narrow")),
        P(None, ("wide", "narrow")),
        P(None, ("wide", "narrow")),
        P(None, ("wide", "narrow")),
        P(None, ("wide", "narrow")),
    )
    special = dict(mesh.shape) == {"wide": 8, "narrow": 4}
    return jax.shard_map(
        functools.partial(local, special=special),
        mesh=mesh,
        in_specs=placed,
        out_specs=(
            P(("wide", "narrow"), None, None),
            P(("wide", "narrow"), None, None),
            P(),
            P(("wide", "narrow"), None),
            P(("wide", "narrow"), None),
            P(("wide", "narrow"), None),
            P(("wide", "narrow"), None),
            P(("wide", "narrow"), None),
            P(("wide", "narrow"), None),
            P(("wide", "narrow"), None),
            P(("wide", "narrow"), None),
            P(None, ("wide", "narrow")),
            P(None, ("wide", "narrow")),
            P(None, ("wide", "narrow")),
            P(None, ("wide", "narrow")),
            P(None, ("wide", "narrow")),
            P(None, ("wide", "narrow")),
            P(None, ("wide", "narrow")),
            P(None, ("wide", "narrow")),
            P(None, ("wide", "narrow")),
            P(None, ("wide", "narrow")),
            P(None, ("wide", "narrow")),
            P(None, ("wide", "narrow")),
        ),
        check_vma=False,
    )
```

```python
import functools

import jax
import jax.numpy as jnp
from jax import lax
from jax.experimental import pallas as pl
from jax.experimental.pallas import tpu as pltpu
from jax.sharding import PartitionSpec as P

D = 512
HEADS = 8
MLP_WIDTH = 2048
GRID = 7
STEP = 10
BROWS = 12


NORM_EPS = 1e-06
BETA_ONE = 0.9
BETA_TWO = 0.999
ADAM_EPS = 1e-08
HIGHEST = lax.Precision.HIGHEST
RATES = (0.04, 0.02, 0.1, 0.8, 0.25)
DECAYS = (0.05, 0.05, 0.05, 0.0, 0.0)


MESH_ID = pl.DeviceIdType.MESH
SPLIT = 3072
SMALL_ROWS = 16


def place():
    w = lax.axis_index("wide")
    n = lax.axis_index("narrow")
    return w // 2, w % 2, n // 2, n % 2


def device(z, y, x, c):
    return (z * 2 + y, x * 2 + c)


def neighbour(at, axis, step=1):
    z, y, x, c = at
    if axis == 0:
        return (lax.rem(z + step, 4), y, x, c)
    if axis == 1:
        return (z, 1 - y, x, c)
    if axis == 2:
        return (z, y, 1 - x, c)
    return (z, y, x, 1 - c)


def square_of(lines):
    return jnp.concatenate([lines, jnp.zeros((128 - lines.shape[0], 128), lines.dtype)], axis=0)


def gather_kernel(
    counts, wi_f, wo_f, kern, gain, bias, gi, go, gs, wi, wo, sm, lines, send_sem, recv_sem, own_sem
):
    at = place()
    z, y, x, c = at
    partners = [device(*neighbour(at, 0, s)) for s in (1, 2, 3)]
    partners += [device(*neighbour(at, a)) for a in (1, 2, 3)]
    barrier = pltpu.get_barrier_semaphore()
    for partner in partners:
        pl.semaphore_signal(barrier, inc=1, device_id=partner, device_id_type=MESH_ID)
    low = jnp.bfloat16
    wi[...] = wi_f[...].astype(low)
    wo[...] = wo_f[...].astype(low)
    kept, own = kern.shape[1], kern.shape[0]
    after_gain = kept + gain.shape[0]
    after_bias = after_gain + bias.shape[0]
    lines[...] = jnp.zeros_like(lines)
    lines[kept:after_gain, 0:own] = gain[...]
    lines[after_gain:after_bias, 0:own] = bias[...]
    lines[after_bias : after_bias + 1, :] = jnp.full((1, 128), counts[0], jnp.int32).astype(
        jnp.float32
    )
    turned = lines[...].T[0:own, :]
    lines[0:own, :] = turned
    lines[0:own, 0:kept] = kern[...]
    sm[...] = lines[0:own, :].astype(low)
    pl.semaphore_wait(barrier, len(partners))

    width = wi.shape[1]
    pieces = (
        (wi, gi, 0, pl.ds(0, SPLIT)),
        (sm, gs, 0, pl.ds(0, 128)),
        (wi, gi, 1, pl.ds(SPLIT, width - SPLIT)),
        (wo, go, 1, pl.ds(0, wo.shape[1])),
    )
    orders = ((0, 1, 2, 3), (0, 2, 1, 3))

    def slot(r):
        zs = lax.rem(z - r[0] + 4, 4)
        ys = 1 - y if r[1] else y
        xs = 1 - x if r[2] else x
        cs = 1 - c if r[3] else c
        return ((zs * 2 + ys) * 2 + xs) * 2 + cs

    def flat(r):
        return ((r[0] * 2 + r[1]) * 2 + r[2]) * 2 + r[3]

    def moved(r, axis, step):
        r = list(r)
        r[axis] = step
        return tuple(r)

    def transfer(p, r, axis, step):
        own, out, color, cols = pieces[p]
        there = out.at[slot(r), :, cols]
        here = own.at[:, cols] if r == (0, 0, 0, 0) else there
        to = moved(r, axis, step)
        return pltpu.make_async_remote_copy(
            src_ref=here,
            dst_ref=there,
            send_sem=send_sem.at[p, flat(to)],
            recv_sem=recv_sem.at[p, flat(to)],
            device_id=device(*neighbour(at, axis, step)),
            device_id_type=MESH_ID,
        )

    def onward(p, r):
        order = orders[pieces[p][2]]
        last = max([i for i in range(4) if r[order[i]]], default=-1)
        for i in range(last + 1, 4):
            axis = order[i]
            for step in (1, 2, 3) if axis == 0 else (1,):
                yield axis, step

    started = []

    def forward(p, r):
        for axis, step in onward(p, r):
            copy = transfer(p, r, axis, step)
            copy.start()
            started.append(copy)

    zero = (0, 0, 0, 0)
    for p in range(4):
        forward(p, zero)
    own_copies = []
    for p in range(4):
        own, out, color, cols = pieces[p]
        copy = pltpu.make_async_copy(
            own.at[:, cols], out.at[slot(zero), :, cols], own_sem.at[p]
        )
        copy.start()
        own_copies.append(copy)

    def arrival(p, r):
        order = orders[pieces[p][2]]
        axis = [a for a in order if r[a]][-1]
        back = moved(r, axis, 0)
        return transfer(p, back, axis, r[axis])

    offsets = [
        (dz, dy, dx, dc) for dz in range(4) for dy in range(2) for dx in range(2) for dc in range(2)
    ]
    cost = {0: 0, 1: 2, 2: 4, 3: 2}

    def when(r):
        return cost[r[0]] + r[1] * 2 + r[2] * 2 + r[3]

    for r in sorted(offsets[1:], key=when):
        for p in range(4):
            copy = arrival(p, r)
            copy.wait_recv()
            forward(p, r)
    for copy in started:
        copy.wait_send()
    for copy in own_copies:
        copy.wait()


def gather_all(counts, in_mats, out_mat, kern, gain, bias):
    low = jnp.bfloat16
    hbm = pl.BlockSpec(memory_space=pl.ANY)
    vmem = pl.BlockSpec(memory_space=pltpu.VMEM)
    shapes = (in_mats.shape, out_mat.shape, (SMALL_ROWS, 128))
    return pl.pallas_call(
        gather_kernel,
        out_shape=tuple(jax.ShapeDtypeStruct((32,) + shape, low) for shape in shapes),
        in_specs=[pl.BlockSpec(memory_space=pltpu.SMEM)] + [vmem] * 5,
        out_specs=(hbm,) * 3,
        scratch_shapes=[pltpu.VMEM(shape, low) for shape in shapes]
        + [
            pltpu.VMEM((128, 128), jnp.float32),
            pltpu.SemaphoreType.DMA((4, 32)),
            pltpu.SemaphoreType.DMA((4, 32)),
            pltpu.SemaphoreType.DMA((4,)),
        ],
        compiler_params=pltpu.CompilerParams(collective_id=0, has_side_effects=True),
        name="gather_all",
    )(counts, in_mats, out_mat, kern, gain, bias)


def add_low(left, right):
    return (left.astype(jnp.float32) + right.astype(jnp.float32)).astype(left.dtype)


IN_CHUNKS = 4
OUT_CHUNKS = 2
LAGS = (2, 4, 6, 8)


def reduce_kernel(
    n1_h, gq_h, at_h, gp_h, n2_h, gh_h, act_h, gf_h, gs, fi, fo, fs, fq,
    n1, gq, at_v, gp, n2, gh, act, gf,
    gi, go, r0i, r0o, r0s, r1i, r1o, r1s, r2i, r2o, r2s, r3i, r3o, r3s,
    squares_narrow, squares_wide, load_sem, send_sem, recv_sem, norm_send, norm_recv,
):
    at = place()
    z, y, x, c = at
    w = z * 2 + y
    n = x * 2 + c
    loads = []
    half = gh.shape[1] // 2
    for src, dst, cols in (
        (n2_h, n2, None),
        (gh_h, gh, pl.ds(0, half)),
        (gh_h, gh, pl.ds(half, half)),
        (gf_h, gf, None),
        (act_h, act, None),
        (n1_h, n1, None),
        (gq_h, gq, None),
        (at_h, at_v, None),
        (gp_h, gp, None),
    ):
        real, padded = src.shape[0], dst.shape[0]
        if cols is None:
            cols = pl.ds(0, src.shape[1])
        if padded > real:
            dst[pl.ds(real, padded - real), cols] = jnp.zeros(
                (padded - real, cols.size), dst.dtype
            )
        src, dst = src.at[:, cols], dst.at[pl.ds(0, real), cols]
        copy = pltpu.make_async_copy(src, dst, load_sem.at[len(loads)])
        copy.start()
        loads.append(copy)
    waited = [0]

    def loaded(upto):
        while waited[0] < upto:
            loads[waited[0]].wait()
            waited[0] += 1

    partners = [(w, lax.rem(n + s, 4)) for s in (1, 2, 3)]
    partners += [(lax.rem(w + s, 8), n) for s in range(1, 8)]
    barrier = pltpu.get_barrier_semaphore()
    for partner in partners:
        pl.semaphore_signal(barrier, inc=1, device_id=partner, device_id_type=MESH_ID)

    count = [0]
    sent = []

    def send(src, dst, axis, step=1):
        index = count[0]
        count[0] += 1
        copy = pltpu.make_async_remote_copy(
            src_ref=src,
            dst_ref=dst,
            send_sem=send_sem.at[index],
            recv_sem=recv_sem.at[index],
            device_id=device(*neighbour(at, axis, step)),
            device_id_type=MESH_ID,
        )
        copy.start()
        sent.append(copy)
        return copy

    def product(left, right, cols):
        value = dot_tn(left[...], right[:, cols]).astype(gi.dtype)
        return value.reshape(4, 2, 2, 2, -1, value.shape[1])

    def make_in(chunk):
        width = gi.shape[-1]
        if chunk >= 2:
            loaded(chunk)
            gi[chunk] = product(n2, gh, pl.ds((chunk - 2) * width, width))
        elif chunk == 1:
            loaded(9)
            gi[1, :, :, :, :, :, pl.ds(0, D)] = product(n1, gq, pl.ds(width, D))
            gi[1, :, :, :, :, :, pl.ds(D, D)] = product(at_v, gp, pl.ds(0, D))
        else:
            loaded(7)
            gi[0] = product(n1, gq, pl.ds(0, width))

    def make_out(chunk):
        if chunk:
            return
        loaded(5)
        width = go.shape[-1]

        def block(m, carry):
            left = act[:, pl.ds(pl.multiple_of(m * D, D), D)]
            value = dot_tn(left, gf[...]).astype(go.dtype)
            for k in range(OUT_CHUNKS):
                part = value[:, k * width : k * width + width]
                go[k, m] = part.reshape(2, 2, 2, -1, width)
            return carry

        lax.fori_loop(0, 4, block, 0)

    def entry(make, chunk, color, g, r0, r1, r2, r3, out, cols):
        return dict(
            make=make, chunk=chunk, color=color, g=g, r0=r0, r1=r1, r2=r2, r3=r3, out=out, cols=cols
        )

    entries = [entry(None, 0, 1, gs, r0s, r1s, r2s, r3s, fs, pl.ds(0, 128))]

    def in_entry(chunk, color):
        refs = [ref.at[chunk] for ref in (gi, r0i, r1i, r2i, r3i)]
        width = gi.shape[-1]
        return entry(make_in, chunk, color, *refs, fi, pl.ds(chunk * width, width))

    def out_entry(chunk, color):
        refs = [ref.at[chunk] for ref in (go, r0o, r1o, r2o, r3o)]
        width = go.shape[-1]
        return entry(make_out, chunk, color, *refs, fo, pl.ds(chunk * width, width))

    entries += [in_entry(2, 0), in_entry(3, 1), out_entry(0, 0), out_entry(1, 1)]
    entries += [in_entry(0, 0), in_entry(1, 1)]

    def begin(e):
        e["copy"] = send(e["g"].at[:, :, :, 1 - c], e["r0"], 3)

    def across(e):
        e["copy"].wait_recv()
        g, r0 = e["g"], e["r0"]

        def add(k, carry):
            zi, yi, xi = k // 4, lax.rem(k // 2, 2), lax.rem(k, 2)
            r0[zi, yi, xi] = add_low(g[zi, yi, xi, c], r0[zi, yi, xi])
            return carry

        lax.fori_loop(0, 16, add, 0)
        if e["color"] == 0:
            e["copy"] = send(r0.at[:, :, 1 - x], e["r1"], 2)
        else:
            e["copy"] = send(r0.at[:, 1 - y], e["r1"], 1)

    def onward(e):
        e["copy"].wait_recv()
        r0, r1, color = e["r0"], e["r1"], e["color"]

        def add(k, carry):
            zi, j = k // 2, lax.rem(k, 2)
            own = r0[zi, j, x] if color == 0 else r0[zi, y, j]
            r1[zi, j] = add_low(own, r1[zi, j])
            return carry

        lax.fori_loop(0, 8, add, 0)
        if color == 0:
            e["copy"] = send(r1.at[:, 1 - y], e["r2"], 1)
        else:
            e["copy"] = send(r1.at[:, 1 - x], e["r2"], 2)

    def along(e):
        e["copy"].wait_recv()
        r1, r2, keep = e["r1"], e["r2"], y if e["color"] == 0 else x

        def add(k, carry):
            r2[k] = add_low(r1[k, keep], r2[k])
            return carry

        lax.fori_loop(0, 4, add, 0)
        e["copies"] = [
            send(r2.at[lax.rem(z + step, 4)], e["r3"].at[step - 1], 0, step) for step in (1, 2, 3)
        ]

    squares = [jnp.zeros((8, 128), jnp.float32)]

    def finish(e):
        for copy in e["copies"]:
            copy.wait_recv()
        value = e["r2"][z].astype(jnp.float32)
        for k in range(3):
            value = value + e["r3"][k].astype(jnp.float32)
        e["out"][:, e["cols"]] = value
        rows, cols = value.shape
        total = jnp.sum((value * value).reshape(rows // 8, 8, cols), axis=0)
        for j in range(cols // 128):
            squares[0] = squares[0] + total[:, j * 128 : j * 128 + 128]

    for t in range(len(entries) + LAGS[-1]):
        for action, lag in zip((finish, along, onward, across), LAGS[::-1]):
            if 0 <= t - lag < len(entries):
                action(entries[t - lag])
        if t < len(entries):
            e = entries[t]
            if e["make"] is not None:
                e["make"](e["chunk"])
            if t == 0:
                pl.semaphore_wait(barrier, len(partners))
            begin(e)

    def exchange(buffer, mine, size, axis, base):
        copies = []
        for step in range(1, size):
            to = lax.rem(mine + step, size)
            copy = pltpu.make_async_remote_copy(
                src_ref=buffer.at[mine],
                dst_ref=buffer.at[mine],
                send_sem=norm_send.at[base + step],
                recv_sem=norm_recv.at[base + step],
                device_id=(to, n) if axis == 0 else (w, to),
                device_id_type=MESH_ID,
            )
            copy.start()
            copies.append(copy)
        for copy in copies:
            copy.wait()
        value = buffer[0]
        for k in range(1, size):
            value = value + buffer[k]
        return value

    squares_narrow[n] = squares[0]
    squares_wide[w] = exchange(squares_narrow, n, 4, 1, 0)
    fq[...] = exchange(squares_wide, w, 8, 0, 4)
    for copy in sent:
        copy.wait_send()


def reduce_all(n1, gq, attended, gp, n2, gh, act, gf, small):
    low, full = jnp.bfloat16, jnp.float32
    arrays = (n1, gq, attended, gp, n2, gh, act, gf)
    width = gq.shape[1] + gp.shape[1] + gh.shape[1]
    rows_in, rows_out = n1.shape[1] // 32, act.shape[1] // 32
    cols_out = gf.shape[1]
    vmem = pl.BlockSpec(memory_space=pltpu.VMEM)
    hbm = pl.BlockSpec(memory_space=pl.ANY)

    def trio(lead):
        return [
            pltpu.VMEM((IN_CHUNKS,) + lead + (rows_in, width // IN_CHUNKS), low),
            pltpu.VMEM((OUT_CHUNKS,) + lead + (rows_out, cols_out // OUT_CHUNKS), low),
            pltpu.VMEM(lead + (SMALL_ROWS, 128), full),
        ]

    padded = -(-n1.shape[0] // 256) * 256
    scratch = [pltpu.VMEM((padded, array.shape[1]), array.dtype) for array in arrays]
    scratch += trio((4, 2, 2, 2))[:2] + trio((4, 2, 2)) + trio((4, 2)) + trio((4,)) + trio((3,))
    copies = (IN_CHUNKS + OUT_CHUNKS + 1) * 6
    scratch += [
        pltpu.VMEM((4, 8, 128), full),
        pltpu.VMEM((8, 8, 128), full),
        pltpu.SemaphoreType.DMA((len(arrays) + 1,)),
        pltpu.SemaphoreType.DMA((copies,)),
        pltpu.SemaphoreType.DMA((copies,)),
        pltpu.SemaphoreType.DMA((12,)),
        pltpu.SemaphoreType.DMA((12,)),
    ]
    return pl.pallas_call(
        reduce_kernel,
        out_shape=(
            jax.ShapeDtypeStruct((rows_in, width), full),
            jax.ShapeDtypeStruct((rows_out, cols_out), full),
            jax.ShapeDtypeStruct((SMALL_ROWS, 128), full),
            jax.ShapeDtypeStruct((8, 128), full),
        ),
        in_specs=[hbm] * 8 + [vmem],
        out_specs=(vmem,) * 4,
        scratch_shapes=scratch,
        compiler_params=pltpu.CompilerParams(
            collective_id=1, has_side_effects=True, vmem_limit_bytes=62 << 20
        ),
        name="reduce_all",
    )(*arrays, small.reshape(4, 2, 2, 2, SMALL_ROWS, 128))


def update_kernel(
    num_tokens,
    fi, fo, fs, fq, all_small,
    wi, wi_m, wi_v, wo, wo_m, wo_v, kern, kern_m, kern_v, gain, gain_m, gain_v, bias, bias_m, bias_v,
    norm_o,
    wi_o, wi_m_o, wi_v_o, wi_low, wo_o, wo_m_o, wo_v_o, wo_low,
    kern_o, kern_m_o, kern_v_o, kern_low, gain_o, gain_m_o, gain_v_o, gain_low,
    bias_o, bias_m_o, bias_v_o, bias_low,
):
    total = jnp.sum(fq[...], axis=0, keepdims=True)
    total = jnp.sum(total, axis=1, keepdims=True)
    kept = kern.shape[1]
    after_gain = kept + gain.shape[0]
    after_bias = after_gain + bias.shape[0]
    lives = jnp.sum(all_small[...].astype(jnp.float32), axis=0)[0:1, after_bias : after_bias + 1]
    scale = 1.0 / (lives * num_tokens)
    norm = jnp.sqrt(total) * scale
    norm_o[...] = norm
    clip = jnp.minimum(1.0, 1.0 / (norm + 1e-06))

    def update(group, state, outs, where, gradient):
        news = adamw_update(
            *(ref[where] for ref in state), gradient * scale, clip, RATES[group], DECAYS[group]
        )
        for ref, new in zip(outs, news):
            ref[where] = new

    def update_in(k, carry):
        where = (slice(None), pl.ds(pl.multiple_of(k * D, D), D))
        update(0, (wi, wi_m, wi_v), (wi_o, wi_m_o, wi_v_o, wi_low), where, fi[where])
        return carry

    lax.fori_loop(0, fi.shape[1] // D, update_in, 0)

    def update_out(k, carry):
        where = (pl.ds(pl.multiple_of(k * 16, 16), 16), slice(None))
        update(1, (wo, wo_m, wo_v), (wo_o, wo_m_o, wo_v_o, wo_low), where, fo[where])
        return carry

    lax.fori_loop(0, fo.shape[0] // 16, update_out, 0)
    own = kern.shape[0]
    turned = square_of(fs[...]).T
    update(2, (kern, kern_m, kern_v), (kern_o, kern_m_o, kern_v_o, kern_low), ..., fs[:, 0:kept])
    update(
        3, (gain, gain_m, gain_v), (gain_o, gain_m_o, gain_v_o, gain_low), ...,
        turned[kept:after_gain, 0:own],
    )
    update(
        4, (bias, bias_m, bias_v), (bias_o, bias_m_o, bias_v_o, bias_low), ...,
        turned[after_gain:after_bias, 0:own],
    )


def update_all(sums, all_small, state, num_tokens):
    low, full = jnp.bfloat16, jnp.float32
    vmem = pl.BlockSpec(memory_space=pltpu.VMEM)
    return pl.pallas_call(
        functools.partial(update_kernel, float(num_tokens)),
        out_shape=(jax.ShapeDtypeStruct((1, 1), full),)
        + tuple(
            jax.ShapeDtypeStruct(master.shape, kind)
            for master in state[::3]
            for kind in (full, full, full, low)
        ),
        in_specs=[vmem] * 20,
        out_specs=(vmem,) * 21,
        compiler_params=pltpu.CompilerParams(vmem_limit_bytes=32 << 20),
        name="update_all",
    )(*sums, all_small, *state)


def cross_rows(left, right):
    return lax.dot_general(
        left, right, (((0,), (0,)), ((), ())), preferred_element_type=jnp.float32
    )


SIDE = 8
TALL = 512
CHUNK = 10
GAIN_ROW = 58
BIAS_ROW = 60


def tokens_of(value):
    return value.reshape(-1, SIDE, value.shape[-1])


def column_partial(value):
    return jnp.sum(tokens_of(value), axis=0)


def dot(left, right):
    return jnp.dot(left, right, preferred_element_type=jnp.float32)


def dot_nt(left, right):
    return lax.dot_general(
        left, right, (((1,), (1,)), ((), ())), preferred_element_type=jnp.float32
    )


def dot_tn(left, right):
    return lax.dot_general(
        left, right, (((0,), (0,)), ((), ())), preferred_element_type=jnp.float32
    )


def lane_tile(j):
    if isinstance(j, int):
        return pl.ds(j * 128, 128)
    return pl.ds(pl.multiple_of(j * 128, 128), 128)


def grid_rows(row, col):
    return pl.ds((1 + row * GRID + col) * SIDE, SIDE)


CLASS_ROWS = pl.ds(0, SIDE)


def put(grid, at, value):
    for j in range(D // 128):
        grid[j, at, :] = value[:, j * 128 : j * 128 + 128]


def get(grid, at, tiles=(0, 1, 2, 3)):
    return jnp.concatenate([grid[j, at, :] for j in tiles], axis=1)


def conv_tile(src, taps, base, width, reach, j, finish, flip=False):
    lanes = lane_tile(j)
    margin = width // 2
    offsets = range(-reach, reach + 1)

    def tap(dy, dx):
        if flip:
            dy, dx = -dy, -dx
        index = base + (dy + margin) * width + dx + margin
        return jnp.broadcast_to(taps[index : index + 1, lanes], (SIDE, 128))

    held = {(dy, dx): tap(dy, dx) for dy in offsets for dx in offsets}
    for row in range(GRID):
        sums = [jnp.zeros((SIDE, 128), jnp.float32) for _ in range(GRID)]
        for dy in offsets:
            if not 0 <= row + dy < GRID:
                continue
            line = [src[j, grid_rows(row + dy, col), :] for col in range(GRID)]
            for dx in offsets:
                for col in range(GRID):
                    if 0 <= col + dx < GRID:
                        sums[col] = sums[col] + line[col + dx] * held[dy, dx]
        for col in range(GRID):
            finish(grid_rows(row, col), sums[col])


def tap_sums(grad, src, base, width, reach, j, total):
    lanes = lane_tile(j)
    margin = width // 2
    offsets = range(-reach, reach + 1)
    for dy in offsets:
        sums = {dx: jnp.zeros((SIDE, 128), jnp.float32) for dx in offsets}
        for row in range(GRID):
            if not 0 <= row + dy < GRID:
                continue
            up = [grad[j, grid_rows(row, col), :] for col in range(GRID)]
            line = [src[j, grid_rows(row + dy, col), :] for col in range(GRID)]
            for dx in offsets:
                for col in range(GRID):
                    if 0 <= col + dx < GRID:
                        sums[dx] = sums[dx] + up[col] * line[col + dx]
        for dx in offsets:
            index = base + (dy + margin) * width + dx + margin
            total[index, :, lanes] = total[index, :, lanes] + sums[dx]


def mask_far_taps(rows):
    lanes = pl.ds(256, 128)
    keep = (lax.broadcasted_iota(jnp.int32, (1, 128), 1) >= 64).astype(jnp.float32)
    for tap in range(49):
        if max(abs(tap // 7 - 3), abs(tap % 7 - 3)) == 3:
            line = pl.ds(9 + tap, 1)
            rows[line, lanes] = rows[line, lanes] * keep


def relative_tiles(body):
    body(0, 1)
    body(1, 2)

    def rest(j, carry):
        body(j, 3)
        return carry

    lax.fori_loop(2, 4, rest, 0)


def all_tiles(body):
    def step(j, carry):
        body(j)
        return carry

    lax.fori_loop(0, 4, step, 0)


def all_chunks(body):
    def step(k, carry):
        body(pl.ds(pl.multiple_of(k * CHUNK * SIDE, 16), CHUNK * SIDE))
        return carry

    lax.fori_loop(0, 50 // CHUNK, step, 0, unroll=True)


def normalise(values):
    centred = values - jnp.mean(values, axis=-1, keepdims=True)
    scale = lax.rsqrt(jnp.mean(centred * centred, axis=-1, keepdims=True) + NORM_EPS)
    return centred * scale, scale


def norm_back(grad, hat, scale, gain):
    inner = grad * gain
    mean = jnp.mean(inner, axis=-1, keepdims=True)
    along = jnp.mean(inner * hat, axis=-1, keepdims=True)
    return scale * (inner - mean - hat * along)


def spread_images(src, grid, first, limit):
    for i in range(SIDE):
        image = src[i]
        keep = jnp.full(image.shape, first + i, jnp.int32) < limit
        at = pl.ds(i, image.shape[0], stride=SIDE)
        put(grid, at, jnp.where(keep, image.astype(jnp.float32), 0.0))


def set_parameters(small, par, heads):
    par[...] = small[...].astype(jnp.float32).T
    mask_far_taps(par)
    row_head = lax.broadcasted_iota(jnp.int32, heads.shape, 0) // 64
    col_head = lax.broadcasted_iota(jnp.int32, heads.shape, 1) // 64
    heads[...] = jnp.where(row_head == col_head, 1.0, 0.0).astype(heads.dtype)


def every_image(body):
    for i in range(SIDE):
        for half in range(2):
            body(pl.ds(i, TALL // SIDE, stride=SIDE), (2 * half, 2 * half + 1))


def forward_kernel(
    num_images, rows, counts, x_in, dy_in, w_in, w_out, small,
    out, act_o, gh_o, n1_o, n2_o, at_o, gf_o, gp_o, gx_o, xt_o, hat_o, sc_o, q_o, k_o, v_o, cv_o,
    cols_o, hcols_o,
    par, heads, x, x1, v, q, k, conv, hat2, slope, gn, scale2,
):
    low = jnp.bfloat16
    step = pl.program_id(0)
    first = step * SIDE
    live = pl.ds(0, rows)

    @pl.when(step == 0)
    def _():
        set_parameters(small, par, heads)
        for grid in (q, k, v):
            grid[...] = jnp.zeros_like(grid)
        cols_o[...] = jnp.zeros_like(cols_o)
        hcols_o[...] = jnp.zeros_like(hcols_o)

    def bias(row):
        return par[BIAS_ROW + row : BIAS_ROW + row + 1, :]

    def gain(row):
        return par[GAIN_ROW + row : GAIN_ROW + row + 1, :]

    spread_images(x_in, x, first, num_images)
    xt_o[...] = get(x, live).astype(low)
    spread_images(dy_in, gn, first, jnp.minimum(counts[0], num_images))
    gf_o[...] = get(gn, live).astype(low)

    def position(j):
        lanes = lane_tile(j)
        shift = jnp.broadcast_to(par[BIAS_ROW + 10 : BIAS_ROW + 11, lanes], (SIDE, 128))

        def finish(at, total):
            x1[j, at, :] = x[j, at, :] + total + shift

        conv_tile(x, par, 0, 3, 1, j, finish)
        x1[j, CLASS_ROWS, :] = x[j, CLASS_ROWS, :]

    all_tiles(position)

    def first_norm(at):
        hat, scale = normalise(get(x1, at))
        hat_o[at, :] = hat.astype(low)
        sc_o[at, :] = jnp.broadcast_to(scale, (CHUNK * SIDE, 128))
        n1_o[at, :] = (hat * gain(0) + bias(0)).astype(low)

    all_chunks(first_norm)
    n1 = n1_o[...]
    put(gn, live, dot(n1, w_in[:, D : 2 * D]))

    def weights(j):
        lanes = lane_tile(j)
        keys = tokens_of(gn[j, live, :])
        powers = jnp.exp(keys - jnp.max(keys, axis=0, keepdims=True))
        share = 0.125 / jnp.sum(powers, axis=0, keepdims=True)
        value = (powers * share).reshape(-1, 128)
        k[j, live, :] = value
        k_o[:, lanes] = value.astype(low)

    all_tiles(weights)
    value = dot(n1, w_in[:, 2 * D : 3 * D]) + bias(3)
    put(v, live, value)
    v_o[...] = value.astype(low)

    def relative(j, reach):
        lanes = lane_tile(j)
        shift = jnp.broadcast_to(par[BIAS_ROW + 11 : BIAS_ROW + 12, lanes], (SIDE, 128))

        def finish(at, total):
            conv[j, at, :] = total + shift

        conv_tile(v, par, 9, 7, reach, j, finish)
        conv[j, CLASS_ROWS, :] = jnp.zeros((SIDE, 128), jnp.float32)

    relative_tiles(relative)
    cv_o[...] = get(conv, live).astype(low)
    value = dot(n1, w_in[:, :D]) + bias(2)
    q_o[...] = value.astype(low)
    put(q, live, value)

    def attention(at, tiles):
        context = dot_tn(get(k, at, tiles).astype(low), get(v, at, tiles).astype(low))
        context = context.astype(low) * heads[...]
        value = dot(get(q, at, tiles).astype(low), context)
        for n, j in enumerate(tiles):
            gn[j, at, :] = value[:, n * 128 : n * 128 + 128]

    every_image(attention)
    for j in range(D // 128):
        at_o[:, lane_tile(j)] = (gn[j, live, :] + conv[j, live, :] * q[j, live, :]).astype(low)
    put(x1, live, get(x1, live) + (dot(at_o[...], w_in[:, 3 * D : 4 * D]) + bias(4)))

    def second_norm(at):
        hat, scale = normalise(get(x1, at))
        hat2[at, :] = hat
        scale2[at, :] = jnp.broadcast_to(scale, (CHUNK * SIDE, 128))
        n2_o[at, :] = (hat * gain(1) + bias(1)).astype(low)

    all_chunks(second_norm)
    n2 = n2_o[...]
    for part in range(MLP_WIDTH // D):
        cols = pl.ds(part * D, D)
        put(gn, live, dot(n2, w_in[:, pl.ds((4 + part) * D, D)]))

        def gelu(at):
            h = get(gn, at) + bias(5 + part)
            below = 0.5 + 0.5 * lax.erf(h * (0.5**0.5))
            density = jnp.exp(-0.5 * h * h) * 0.3989422804014327
            act_o[at, cols] = (h * below).astype(low)
            slope[at, cols] = below + h * density

        all_chunks(gelu)
    put(x1, live, get(x1, live) + dot(act_o[...], w_out[...]) + bias(9))
    for i in range(SIDE):
        out[i] = get(x1, pl.ds(i, out.shape[1], stride=SIDE)).astype(low)

    gf = gf_o[...]
    for part in range(MLP_WIDTH // D):
        cols = pl.ds(part * D, D)
        grad = (dot_nt(gf, w_out[cols, :]) * slope[:, cols]).astype(low)
        gh_o[:, cols] = grad
        hcols_o[:, cols] = hcols_o[:, cols] + column_partial(grad.astype(jnp.float32))
    put(gn, live, dot_nt(gh_o[...], w_in[:, 4 * D :]))

    def second_back(at):
        grad = get(gn, at)
        hat = hat2[at, :]
        scale = scale2[at, 0:1]
        upstream = gf_o[at, :].astype(jnp.float32)
        total = upstream + norm_back(grad, hat, scale, gain(1))
        gx_o[at, :] = total
        rounded = total.astype(low)
        gp_o[at, :] = rounded
        cols_o[0] = cols_o[0] + column_partial(grad)
        cols_o[1] = cols_o[1] + column_partial(grad * hat)
        cols_o[2] = cols_o[2] + column_partial(rounded.astype(jnp.float32))
        cols_o[3] = cols_o[3] + column_partial(upstream)

    all_chunks(second_back)


def backward_kernel(
    rows, w_in, small, cols_in, hcols_in, gx, hat, sc, q_in, k_in, v_in, cv, xt,
    out, gq_o, small_o,
    par, heads, cols, taps, lines, g, gc, q, k, v, gq, gk, gv, x, g1,
):
    low = jnp.bfloat16
    step = pl.program_id(0)
    live = pl.ds(0, rows)

    @pl.when(step == 0)
    def _():
        set_parameters(small, par, heads)
        for grid in (g, q, k, v, gq, gk, gv):
            grid[...] = jnp.zeros_like(grid)
        cols[...] = jnp.zeros_like(cols)
        taps[...] = jnp.zeros_like(taps)

    grad = dot_nt(gx[...].astype(low), w_in[:, 3 * D : 4 * D])
    put(g, live, grad)
    for j in range(D // 128):
        lanes = lane_tile(j)
        part = g[j, live, :]
        queries = q_in[:, lanes].astype(jnp.float32)
        q[j, live, :] = queries
        k[j, live, :] = k_in[:, lanes].astype(jnp.float32)
        v[j, live, :] = v_in[:, lanes].astype(jnp.float32)
        x[j, live, :] = xt[:, lanes].astype(jnp.float32)
        gq[j, live, :] = part * cv[:, lanes].astype(jnp.float32)
        gc[j, live, :] = part * queries
        gc[j, CLASS_ROWS, :] = jnp.zeros((SIDE, 128), jnp.float32)
        cols[0, :, lanes] = cols[0, :, lanes] + column_partial(gc[j, live, :])

    def relative(j, reach):
        def finish(at, total):
            gv[j, at, :] = total

        conv_tile(gc, par, 9, 7, reach, j, finish, flip=True)
        gv[j, CLASS_ROWS, :] = jnp.zeros((SIDE, 128), jnp.float32)
        tap_sums(gc, v, 9, 7, reach, j, taps)

    relative_tiles(relative)

    def attention(at, tiles):
        qs, ks, vs, gs = (get(grid, at, tiles).astype(low) for grid in (q, k, v, g))
        context = dot_tn(ks, vs).astype(low) * heads[...]
        grads = dot_tn(qs, gs).astype(low) * heads[...]
        to_q, to_k, to_v = dot_nt(gs, context), dot_nt(vs, grads), dot(ks, grads)
        for n, j in enumerate(tiles):
            here = slice(n * 128, n * 128 + 128)
            gq[j, at, :] = gq[j, at, :] + to_q[:, here]
            gk[j, at, :] = to_k[:, here]
            gv[j, at, :] = gv[j, at, :] + to_v[:, here]

    every_image(attention)

    def finish_qkv(j):
        lanes = lane_tile(j)
        share = tokens_of(k[j, live, :])
        up = tokens_of(gk[j, live, :])
        along = jnp.sum(share * up, axis=0, keepdims=True) * 8.0
        gq_o[:, pl.ds(pl.multiple_of(D + j * 128, 128), 128)] = (
            (share * (up - along)).reshape(-1, 128).astype(low)
        )
        part = gq[j, live, :].astype(low)
        gq_o[:, lanes] = part
        cols[1, :, lanes] = cols[1, :, lanes] + column_partial(part.astype(jnp.float32))
        part = gv[j, live, :].astype(low)
        gq_o[:, pl.ds(pl.multiple_of(2 * D + j * 128, 128), 128)] = part
        cols[2, :, lanes] = cols[2, :, lanes] + column_partial(part.astype(jnp.float32))

    all_tiles(finish_qkv)
    put(gk, live, dot_nt(gq_o[...], w_in[:, : 3 * D]))

    def first_back(at):
        grad = get(gk, at)
        hats = hat[at, :].astype(jnp.float32)
        total = gx[at, :] + norm_back(grad, hats, sc[at, 0:1], par[GAIN_ROW : GAIN_ROW + 1, :])
        put(g1, at, total)
        cols[3] = cols[3] + column_partial(grad)
        cols[4] = cols[4] + column_partial(grad * hats)
        cols[5] = cols[5] + column_partial(total)

    all_chunks(first_back)
    cols[5] = cols[5] - get(g1, CLASS_ROWS)

    def position(j):
        def finish(at, total):
            gv[j, at, :] = g1[j, at, :] + total

        conv_tile(g1, par, 0, 3, 1, j, finish, flip=True)
        gv[j, CLASS_ROWS, :] = g1[j, CLASS_ROWS, :]
        tap_sums(g1, x, 0, 3, 1, j, taps)

    all_tiles(position)
    for i in range(SIDE):
        out[i] = get(gv, pl.ds(i, out.shape[1], stride=SIDE))

    @pl.when(step == pl.num_programs(0) - 1)
    def _():
        lines[...] = jnp.zeros_like(lines)
        for tap in range(taps.shape[0]):
            lines[tap : tap + 1, :] = jnp.sum(taps[tap], axis=0, keepdims=True)
        mask_far_taps(lines)
        hidden = [hcols_in[:, i * D : i * D + D] for i in range(MLP_WIDTH // D)]
        order = [cols[4], cols_in[1], cols[3], cols_in[0], cols[1], cols[2], cols_in[2]]
        for i, part in enumerate(order + hidden + [cols_in[3], cols[5], cols[0]]):
            row = GAIN_ROW + i
            lines[row : row + 1, :] = jnp.sum(part, axis=0, keepdims=True)
        small_o[...] = lines[...].T


def fixed(shape):
    zeros = (0,) * len(shape)
    return pl.BlockSpec(shape, lambda g: zeros, pipeline_mode=pl.Buffered(1))


def compute(images, cotangent, counts, w_in, w_out, small):
    low, full = jnp.bfloat16, jnp.float32
    num_images, num_tokens, channels = images.shape
    groups = -(-num_images // SIDE)
    rows = num_tokens * SIDE
    total = groups * rows

    def block(cols):
        return pl.BlockSpec((rows, cols), lambda g: (g, 0))

    def image_block():
        return pl.BlockSpec((SIDE, num_tokens, channels), lambda g: (g, 0, 0))

    def made(cols, kind=low):
        return jax.ShapeDtypeStruct((total, cols), kind)

    def grid():
        return pltpu.VMEM((channels // 128, TALL, 128), full)

    shared = [pltpu.VMEM((128, channels), full), pltpu.VMEM((256, 256), low)]
    wide = w_out.shape[0]
    forward = pl.pallas_call(
        functools.partial(forward_kernel, num_images, rows),
        grid=(groups,),
        in_specs=[
            pl.BlockSpec(memory_space=pltpu.SMEM),
            image_block(),
            image_block(),
            fixed(w_in.shape),
            fixed(w_out.shape),
            fixed(small.shape),
        ],
        out_specs=[image_block(), block(wide), block(wide)]
        + [block(channels)] * 8
        + [block(128)]
        + [block(channels)] * 4
        + [fixed((4, SIDE, channels)), fixed((SIDE, wide))],
        out_shape=[jax.ShapeDtypeStruct(images.shape, low), made(wide), made(wide)]
        + [made(channels)] * 5
        + [made(channels, full), made(channels), made(channels), made(128, full)]
        + [made(channels)] * 4
        + [
            jax.ShapeDtypeStruct((4, SIDE, channels), full),
            jax.ShapeDtypeStruct((SIDE, wide), full),
        ],
        scratch_shapes=shared
        + [grid() for _ in range(6)]
        + [pltpu.VMEM((rows, channels), full), pltpu.VMEM((rows, wide), full), grid(), pltpu.VMEM((rows, 128), full)],
        compiler_params=pltpu.CompilerParams(vmem_limit_bytes=60 << 20),
        name="forward",
    )
    (
        out, act, gh, n1, n2, attended, gf, gp, gx, xt, hat, scale, q, k, v, cv, cols, hcols,
    ) = forward(counts, images, cotangent, w_in, w_out, small)

    backward = pl.pallas_call(
        functools.partial(backward_kernel, rows),
        grid=(groups,),
        in_specs=[
            pl.BlockSpec(
                (channels, 4 * channels), lambda g: (0, 0), pipeline_mode=pl.Buffered(1)
            ),
            fixed(small.shape),
            fixed(cols.shape),
            fixed(hcols.shape),
            block(channels),
            block(channels),
            block(128),
        ]
        + [block(channels)] * 5,
        out_specs=[image_block(), block(3 * channels), fixed(small.shape)],
        out_shape=[
            jax.ShapeDtypeStruct(images.shape, full),
            made(3 * channels),
            jax.ShapeDtypeStruct(small.shape, full),
        ],
        scratch_shapes=shared
        + [
            pltpu.VMEM((6, SIDE, channels), full),
            pltpu.VMEM((GAIN_ROW, SIDE, channels), full),
            pltpu.VMEM((128, channels), full),
        ]
        + [grid() for _ in range(10)],
        compiler_params=pltpu.CompilerParams(vmem_limit_bytes=60 << 20),
        name="backward",
    )
    input_grad, gq, grad_small = backward(
        w_in, small, cols, hcols, gx, hat, scale, q, k, v, cv, xt
    )
    return out, input_grad, (n1, gq, attended, gp, n2, gh, act, gf), grad_small


def adamw_update(master, first_moment, second_moment, gradient, clip_factor, rate, decay):
    clipped = gradient * clip_factor
    first_new = BETA_ONE * first_moment + (1.0 - BETA_ONE) * clipped
    second_new = BETA_TWO * second_moment + (1.0 - BETA_TWO) * clipped * clipped
    first_hat = first_new / (1.0 - BETA_ONE**STEP)
    second_hat = second_new / (1.0 - BETA_TWO**STEP)
    master_new = master - rate * (first_hat / (jnp.sqrt(second_hat) + ADAM_EPS) + decay * master)
    return (master_new, first_new, second_new, master_new.astype(jnp.bfloat16))


def local(
    images,
    cotangent,
    counts,
    in_mats,
    in_mats_m,
    in_mats_v,
    out_mat,
    out_mat_m,
    out_mat_v,
    kernels,
    kernels_m,
    kernels_v,
    gains,
    gains_m,
    gains_v,
    biases,
    biases_m,
    biases_v,
    special,
):
    if special:
        all_in, all_out, all_small = gather_all(counts, in_mats, out_mat, kernels.T, gains, biases)
        block_out, input_grad, factors, grad_small = compute(
            images,
            cotangent,
            counts,
            all_in.reshape(-1, in_mats.shape[1]),
            all_out.reshape(-1, out_mat.shape[1]),
            all_small.reshape(-1, 128),
        )
        sums = reduce_all(*factors, grad_small)
        state = (
            in_mats, in_mats_m, in_mats_v,
            out_mat, out_mat_m, out_mat_v,
            kernels.T, kernels_m.T, kernels_v.T,
            gains, gains_m, gains_v,
            biases, biases_m, biases_v,
        )
        norm, *news = update_all(sums, all_small, state, images.shape[1])
        news[8:12] = [part.T for part in news[8:12]]
        return (block_out, input_grad, norm.reshape(()), *news)
    in_copy = in_mats.astype(jnp.bfloat16)
    out_copy = out_mat.astype(jnp.bfloat16)
    shards = (kernels, gains, biases)
    sizes = [shard.shape[0] for shard in shards]
    used = sum(sizes)
    count_row = jnp.broadcast_to(counts.astype(jnp.float32)[:, None], (1, kernels.shape[1]))
    rows = jnp.concatenate(shards + (count_row,), axis=0)
    small = jnp.pad(rows, ((0, 128 - used - 1), (0, 0))).T.astype(jnp.bfloat16)
    all_in, all_out, all_small = (
        lax.all_gather(part, ("wide", "narrow"), axis=0, tiled=True)
        for part in (in_copy, out_copy, small)
    )
    all_small = all_small.reshape(-1, small.shape[0], 128)
    live_total = jnp.sum(all_small[:, 0, used].astype(jnp.float32)) * images.shape[1]
    scale_factor = 1.0 / live_total
    block_out, input_grad, factors, grad_small = compute(
        images,
        cotangent,
        counts,
        all_in.reshape(-1, in_copy.shape[1]),
        all_out.reshape(-1, out_copy.shape[1]),
        all_small.reshape(-1, 128),
    )
    n1, gq, attended, gp, n2, gh, act, gf = factors
    grad_in = jnp.concatenate(
        [cross_rows(n1, gq), cross_rows(attended, gp), cross_rows(n2, gh)], axis=1
    )
    grad_fc2 = cross_rows(act, gf)
    sum_in, sum_out, sum_small = (
        lax.psum_scatter(part, ("wide", "narrow"), scatter_dimension=0, tiled=True)
        for part in (grad_in, grad_fc2, grad_small)
    )
    total_squares = lax.psum(
        sum(jnp.sum(part * part) for part in (sum_in, sum_out, sum_small)), ("wide", "narrow")
    )
    rows = sum_small.T
    summed = (
        sum_in,
        sum_out,
        rows[: sizes[0]],
        rows[sizes[0] : sizes[0] + sizes[1]],
        rows[sizes[0] + sizes[1] : used],
    )
    summed = tuple(part * scale_factor for part in summed)
    grad_norm = jnp.sqrt(total_squares) * scale_factor
    clip_factor = jnp.minimum(1.0, 1.0 / (grad_norm + 1e-06))
    in_new = adamw_update(
        in_mats, in_mats_m, in_mats_v, summed[0], clip_factor, RATES[0], DECAYS[0]
    )
    out_new = adamw_update(
        out_mat, out_mat_m, out_mat_v, summed[1], clip_factor, RATES[1], DECAYS[1]
    )
    kern_new = adamw_update(
        kernels, kernels_m, kernels_v, summed[2], clip_factor, RATES[2], DECAYS[2]
    )
    gain_new = adamw_update(gains, gains_m, gains_v, summed[3], clip_factor, RATES[3], DECAYS[3])
    bias_new = adamw_update(biases, biases_m, biases_v, summed[4], clip_factor, RATES[4], DECAYS[4])
    return (
        block_out,
        input_grad,
        grad_norm,
        in_new[0],
        in_new[1],
        in_new[2],
        in_new[3],
        out_new[0],
        out_new[1],
        out_new[2],
        out_new[3],
        kern_new[0],
        kern_new[1],
        kern_new[2],
        kern_new[3],
        gain_new[0],
        gain_new[1],
        gain_new[2],
        gain_new[3],
        bias_new[0],
        bias_new[1],
        bias_new[2],
        bias_new[3],
    )


def solution(mesh):
    placed = (
        P(("wide", "narrow"), None, None),
        P(("wide", "narrow"), None, None),
        P(("wide", "narrow")),
        P(("wide", "narrow"), None),
        P(("wide", "narrow"), None),
        P(("wide", "narrow"), None),
        P(("wide", "narrow"), None),
        P(("wide", "narrow"), None),
        P(("wide", "narrow"), None),
        P(None, ("wide", "narrow")),
        P(None, ("wide", "narrow")),
        P(None, ("wide", "narrow")),
        P(None, ("wide", "narrow")),
        P(None, ("wide", "narrow")),
        P(None, ("wide", "narrow")),
        P(None, ("wide", "narrow")),
        P(None, ("wide", "narrow")),
        P(None, ("wide", "narrow")),
    )
    special = dict(mesh.shape) == {"wide": 8, "narrow": 4}
    return jax.shard_map(
        functools.partial(local, special=special),
        mesh=mesh,
        in_specs=placed,
        out_specs=(
            P(("wide", "narrow"), None, None),
            P(("wide", "narrow"), None, None),
            P(),
            P(("wide", "narrow"), None),
            P(("wide", "narrow"), None),
            P(("wide", "narrow"), None),
            P(("wide", "narrow"), None),
            P(("wide", "narrow"), None),
            P(("wide", "narrow"), None),
            P(("wide", "narrow"), None),
            P(("wide", "narrow"), None),
            P(None, ("wide", "narrow")),
            P(None, ("wide", "narrow")),
            P(None, ("wide", "narrow")),
            P(None, ("wide", "narrow")),
            P(None, ("wide", "narrow")),
            P(None, ("wide", "narrow")),
            P(None, ("wide", "narrow")),
            P(None, ("wide", "narrow")),
            P(None, ("wide", "narrow")),
            P(None, ("wide", "narrow")),
            P(None, ("wide", "narrow")),
            P(None, ("wide", "narrow")),
        ),
        check_vma=False,
    )
```
